32 devices in a mesh: node: 8 (over z, y), col: 4 (over x, core).
Axes of the slice: x: 2, y: 2, z: 4, core: 2. Of those that a mesh axis runs over, the one named last changes fastest.
Arguments:
- blocks: float32 [2304, 128, 128], P('node'), may hold values from 0.001 to 1
- owner_row: int32 [8, 288], P('node'), may hold values from 0 to 47, never falling along the last dimension, each value on 1 to 10 neighbouring positions
- block_col: int32 [8, 288], P('node'), may hold values from 0 to 383, as said below
- start: float32 [128, 49152], P('col', 'node'), may hold values from -160 to 160
Outputs:
- basis: float32 [128, 49152], P('col', 'node')
- projected_first: float32 [128, 128], P('col')
- projected: float32 [128, 128], P('col')
The draws below stay inside these ranges and needn't reach their ends.
Inputs may be any that keep to these rules, and one draw needn't show every extreme that they name: `owner_row`: the stored blocks of one index of node are listed by block row, never falling; every block row has 1 to 10 stored blocks, one has exactly 10. `block_col`: A block stored at index g of node has its block column among the block rows of index g, among the last 24 block rows of index g - 1, or among the first 24 block rows of index g + 1, cyclically over node; every index has blocks at both of those bounds.
All inputs are finite; a program needn't handle non-finite values.
Results may differ from the reference program's by a relative error of at most 0.0003.
Values sent between devices are 32-bit elements; how exact they have to be, the bound alone decides.
No kernel may reach another device: no remote copies, remote signals or barrier semaphores. Data moves between devices by JAX's collectives and lax.ppermute only.
A program may use at most 128 MiB of HBM per device.

```python
import math
import jax
import jax.numpy as jnp
import numpy as np
from jax import lax

BLOCK = 128
VECS = 128
BR_DEV = 48
PER_ROW = 6
MOST_ROW = 10
DEGREE = 4
ITERS = 2
BLOCK_ROWS = 384
NODES = 49152
STORED = 2304
N_NODE = 8


def draw_block_col(key, part):
    groups = BLOCK_ROWS // BR_DEV
    stored = PER_ROW * BR_DEV
    half = BR_DEV // 2
    key_side, key_near, key_any = jax.random.split(key, 3)
    position = jnp.arange(stored, dtype=jnp.int32)[None, :]
    side = jax.random.randint(key_side, (groups, stored), 0, 3) - 1
    side = jnp.where(position == 0, -1, jnp.where(position == 1, 1, side))
    near = jax.random.randint(key_near, (groups, stored), 0, half)
    near = jnp.where(position == 0, 0, jnp.where(position == 1, half - 1, near))
    anywhere = jax.random.randint(key_any, (groups, stored), 0, BR_DEV)
    local = jnp.where(side < 0, half + near, jnp.where(side > 0, near, anywhere))
    owner = (jnp.arange(groups, dtype=jnp.int32)[:, None] + side) % groups
    return (owner * BR_DEV + local).astype(jnp.int32)


def draw_start(key, part):
    groups = NODES // (BR_DEV * BLOCK)
    waves = 8
    keys = jax.random.split(key, 6)
    base = jax.random.normal(keys[0], (VECS, NODES), jnp.float32)
    amp_cos = 3.5 * jax.random.normal(keys[4], (VECS, waves), jnp.float32)
    amp_sin = 3.5 * jax.random.normal(keys[5], (VECS, waves), jnp.float32)
    group_scale = jnp.power(10.0, jax.random.uniform(keys[1], (groups,), jnp.float32, 0.0, 1.0))
    group_scale = jnp.where(jnp.arange(groups, dtype=jnp.int32) == 0, 10.0, group_scale)
    spread = jnp.repeat(group_scale, BR_DEV * BLOCK)
    rough = jnp.power(10.0, 0.5 * jax.random.uniform(keys[2], (NODES,), jnp.float32))
    column = jnp.power(10.0, jax.random.uniform(keys[3], (VECS, 1), jnp.float32))
    column = jnp.where(jnp.arange(VECS, dtype=jnp.int32)[:, None] == 0, 10.0, column)
    noise = base * spread[None, :] * rough[None, :]
    position = jnp.arange(NODES, dtype=jnp.float32) * (2.0 * math.pi / NODES)
    smooth = jnp.zeros((VECS, NODES), jnp.float32)
    for wave in range(waves):
        angle = position * float(wave)
        smooth = smooth + amp_cos[:, wave:wave + 1] * jnp.cos(angle)[None, :]
        smooth = smooth + amp_sin[:, wave:wave + 1] * jnp.sin(angle)[None, :]
    value = (noise + smooth) * column
    return jnp.clip(value, -160.0, 160.0).astype(jnp.float32)


def steps_of(rng, dims, cuts, low, top_value):
    def one(dim, shards_of):
        draws = jax.random.uniform(jax.random.fold_in(jax.random.fold_in(rng, 6), dim), (shards_of,), jnp.float32, low / len(cuts), top_value / len(cuts))
        return jnp.repeat(jnp.exp(draws), dims[dim] // shards_of).reshape((-1,) + (1,) * (len(dims) - dim - 1))

    level = one(*cuts[0])
    for cut in cuts[1:]:
        level = level * one(*cut)
    return level


def length_profile(amount, total, bound, slope):
    portions = [(1 << 20) // math.isqrt(grade ** slope) + 1 for grade in range(2, amount + 1)]
    spare, holding = total - bound - (amount - 1), [1] * (amount - 1)
    while spare > 0:
        movable = [i for i in range(amount - 1) if holding[i] < bound]
        mass, budget = sum([portions[i] for i in movable]), spare
        for i in movable:
            addition = min(bound - holding[i], max(1, budget * portions[i] // mass), spare)
            holding[i] = holding[i] + addition
            spare = spare - addition
    return np.array([bound] + holding)


def ragged(key, count, total, most, slope):
    if count == 2:
        one = jax.random.randint(key, (), max(1, total - most), min(most, total - 1) + 1)
        return jnp.stack([one, total - one])
    tallies = jnp.asarray(length_profile(count, total, most, slope), jnp.int32)
    twos = (count - 1) // 2
    donor, sink = tallies[1:1 + 2 * twos:2], tallies[2:2 + 2 * twos:2]
    margin = jnp.minimum(donor - 1, most - sink)
    moved = jax.random.randint(jax.random.fold_in(key, 1), (twos,), 0, 1 << 20) % (margin + 1)
    tallies = tallies.at[1:1 + 2 * twos:2].set(donor - moved).at[2:2 + 2 * twos:2].set(sink + moved)
    return tallies[jax.random.permutation(jax.random.fold_in(key, 2), count)]


def setup_inputs(seed: int = 0) -> dict:
    streams_of = jax.random.split(jax.random.key(seed), 5)
    blocks = jnp.clip(jnp.exp(math.log(1.0) - 6.9077552 * jax.random.uniform(streams_of[0], (STORED, BLOCK, BLOCK), jnp.float32) ** steps_of(streams_of[0], (STORED, BLOCK, BLOCK), ((0, 8),), -0.2, 0.2)), 0.001, 1.0)
    owner_row = jax.vmap(lambda own: jnp.searchsorted(jnp.cumsum(ragged(own, BR_DEV, PER_ROW * BR_DEV, MOST_ROW, 1)), jnp.arange(PER_ROW * BR_DEV), side="right"))(jax.random.split(streams_of[1], N_NODE)).reshape((N_NODE, PER_ROW * BR_DEV)).astype(jnp.int32)
    block_col = draw_block_col(jax.random.fold_in(streams_of[4], 71), 0)
    start = draw_start(jax.random.fold_in(streams_of[4], 71), 0)
    return dict(blocks=blocks, owner_row=owner_row, block_col=block_col, start=start)


precise = lax.Precision.HIGHEST
center = 1.025
half_width = 0.975

def chebyshev(panel, operate):
    previous = panel
    current = (operate(panel) - center * panel) / half_width
    for step in range(DEGREE - 1):
        following = 2.0 * (operate(current) - center * current) / half_width - previous
        previous = current
        current = following
    return current

def reference(blocks, owner_row, block_col, start):
    groups = BLOCK_ROWS // BR_DEV
    grouped = blocks.reshape(groups, PER_ROW * BR_DEV, BLOCK, BLOCK)
    row_range = jnp.arange(BR_DEV, dtype=jnp.int32)

    def one_degree(args):
        tiles, rows_of = args
        onehot = (rows_of[None, :] == row_range[:, None]).astype(jnp.float32)
        return jnp.einsum('rn,ni->ri', onehot, jnp.sum(tiles, axis=2), precision=precise).reshape(BR_DEV * BLOCK)
    degree = lax.map(one_degree, (grouped, owner_row)).reshape(NODES)

    def operate(panel):
        pieces = panel.reshape(VECS, BLOCK_ROWS, BLOCK)

        def one_group(args):
            tiles, rows_of, cols_of = args
            gathered = jnp.take(pieces, cols_of, axis=1)
            product = jnp.einsum('nij,knj->nki', tiles, gathered, precision=precise)
            onehot = (rows_of[None, :] == row_range[:, None]).astype(jnp.float32)
            summed = jnp.einsum('rn,nki->kri', onehot, product, precision=precise)
            return summed.reshape(VECS, BR_DEV * BLOCK)
        mixed = lax.map(one_group, (grouped, owner_row, block_col))
        mixed = jnp.transpose(mixed, (1, 0, 2)).reshape(VECS, NODES)
        return panel - mixed / degree[None, :]
    basis = start
    results = []
    for step in range(ITERS):
        filtered = chebyshev(basis, operate)
        gram = jnp.dot(filtered, filtered.T, precision=precise) / NODES
        factor = jnp.linalg.cholesky(gram)
        basis = jax.scipy.linalg.solve_triangular(factor, filtered, lower=True)
        image = operate(basis)
        results.append(jnp.dot(basis, image.T, precision=precise) / NODES)
    return (basis, results[0], results[-1])
```

```python
import functools
import jax
import jax.numpy as jnp
from jax import lax
from jax.experimental import pallas as pl
from jax.experimental.pallas import tpu as pltpu
from jax.sharding import PartitionSpec as P

DEGREE = 4
UNROLL = 16
F32, BF16, I32 = jnp.float32, jnp.bfloat16, jnp.int32
precise = lax.Precision.HIGHEST
center = 1.025
half_width = 0.975
MIB = 1 << 20
IN_VMEM = pl.BlockSpec(memory_space=pltpu.VMEM)
IN_SMEM = pl.BlockSpec(memory_space=pltpu.SMEM)


def prep_kernel(UN, R, half, groups, own_ref, col_ref, me_ref, blk_ref, w_ref, deg_ref, src_ref, row_ref, num_ref, pos_ref, cnt_ref):
    chunk = blk_ref.shape[0]
    total = own_ref.shape[1]
    step = pl.program_id(0)

    @pl.when(step == 0)
    def _():
        me = me_ref[0]
        odd = me % 2
        for r in range(R):
            cnt_ref[r] = 0
        def count(b, c):
            r = own_ref[0, b]
            cnt_ref[r] = cnt_ref[r] + 1
            return c
        lax.fori_loop(0, total, count, 0)
        zero = jnp.zeros(w_ref.shape[1:], BF16)
        def slots(r, at):
            n = cnt_ref[r]
            pairs = (n + 1) // 2
            cnt_ref[r] = 2 * at
            row_at = jnp.where(odd == 1, r, jnp.where(r >= half, r - half, r + half))
            def put(p, c):
                row_ref[p] = row_at
                return c
            lax.fori_loop(at, at + pairs, put, 0)
            @pl.when(n % 2 == 1)
            def _():
                w_ref[2 * at + n] = zero
                src_ref[2 * at + n] = 0
            return at + pairs
        used = lax.fori_loop(0, R, slots, 0)
        upto = (used + UN - 1) // UN * UN
        def fill(p, c):
            row_ref[p] = R
            for s in range(2):
                w_ref[2 * p + s] = zero
                src_ref[2 * p + s] = 0
            return c
        lax.fori_loop(used, upto, fill, 0)
        num_ref[0] = upto // UN
        def place(b, c):
            r = own_ref[0, b]
            at = cnt_ref[r]
            cnt_ref[r] = at + 1
            pos_ref[b] = at
            k = col_ref[0, b]
            owner = k // R
            local = k - owner * R
            upper = (local >= half).astype(I32)
            near = local - half * upper
            own_at = near + half * jnp.where(odd == 1, upper, 1 - upper)
            halo_at = 2 * half + near + half * jnp.where(odd == 1, 1 - upper, upper)
            src_ref[at] = jnp.where(owner == me, own_at, halo_at)
            return c
        lax.fori_loop(0, total, place, 0)
        deg_ref[...] = jnp.zeros(deg_ref.shape, F32)

    for c in range(chunk):
        b = step * chunk + c
        at = pos_ref[b]
        r = row_ref[at // 2]
        t = blk_ref[c].T
        hi = t.astype(BF16)
        lo = (t - hi.astype(F32)).astype(BF16)
        w_ref[at, :, :t.shape[1]] = hi
        w_ref[at, :, t.shape[1]:] = lo
        deg_ref[r] = deg_ref[r] + jnp.sum(t, axis=0, keepdims=True)

    @pl.when(step == pl.num_programs(0) - 1)
    def _():
        deg_ref[...] = 1.0 / deg_ref[...]

def prep(own, col, me, blocks, R, groups, UN, chunk=24):
    total, n, _ = blocks.shape
    half = R // 2
    slots = total + R
    slots = (slots // 2 + UN - 1) // UN * UN * 2
    return pl.pallas_call(
        functools.partial(prep_kernel, UN, R, half, groups),
        grid=(total // chunk,),
        in_specs=[IN_SMEM, IN_SMEM, IN_SMEM, pl.BlockSpec((chunk, n, n), lambda i: (i, 0, 0))],
        out_specs=[IN_VMEM, IN_VMEM, IN_SMEM, IN_SMEM, IN_SMEM],
        out_shape=[pltpu.VMEM((slots, n, 2 * n), BF16),
                   jax.ShapeDtypeStruct((R, 1, n), F32),
                   jax.ShapeDtypeStruct((slots,), I32),
                   jax.ShapeDtypeStruct((slots // 2,), I32),
                   jax.ShapeDtypeStruct((1,), I32)],
        scratch_shapes=[pltpu.SMEM((total,), I32), pltpu.SMEM((R,), I32)],
        compiler_params=pltpu.CompilerParams(vmem_limit_bytes=32 * MIB),
        name="prep",
    )(own, col, me, blocks)

def apply_kernel(UN, mode, src_ref, row_ref, num_ref, w_ref, inv_ref, pe_ref, po_ref, he_ref, ho_ref, *rest):
    if mode == "first" or mode == "plain":
        ne_ref, no_ref, sp_ref, acc_ref = rest
    else:
        qe_ref, qo_ref, ne_ref, no_ref, sp_ref, acc_ref = rest
    half, kk, n = pe_ref.shape
    for i, ref in enumerate((pe_ref, po_ref, he_ref, ho_ref)):
        v = ref[...]
        hi = v.astype(BF16)
        sp_ref[i * half:(i + 1) * half, :kk] = hi
        sp_ref[i * half:(i + 1) * half, kk:] = (v - hi.astype(F32)).astype(BF16)
    acc_ref[...] = jnp.zeros(acc_ref.shape, F32)

    def group(g, c):
        for u in range(UN):
            p = g * UN + u
            lhs = jnp.concatenate([sp_ref[src_ref[2 * p]], sp_ref[src_ref[2 * p + 1]]], axis=1)
            w = w_ref[pl.ds(2 * p, 2)].reshape(2 * n, 2 * n)
            y = jnp.dot(lhs, w, preferred_element_type=F32)
            r = row_ref[p]
            acc_ref[r] = acc_ref[r] + ((y[:kk, :n] + y[kk:, :n]) + (y[:kk, n:] + y[kk:, n:]))
        return c
    lax.fori_loop(0, num_ref[0], group, 0)
    for i, (p_ref, n_ref) in enumerate(((pe_ref, ne_ref), (po_ref, no_ref))):
        now = p_ref[...]
        image = now - acc_ref[i * half:(i + 1) * half] * inv_ref[i * half:(i + 1) * half]
        if mode == "plain":
            n_ref[...] = image
        elif mode == "first":
            n_ref[...] = (image - center * now) * (1.0 / half_width)
        else:
            q_ref = (qe_ref, qo_ref)[i]
            n_ref[...] = (image - center * now) * (2.0 / half_width) - q_ref[...]

def apply(UN, mode, meta, w, inv, *panels):
    half, kk, n = panels[0].shape
    out = jax.ShapeDtypeStruct((half, kk, n), F32)
    return pl.pallas_call(
        functools.partial(apply_kernel, UN, mode),
        in_specs=[IN_SMEM] * 3 + [IN_VMEM] * (2 + len(panels)),
        out_specs=[IN_VMEM, IN_VMEM],
        out_shape=[out, out],
        scratch_shapes=[pltpu.VMEM((4 * half, 2 * kk, n), BF16), pltpu.VMEM((2 * half + 1, kk, n), F32)],
        compiler_params=pltpu.CompilerParams(vmem_limit_bytes=16 * MIB),
        cost_estimate=pl.CostEstimate(flops=2 * 4 * w.shape[0] * n * n * kk, bytes_accessed=w.size * 2, transcendentals=0),
        name="apply_" + mode,
    )(*meta, w, inv, *panels)


def nt(a, b):
    return lax.dot_general(
        a, b, (((1,), (1,)), ((), ())), precision=precise, preferred_element_type=F32
    )


def nn(a, b):
    return jnp.dot(a, b, precision=precise, preferred_element_type=F32)


def rows_at(b, *refs):
    return jnp.concatenate([ref[c, b] for c in range(refs[0].shape[0]) for ref in refs], axis=0)


def gram_kernel(fa_ref, fb_ref, za_ref, zb_ref, g_ref, k_ref):
    g_ref[...] = jnp.zeros(g_ref.shape, F32)
    k_ref[...] = jnp.zeros(k_ref.shape, F32)

    def one(b, c):
        f = rows_at(b, fa_ref, fb_ref)
        z = rows_at(b, za_ref, zb_ref)
        g_ref[...] = g_ref[...] + nt(f, f)
        k_ref[...] = k_ref[...] + nt(f, z)
        return c

    lax.fori_loop(0, fa_ref.shape[1], one, 0)


def turn_kernel(inv_ref, fa_ref, fb_ref, f_ref, g_ref):
    g_ref[...] = jnp.zeros(g_ref.shape, F32)

    def one(b, c):
        f = nn(inv_ref[...], rows_at(b, fa_ref, fb_ref))
        f_ref[b] = f
        g_ref[...] = g_ref[...] + nt(f, f)
        return c

    lax.fori_loop(0, fa_ref.shape[1], one, 0)


def cross_kernel(inv_ref, f_ref, za_ref, zb_ref, k_ref):
    k_ref[...] = jnp.zeros(k_ref.shape, F32)

    def one(b, c):
        z = nn(inv_ref[...], rows_at(b, za_ref, zb_ref))
        k_ref[...] = k_ref[...] + nt(f_ref[b], z)
        return c

    lax.fori_loop(0, za_ref.shape[1], one, 0)


def basis_kernel(inv_ref, f_ref, q_ref):
    count, _, each, _ = q_ref.shape

    def one(b, c):
        q = nn(inv_ref[...], f_ref[b])
        for i in range(count):
            q_ref[i, b] = q[i * each:(i + 1) * each]
        return c

    lax.fori_loop(0, f_ref.shape[0], one, 0)


def proj_kernel(nodes, inv_ref, k_ref, g_ref, out_ref):
    image = (half_width * k_ref[...] + center * g_ref[...]) / nodes
    out_ref[...] = nt(nn(inv_ref[...], image), inv_ref[...])


def call(kernel, name, outs, *args):
    return pl.pallas_call(
        kernel,
        in_specs=[IN_VMEM] * len(args),
        out_specs=[IN_VMEM] * len(outs),
        out_shape=[jax.ShapeDtypeStruct(o, F32) for o in outs],
        compiler_params=pltpu.CompilerParams(vmem_limit_bytes=16 * MIB),
        name=name,
    )(*args)


def exchange(pair):
    count = lax.axis_size("node")
    even = [(i, i ^ 1) for i in range(count)]
    odd = [(i, (i - 1 if i % 2 == 0 else i + 1) % count) for i in range(count)]
    return lax.ppermute(pair[0], "node", even), lax.ppermute(pair[1], "node", odd)


def total(value):
    for axis in ("col", "node"):
        count = lax.axis_size(axis)
        hop = 1
        while hop < count:
            value = value + lax.ppermute(value, axis, [(i, i ^ hop) for i in range(count)])
            hop *= 2
    return value


def to_rows(pair):
    count = lax.axis_size("col")
    whole = jnp.concatenate(pair, axis=0)
    slots, each, n = whole.shape
    return lax.all_to_all(
        whole.reshape(count, slots // count, each, n), "col", split_axis=0, concat_axis=0, tiled=True
    )


def inverse_factor(gram, nodes):
    factor = jnp.linalg.cholesky(gram / nodes)
    return jax.scipy.linalg.solve_triangular(
        factor, jnp.eye(gram.shape[0], dtype=F32), lower=True
    )


def body(blocks, owner_row, block_col, start):
    cols_here, width = start.shape
    block = blocks.shape[1]
    slots = width // block
    half = slots // 2
    count = lax.axis_size("col")
    groups = lax.axis_size("node")
    nodes = width * groups
    vecs = cols_here * count
    each = cols_here // 2
    me = lax.axis_index("node").astype(I32)
    odd = me % 2 == 1

    tiles = start.reshape(2, each, slots, block).transpose(0, 2, 1, 3)
    low, high = tiles[:, :half], tiles[:, half:]
    left = jnp.where(odd, low, high)
    right = jnp.where(odd, high, low)
    chains = [(left[i], right[i]) for i in range(2)]

    w, inv, src, row, num = prep(owner_row, block_col, me.reshape(1), blocks, slots, groups, UNROLL)
    meta = (src, row, num)

    def first(pair):
        return tuple(apply(UNROLL, "first", meta, w, inv, *pair, *exchange(pair)))

    def later(pair, previous):
        return tuple(apply(UNROLL, "cheb", meta, w, inv, *pair, *exchange(pair), *previous))

    before = chains
    now = [first(c) for c in before]
    for _ in range(DEGREE - 1):
        before, now = now, [later(c, p) for c, p in zip(now, before)]
    filtered = now
    rows = [to_rows(c) for c in filtered]
    before, now = now, [first(c) for c in now]
    image = [to_rows(c) for c in now]
    square = (vecs, vecs)
    gram, cross = call(gram_kernel, "gram", [square] * 2, *rows, *image)
    gram, cross = total(jnp.stack([gram, cross]))
    for _ in range(DEGREE - 1):
        before, now = now, [later(c, p) for c, p in zip(now, before)]
    inverse = inverse_factor(gram, nodes)
    (projected_first,) = call(functools.partial(proj_kernel, nodes), "proj", [square], inverse, cross, gram)

    rows = [to_rows(c) for c in now]
    turned, gram = call(
        turn_kernel, "turn", [(slots // count, vecs, block), square], inverse, *rows
    )
    gram = total(gram)
    last = [first(c) for c in now]
    image = [to_rows(c) for c in last]
    (cross,) = call(cross_kernel, "cross", [square], inverse, turned, *image)
    cross = total(cross)
    inverse = inverse_factor(gram, nodes)
    (q,) = call(basis_kernel, "basis", [(count, slots // count, cols_here, block)], inverse, turned)
    q = lax.all_to_all(q, "col", split_axis=0, concat_axis=0, tiled=True)
    q = q.reshape(slots, cols_here, block)
    low = jnp.where(odd, q[:half], q[half:])
    high = jnp.where(odd, q[half:], q[:half])
    basis = jnp.concatenate([low, high], axis=0).transpose(1, 0, 2).reshape(cols_here, width)
    (projected,) = call(functools.partial(proj_kernel, nodes), "proj", [square], inverse, cross, gram)

    def mine(value):
        at = lax.axis_index("col") * cols_here
        return lax.dynamic_slice_in_dim(value, at, cols_here, 0)

    return basis, mine(projected_first), mine(projected)


def solution(mesh):
    placed = (P("node", None, None), P("node", None), P("node", None), P("col", "node"))
    return jax.shard_map(
        body,
        mesh=mesh,
        in_specs=placed,
        out_specs=(P("col", "node"), P("col", None), P("col", None)),
        check_vma=False,
    )
```

```python
import functools
import jax
import jax.numpy as jnp
from jax import lax
from jax.experimental import pallas as pl
from jax.experimental.pallas import tpu as pltpu
from jax.sharding import PartitionSpec as P

DEGREE = 4
UNROLL = 16
CHUNK = 24
F32, BF16, I32 = jnp.float32, jnp.bfloat16, jnp.int32
precise = lax.Precision.HIGHEST
center = 1.025
half_width = 0.975
MIB = 1 << 20
IN_VMEM = pl.BlockSpec(memory_space=pltpu.VMEM)
IN_SMEM = pl.BlockSpec(memory_space=pltpu.SMEM)


def nt(a, b):
    return lax.dot_general(
        a, b, (((1,), (1,)), ((), ())), precision=precise, preferred_element_type=F32
    )


def tn(a, b):
    return lax.dot_general(
        a, b, (((0,), (0,)), ((), ())), precision=precise, preferred_element_type=F32
    )


def nn(a, b):
    return jnp.dot(a, b, precision=precise, preferred_element_type=F32)


def call(kernel, name, outs, *args, scalars=0, scratch=(), cost=None):
    return pl.pallas_call(
        kernel,
        in_specs=[IN_SMEM] * scalars + [IN_VMEM] * (len(args) - scalars),
        out_specs=[IN_VMEM] * len(outs),
        out_shape=[jax.ShapeDtypeStruct(o, F32) for o in outs],
        scratch_shapes=list(scratch),
        compiler_params=pltpu.CompilerParams(vmem_limit_bytes=12 * MIB),
        cost_estimate=cost,
        name=name,
    )(*args)


def prep_kernel(rows, ids_ref, own_ref, col_ref, blk_ref, w_ref, inv_ref, src_ref, row_ref, num_ref,
                eye_ref, state_ref):
    chunk, n, _ = blk_ref.shape
    half = rows // 2
    step = pl.program_id(0)
    me = ids_ref[0]
    odd = me % 2
    zero = jnp.zeros(w_ref.shape[1:], BF16)

    @pl.when(step == 0)
    def _():
        state_ref[0] = 0
        state_ref[1] = -1
        inv_ref[...] = jnp.zeros(inv_ref.shape, F32)
        lines = lax.broadcasted_iota(I32, eye_ref.shape, 0)
        lanes = lax.broadcasted_iota(I32, eye_ref.shape, 1)
        eye_ref[...] = jnp.where((lines == lanes) | (lines >= n), 1.0, 0.0).astype(BF16)

    at = state_ref[0]
    last = state_ref[1]
    for c in range(chunk):
        b = step * chunk + c
        r = own_ref[0, b]
        k = col_ref[0, b]
        at = jnp.where(r == last, at, (at + 1) // 2 * 2)
        last = r
        owner = k // rows
        local = k - owner * rows
        upper = (local >= half).astype(I32)
        near = local - half * upper
        swap = odd * upper + (1 - odd) * (1 - upper)
        src_ref[at] = jnp.where(owner == me, near + half * swap, 2 * half + near + half * (1 - swap))
        src_ref[at + 1] = 0
        top = (r >= half).astype(I32)
        r_at = r + half * (1 - odd) * (1 - 2 * top)
        row_ref[at // 2] = r_at
        w_ref[at + 1] = zero
        a = blk_ref[c]
        high = a.astype(BF16)
        low = (a - high.astype(F32)).astype(BF16)
        both = jnp.concatenate([high, low], axis=0)
        t = lax.dot_general(
            eye_ref[...], both, (((1,), (1,)), ((), ())), preferred_element_type=F32
        )
        w_ref[at] = t[:n].astype(BF16)
        inv_ref[r_at] = inv_ref[r_at] + (t[n:n + 1, :n] + t[n:n + 1, n:])
        at = at + 1
    state_ref[0] = at
    state_ref[1] = last

    @pl.when(step == pl.num_programs(0) - 1)
    def _():
        used = (at + 1) // 2
        upto = (used + UNROLL - 1) // UNROLL * UNROLL
        def fill(p, c):
            row_ref[p] = rows
            for s in range(2):
                w_ref[2 * p + s] = zero
                src_ref[2 * p + s] = 0
            return c
        lax.fori_loop(used, upto, fill, 0)
        num_ref[0] = upto // UNROLL
        inv_ref[...] = 1.0 / inv_ref[...]


def prep(ids, own, col, blocks, rows):
    count, n, _ = blocks.shape
    chunk = CHUNK if count % CHUNK == 0 else 1
    slots = ((count + rows) // 2 + UNROLL) // UNROLL * UNROLL * 2
    return pl.pallas_call(
        functools.partial(prep_kernel, rows),
        grid=(count // chunk,),
        in_specs=[IN_SMEM, IN_SMEM, IN_SMEM, pl.BlockSpec((chunk, n, n), lambda i: (i, 0, 0))],
        out_specs=[IN_VMEM, IN_VMEM, IN_SMEM, IN_SMEM, IN_SMEM],
        out_shape=[pltpu.VMEM((slots, n, 2 * n), BF16),
                   jax.ShapeDtypeStruct((rows, 1, n), F32),
                   jax.ShapeDtypeStruct((slots,), I32),
                   jax.ShapeDtypeStruct((slots // 2,), I32),
                   jax.ShapeDtypeStruct((1,), I32)],
        scratch_shapes=[pltpu.VMEM((n + 16, n), BF16), pltpu.SMEM((2,), I32)],
        compiler_params=pltpu.CompilerParams(vmem_limit_bytes=12 * MIB),
        cost_estimate=pl.CostEstimate(
            flops=2 * count * n * n * n, bytes_accessed=4 * blocks.size, transcendentals=0
        ),
        name="prep",
    )(ids, own, col, blocks)


def apply_kernel(recur, mate, *refs):
    refs = list(refs)
    ids_ref, src_ref, row_ref, num_ref, w_ref, inv_ref = refs[:6]
    panels = refs[6:10]
    del refs[:10]
    olds = [refs.pop(0) for _ in range(2 if recur else 0)]
    mates = [refs.pop(0) for _ in range(2 if mate else 0)]
    outs = [refs.pop(0) for _ in range(2)]
    parts = refs[:-2]
    sp_ref, acc_ref = refs[-2:]
    half, kk, n = panels[0].shape
    for i, ref in enumerate(panels):
        v = ref[...]
        high = v.astype(BF16)
        sp_ref[i * half:(i + 1) * half, :kk] = high
        sp_ref[i * half:(i + 1) * half, kk:] = (v - high.astype(F32)).astype(BF16)
    acc_ref[...] = jnp.zeros(acc_ref.shape, F32)

    def group(g, c):
        for u in range(UNROLL):
            p = g * UNROLL + u
            piece = jnp.concatenate([sp_ref[src_ref[2 * p]], sp_ref[src_ref[2 * p + 1]]], axis=1)
            w = w_ref[pl.ds(2 * p, 2)].reshape(2 * n, 2 * n)
            y = jnp.dot(piece, w, preferred_element_type=F32)
            r = row_ref[p]
            acc_ref[r] = acc_ref[r] + ((y[:kk, :n] + y[kk:, :n]) + (y[:kk, n:] + y[kk:, n:]))
        return c

    lax.fori_loop(0, num_ref[0], group, 0)
    scale = (2.0 if recur else 1.0) / half_width
    for i in range(2):
        span = slice(i * half, (i + 1) * half)
        now = panels[i][...]
        image = (now - acc_ref[span] * inv_ref[span] - center * now) * scale
        if recur:
            image = image - olds[i][...]
        outs[i][...] = image
        if mate:
            acc_ref[span] = image
            sp_ref2 = parts[-1]
            sp_ref2[span] = mates[i][...]
    if mate:
        count = len(parts) - 1
        me = ids_ref[1]
        each = 2 * half // count
        for s in range(count):
            at = pl.ds((me ^ s) * each, each)
            parts[s][:, :kk] = parts[-1][at]
            parts[s][:, kk:] = acc_ref[at]


def apply(ids, meta, pair, halo, old=(), mate=(), count=0):
    half, kk, n = pair[0].shape
    w = meta[3]
    out = [jax.ShapeDtypeStruct((half, kk, n), F32)] * 2
    if mate:
        out += [jax.ShapeDtypeStruct((2 * half // count, 2 * kk, n), F32)] * count
    args = (*pair, *halo, *old, *mate)
    scratch = [pltpu.VMEM((4 * half, 2 * kk, n), BF16), pltpu.VMEM((2 * half + 1, kk, n), F32)]
    if mate:
        scratch = [pltpu.VMEM((2 * half, kk, n), F32)] + scratch
    res = pl.pallas_call(
        functools.partial(apply_kernel, bool(old), bool(mate)),
        in_specs=[IN_SMEM] * 4 + [IN_VMEM] * (2 + len(args)),
        out_specs=[IN_VMEM] * len(out),
        out_shape=out,
        scratch_shapes=scratch,
        compiler_params=pltpu.CompilerParams(vmem_limit_bytes=12 * MIB),
        cost_estimate=pl.CostEstimate(
            flops=8 * w.shape[0] * n * n * kk, bytes_accessed=2 * w.size, transcendentals=0
        ),
        name="apply" + "_recur" * bool(old) + "_parts" * bool(mate),
    )(ids, *meta, *args)
    return tuple(res[:2]), tuple(res[2:])


def factor_kernel(nodes, g_ref, out_ref, both_ref):
    n = g_ref.shape[0]
    p = 8
    lines = lax.broadcasted_iota(I32, (n, n), 0)
    lanes = lax.broadcasted_iota(I32, (n, n), 1)
    both_ref[:, :n] = g_ref[...] * (1.0 / nodes)
    both_ref[:, n:] = jnp.where(lines == lanes, 1.0, 0.0).astype(F32)
    sub = lax.broadcasted_iota(I32, (p, n), 0)
    for j in range(0, n, p):
        left = both_ref[j:j + p, :n]
        right = both_ref[j:j + p, n:]
        cols = [jnp.broadcast_to(left[:, j + i:j + i + 1], (p, n)) for i in range(p)]
        pivot = jnp.zeros((p, n), F32)
        for i in range(p):
            own = jnp.broadcast_to(cols[i][i:i + 1], (p, n))
            pivot = jnp.where(sub == i, own, pivot)
            if i + 1 < p:
                ratio = jnp.where(sub > i, cols[i] / own, 0.0)
                for k in range(i + 1, p):
                    cols[k] = cols[k] - ratio * jnp.broadcast_to(cols[k][i:i + 1], (p, n))
                left = left - ratio * jnp.broadcast_to(left[i:i + 1], (p, n))
                right = right - ratio * jnp.broadcast_to(right[i:i + 1], (p, n))
        root = lax.rsqrt(pivot)
        left = left * root
        right = right * root
        out_ref[j:j + p] = right
        if j + p < n:
            change = tn(left, jnp.concatenate([left, right], axis=1))
            both_ref[j + p:] = both_ref[j + p:] - change[j + p:]


def inverse_factor(gram, nodes):
    n = gram.shape[0]
    return call(
        functools.partial(factor_kernel, nodes), "factor", [(n, n)], gram,
        scratch=[pltpu.VMEM((n, 2 * n), F32)],
    )[0]


def gathered(ids_ref, parts, b, x_ref):
    each = parts[0].shape[1]
    me = ids_ref[1]
    for s, part in enumerate(parts):
        x_ref[b, pl.ds(pl.multiple_of((me ^ s) * each, each), each)] = part[b]
    return x_ref[b]


def gram_kernel(ids_ref, *refs):
    parts, (f_ref, g_ref) = refs[:-2], refs[-2:]
    total = jnp.zeros(g_ref.shape, F32)
    for b in range(f_ref.shape[0]):
        f = gathered(ids_ref, parts, b, f_ref)
        total = total + nt(f, f)
    g_ref[...] = total


def cross_kernel(ids_ref, f_ref, *refs):
    parts, (k_ref, x_ref) = refs[:-2], refs[-2:]
    total = jnp.zeros(k_ref.shape, F32)
    for b in range(f_ref.shape[0]):
        total = total + nt(f_ref[b], gathered(ids_ref, parts, b, x_ref))
    k_ref[...] = total


def turn_kernel(ids_ref, inv_ref, *refs):
    parts, (f_ref, g_ref, x_ref) = refs[:-3], refs[-3:]
    total = jnp.zeros(g_ref.shape, F32)
    for b in range(f_ref.shape[0]):
        f = nn(inv_ref[...], gathered(ids_ref, parts, b, x_ref))
        f_ref[b] = f
        total = total + nt(f, f)
    g_ref[...] = total


def turn_cross_kernel(ids_ref, inv_ref, f_ref, *refs):
    parts, (k_ref, x_ref) = refs[:-2], refs[-2:]
    total = jnp.zeros(k_ref.shape, F32)
    for b in range(f_ref.shape[0]):
        z = nn(inv_ref[...], gathered(ids_ref, parts, b, x_ref))
        total = total + nt(f_ref[b], z)
    k_ref[...] = total


def basis_kernel(ids_ref, inv_ref, f_ref, *refs):
    parts, x_ref = refs[:-1], refs[-1]
    each = parts[0].shape[1]
    me = ids_ref[1]
    for b in range(f_ref.shape[0]):
        x_ref[b] = nn(inv_ref[...], f_ref[b])
        for s, part in enumerate(parts):
            part[b] = x_ref[b, pl.ds(pl.multiple_of((me ^ s) * each, each), each)]


def proj_kernel(nodes, ids_ref, *refs):
    pairs = len(refs[:6]) // 3
    parts, x_ref = refs[6:-1], refs[-1]
    each = parts[0].shape[1]
    me = ids_ref[1]
    for i in range(pairs):
        inv_ref, k_ref, g_ref = refs[3 * i:3 * i + 3]
        image = (half_width * k_ref[...] + center * g_ref[...]) * (1.0 / nodes)
        x_ref[...] = nt(nn(inv_ref[...], image), inv_ref[...])
        for s, part in enumerate(parts):
            part[i] = x_ref[pl.ds(pl.multiple_of((me ^ s) * each, each), each)]


def slot_row(slot, half, odd):
    return slot + half * (1 - odd) * jnp.where(slot >= half, -1, 1)


def split_kernel(ids_ref, start_ref, *outs):
    half, kk, n = outs[0].shape
    odd = ids_ref[0] % 2
    for slot in range(2 * half):
        row = slot_row(slot, half, odd)
        piece = start_ref[:, pl.ds(pl.multiple_of(row * n, n), n)]
        for i in range(2):
            outs[2 * i + slot // half][slot % half] = piece[i * kk:(i + 1) * kk]


def join_kernel(half, ids_ref, *refs):
    parts, out_ref = refs[:-1], refs[-1]
    each, _, n = parts[0].shape
    odd = ids_ref[0] % 2
    me = ids_ref[1]
    for s, part in enumerate(parts):
        for b in range(each):
            row = slot_row((me ^ s) * each + b, half, odd)
            out_ref[:, pl.ds(pl.multiple_of(row * n, n), n)] = part[b]


def exchange(pair):
    count = lax.axis_size("node")
    even = [(i, i ^ 1) for i in range(count)]
    odd = [(i, (i - 1 if i % 2 == 0 else i + 1) % count) for i in range(count)]
    return lax.ppermute(pair[0], "node", even), lax.ppermute(pair[1], "node", odd)


def swap(value, axis, hop):
    return lax.ppermute(value, axis, [(i, i ^ hop) for i in range(lax.axis_size(axis))])


def swapped(parts):
    return [parts[0]] + [swap(parts[s], "col", s) for s in range(1, len(parts))]


def summed(value, *axes):
    for axis in axes:
        hop = 1
        while hop < lax.axis_size(axis):
            value = value + swap(value, axis, hop)
            hop *= 2
    return value


def body(blocks, owner_row, block_col, start):
    cols_here, width = start.shape
    block = blocks.shape[1]
    slots = width // block
    half = slots // 2
    count = lax.axis_size("col")
    nodes = width * lax.axis_size("node")
    vecs = cols_here * count
    each = cols_here // 2
    quarter = slots // count
    square = (vecs, vecs)
    wide = (quarter, vecs, block)
    held = pltpu.VMEM(wide, F32)
    ids = jnp.stack([lax.axis_index("node"), lax.axis_index("col")]).astype(I32)

    halves = call(split_kernel, "split", [(half, each, block)] * 4, ids, start, scalars=1)
    before = [tuple(halves[:2]), tuple(halves[2:])]
    w, inv, src, row, num = prep(ids, owner_row, block_col, blocks, slots)
    meta = (src, row, num, w, inv)

    def advance(now, before=((), ()), parts=False):
        first, _ = apply(ids, meta, now[0], exchange(now[0]), before[0])
        mate = first if parts else ()
        second, out = apply(ids, meta, now[1], exchange(now[1]), before[1], mate, count)
        return [first, second], (swapped(out) if parts else None)

    now, _ = advance(before)
    for step in range(DEGREE - 1):
        after, parts = advance(now, before, step == DEGREE - 2)
        before, now = now, after
    panel, gram_first = call(gram_kernel, "gram", [wide, square], ids, *parts, scalars=1)
    gram = summed(gram_first, "col", "node")
    after, parts = advance(now, parts=True)
    before, now = now, after
    (cross_first,) = call(
        cross_kernel, "cross", [square], ids, panel, *parts, scalars=1, scratch=[held]
    )
    inverse_first = inverse_factor(gram, nodes)
    for step in range(DEGREE - 1):
        if step == DEGREE - 2:
            now, inverse_first = lax.optimization_barrier((now, inverse_first))
        after, parts = advance(now, before, step == DEGREE - 2)
        before, now = now, after

    turned, gram_last = call(
        turn_kernel, "turn", [wide, square], ids, inverse_first, *parts, scalars=1, scratch=[held]
    )
    gram = summed(gram_last, "col", "node")
    _, parts = advance(now, parts=True)
    (cross_last,) = call(
        turn_cross_kernel, "turn_cross", [square], ids, inverse_first, turned, *parts,
        scalars=1, scratch=[held],
    )
    inverse_last = inverse_factor(gram, nodes)
    parts = call(
        basis_kernel, "basis", [(quarter, cols_here, block)] * count, ids, inverse_last, turned,
        scalars=1, scratch=[held],
    )
    (basis,) = call(
        functools.partial(join_kernel, half), "join", [(cols_here, width)], ids, *swapped(parts), scalars=1
    )
    parts = call(
        functools.partial(proj_kernel, nodes), "proj", [(2, cols_here, vecs)] * count, ids,
        inverse_first, cross_first, gram_first, inverse_last, cross_last, gram_last,
        scalars=1, scratch=[pltpu.VMEM(square, F32)],
    )
    projected = summed(sum(swapped(parts)), "node")
    return basis, projected[0], projected[1]


def solution(mesh):
    placed = (P("node", None, None), P("node", None), P("node", None), P("col", "node"))
    return jax.shard_map(
        body,
        mesh=mesh,
        in_specs=placed,
        out_specs=(P("col", "node"), P("col", None), P("col", None)),
        check_vma=False,
    )
```

```python
import functools
import jax
import jax.numpy as jnp
from jax import lax
from jax.experimental import pallas as pl
from jax.experimental.pallas import tpu as pltpu
from jax.sharding import PartitionSpec as P

DEGREE = 4
UNROLL = 16
CHUNK = 24
F32, BF16, I32 = jnp.float32, jnp.bfloat16, jnp.int32
precise = lax.Precision.HIGHEST
center = 1.025
half_width = 0.975
MIB = 1 << 20
IN_VMEM = pl.BlockSpec(memory_space=pltpu.VMEM)
IN_SMEM = pl.BlockSpec(memory_space=pltpu.SMEM)


def nt(a, b):
    return lax.dot_general(
        a, b, (((1,), (1,)), ((), ())), precision=precise, preferred_element_type=F32
    )


def tn(a, b):
    return lax.dot_general(
        a, b, (((0,), (0,)), ((), ())), precision=precise, preferred_element_type=F32
    )


def nn(a, b):
    return jnp.dot(a, b, precision=precise, preferred_element_type=F32)


def call(kernel, name, outs, *args, scalars=0, scratch=(), cost=None):
    return pl.pallas_call(
        kernel,
        in_specs=[IN_SMEM] * scalars + [IN_VMEM] * (len(args) - scalars),
        out_specs=[IN_VMEM] * len(outs),
        out_shape=[jax.ShapeDtypeStruct(o, F32) for o in outs],
        scratch_shapes=list(scratch),
        compiler_params=pltpu.CompilerParams(vmem_limit_bytes=12 * MIB),
        cost_estimate=cost,
        name=name,
    )(*args)


def prep_kernel(rows, ids_ref, own_ref, col_ref, blk_ref, w_ref, inv_ref, src_ref, row_ref, num_ref,
                eye_ref, state_ref):
    chunk, n, _ = blk_ref.shape
    half = rows // 2
    step = pl.program_id(0)
    me = ids_ref[0]
    odd = me % 2
    zero = jnp.zeros(w_ref.shape[1:], BF16)

    @pl.when(step == 0)
    def _():
        state_ref[0] = 0
        state_ref[1] = -1
        inv_ref[...] = jnp.zeros(inv_ref.shape, F32)
        lines = lax.broadcasted_iota(I32, eye_ref.shape, 0)
        lanes = lax.broadcasted_iota(I32, eye_ref.shape, 1)
        eye_ref[...] = jnp.where((lines == lanes) | (lines >= n), 1.0, 0.0).astype(BF16)

    at = state_ref[0]
    last = state_ref[1]
    for c in range(chunk):
        b = step * chunk + c
        r = own_ref[0, b]
        k = col_ref[0, b]
        at = jnp.where(r == last, at, (at + 1) // 2 * 2)
        last = r
        owner = k // rows
        local = k - owner * rows
        upper = (local >= half).astype(I32)
        near = local - half * upper
        swap = odd * upper + (1 - odd) * (1 - upper)
        src_ref[at] = jnp.where(owner == me, near + half * swap, 2 * half + near + half * (1 - swap))
        src_ref[at + 1] = 0
        top = (r >= half).astype(I32)
        r_at = r + half * (1 - odd) * (1 - 2 * top)
        row_ref[at // 2] = r_at
        w_ref[at + 1] = zero
        a = blk_ref[c]
        high = a.astype(BF16)
        low = (a - high.astype(F32)).astype(BF16)
        both = jnp.concatenate([high, low], axis=0)
        t = lax.dot_general(
            eye_ref[...], both, (((1,), (1,)), ((), ())), preferred_element_type=F32
        )
        w_ref[at] = t[:n].astype(BF16)
        inv_ref[r_at] = inv_ref[r_at] + (t[n:n + 1, :n] + t[n:n + 1, n:])
        at = at + 1
    state_ref[0] = at
    state_ref[1] = last

    @pl.when(step == pl.num_programs(0) - 1)
    def _():
        used = (at + 1) // 2
        upto = (used + UNROLL - 1) // UNROLL * UNROLL
        def fill(p, c):
            row_ref[p] = rows
            for s in range(2):
                w_ref[2 * p + s] = zero
                src_ref[2 * p + s] = 0
            return c
        lax.fori_loop(used, upto, fill, 0)
        num_ref[0] = upto // UNROLL
        inv_ref[...] = 1.0 / inv_ref[...]


def prep(ids, own, col, blocks, rows):
    count, n, _ = blocks.shape
    chunk = CHUNK if count % CHUNK == 0 else 1
    slots = ((count + rows) // 2 + UNROLL) // UNROLL * UNROLL * 2
    return pl.pallas_call(
        functools.partial(prep_kernel, rows),
        grid=(count // chunk,),
        in_specs=[IN_SMEM, IN_SMEM, IN_SMEM, pl.BlockSpec((chunk, n, n), lambda i: (i, 0, 0))],
        out_specs=[IN_VMEM, IN_VMEM, IN_SMEM, IN_SMEM, IN_SMEM],
        out_shape=[pltpu.VMEM((slots, n, 2 * n), BF16),
                   jax.ShapeDtypeStruct((rows, 1, n), F32),
                   jax.ShapeDtypeStruct((slots,), I32),
                   jax.ShapeDtypeStruct((slots // 2,), I32),
                   jax.ShapeDtypeStruct((1,), I32)],
        scratch_shapes=[pltpu.VMEM((n + 16, n), BF16), pltpu.SMEM((2,), I32)],
        compiler_params=pltpu.CompilerParams(vmem_limit_bytes=12 * MIB),
        cost_estimate=pl.CostEstimate(
            flops=2 * count * n * n * n, bytes_accessed=4 * blocks.size, transcendentals=0
        ),
        name="prep",
    )(ids, own, col, pltpu.with_memory_space_constraint(blocks, pltpu.HBM))


def apply_kernel(recur, mate, *refs):
    refs = list(refs)
    ids_ref, src_ref, row_ref, num_ref, w_ref, inv_ref = refs[:6]
    panels = refs[6:10]
    del refs[:10]
    olds = [refs.pop(0) for _ in range(2 if recur else 0)]
    mates = [refs.pop(0) for _ in range(2 if mate else 0)]
    outs = [refs.pop(0) for _ in range(2)]
    parts = refs[:-2]
    sp_ref, acc_ref = refs[-2:]
    half, kk, n = panels[0].shape
    for i, ref in enumerate(panels):
        v = ref[...]
        high = v.astype(BF16)
        sp_ref[i * half:(i + 1) * half, :kk] = high
        sp_ref[i * half:(i + 1) * half, kk:] = (v - high.astype(F32)).astype(BF16)
    acc_ref[...] = jnp.zeros(acc_ref.shape, F32)

    def group(g, c):
        for u in range(UNROLL):
            p = g * UNROLL + u
            piece = jnp.concatenate([sp_ref[src_ref[2 * p]], sp_ref[src_ref[2 * p + 1]]], axis=1)
            w = w_ref[pl.ds(2 * p, 2)].reshape(2 * n, 2 * n)
            y = jnp.dot(piece, w, preferred_element_type=F32)
            r = row_ref[p]
            acc_ref[r] = acc_ref[r] + ((y[:kk, :n] + y[kk:, :n]) + (y[:kk, n:] + y[kk:, n:]))
        return c

    lax.fori_loop(0, num_ref[0], group, 0)
    scale = (2.0 if recur else 1.0) / half_width
    for i in range(2):
        span = slice(i * half, (i + 1) * half)
        now = panels[i][...]
        image = (now - acc_ref[span] * inv_ref[span] - center * now) * scale
        if recur:
            image = image - olds[i][...]
        outs[i][...] = image
        if mate:
            acc_ref[span] = image
            sp_ref2 = parts[-1]
            sp_ref2[span] = mates[i][...]
    if mate:
        count = len(parts) - 1
        me = ids_ref[1]
        each = 2 * half // count
        for s in range(count):
            at = pl.ds((me ^ s) * each, each)
            parts[s][:, :kk] = parts[-1][at]
            parts[s][:, kk:] = acc_ref[at]


def apply(ids, meta, pair, halo, old=(), mate=(), count=0):
    half, kk, n = pair[0].shape
    w = meta[3]
    out = [jax.ShapeDtypeStruct((half, kk, n), F32)] * 2
    if mate:
        out += [jax.ShapeDtypeStruct((2 * half // count, 2 * kk, n), F32)] * count
    args = (*pair, *halo, *old, *mate)
    scratch = [pltpu.VMEM((4 * half, 2 * kk, n), BF16), pltpu.VMEM((2 * half + 1, kk, n), F32)]
    if mate:
        scratch = [pltpu.VMEM((2 * half, kk, n), F32)] + scratch
    res = pl.pallas_call(
        functools.partial(apply_kernel, bool(old), bool(mate)),
        in_specs=[IN_SMEM] * 4 + [IN_VMEM] * (2 + len(args)),
        out_specs=[IN_VMEM] * len(out),
        out_shape=out,
        scratch_shapes=scratch,
        compiler_params=pltpu.CompilerParams(vmem_limit_bytes=12 * MIB),
        cost_estimate=pl.CostEstimate(
            flops=8 * w.shape[0] * n * n * kk, bytes_accessed=2 * w.size, transcendentals=0
        ),
        name="apply" + "_recur" * bool(old) + "_parts" * bool(mate),
    )(ids, *meta, *args)
    return tuple(res[:2]), tuple(res[2:])


def factor_kernel(nodes, g_ref, out_ref, both_ref):
    n = g_ref.shape[0]
    p = 8
    lines = lax.broadcasted_iota(I32, (n, n), 0)
    lanes = lax.broadcasted_iota(I32, (n, n), 1)
    both_ref[:, :n] = g_ref[...] * (1.0 / nodes)
    both_ref[:, n:] = jnp.where(lines == lanes, 1.0, 0.0).astype(F32)
    sub = lax.broadcasted_iota(I32, (p, n), 0)
    for j in range(0, n, p):
        left = both_ref[j:j + p, :n]
        right = both_ref[j:j + p, n:]
        cols = [jnp.broadcast_to(left[:, j + i:j + i + 1], (p, n)) for i in range(p)]
        pivot = jnp.zeros((p, n), F32)
        for i in range(p):
            own = jnp.broadcast_to(cols[i][i:i + 1], (p, n))
            pivot = jnp.where(sub == i, own, pivot)
            if i + 1 < p:
                ratio = jnp.where(sub > i, cols[i] / own, 0.0)
                for k in range(i + 1, p):
                    cols[k] = cols[k] - ratio * jnp.broadcast_to(cols[k][i:i + 1], (p, n))
                left = left - ratio * jnp.broadcast_to(left[i:i + 1], (p, n))
                right = right - ratio * jnp.broadcast_to(right[i:i + 1], (p, n))
        root = lax.rsqrt(pivot)
        left = left * root
        right = right * root
        out_ref[j:j + p] = right
        if j + p < n:
            change = tn(left, jnp.concatenate([left, right], axis=1))
            both_ref[j + p:] = both_ref[j + p:] - change[j + p:]


def inverse_factor(gram, nodes):
    n = gram.shape[0]
    return call(
        functools.partial(factor_kernel, nodes), "factor", [(n, n)], gram,
        scratch=[pltpu.VMEM((n, 2 * n), F32)],
    )[0]


def gathered(ids_ref, parts, b, x_ref):
    each = parts[0].shape[1]
    me = ids_ref[1]
    for s, part in enumerate(parts):
        x_ref[b, pl.ds(pl.multiple_of((me ^ s) * each, each), each)] = part[b]
    return x_ref[b]


def gram_kernel(ids_ref, *refs):
    parts, (f_ref, g_ref) = refs[:-2], refs[-2:]
    total = jnp.zeros(g_ref.shape, F32)
    for b in range(f_ref.shape[0]):
        f = gathered(ids_ref, parts, b, f_ref)
        total = total + nt(f, f)
    g_ref[...] = total


def cross_kernel(ids_ref, f_ref, *refs):
    parts, (k_ref, x_ref) = refs[:-2], refs[-2:]
    total = jnp.zeros(k_ref.shape, F32)
    for b in range(f_ref.shape[0]):
        total = total + nt(f_ref[b], gathered(ids_ref, parts, b, x_ref))
    k_ref[...] = total


def turn_kernel(ids_ref, inv_ref, *refs):
    parts, (f_ref, g_ref, x_ref) = refs[:-3], refs[-3:]
    total = jnp.zeros(g_ref.shape, F32)
    for b in range(f_ref.shape[0]):
        f = nn(inv_ref[...], gathered(ids_ref, parts, b, x_ref))
        f_ref[b] = f
        total = total + nt(f, f)
    g_ref[...] = total


def turn_cross_kernel(ids_ref, inv_ref, f_ref, *refs):
    parts, (k_ref, x_ref) = refs[:-2], refs[-2:]
    total = jnp.zeros(k_ref.shape, F32)
    for b in range(f_ref.shape[0]):
        z = nn(inv_ref[...], gathered(ids_ref, parts, b, x_ref))
        total = total + nt(f_ref[b], z)
    k_ref[...] = total


def basis_kernel(ids_ref, inv_ref, f_ref, *refs):
    parts, x_ref = refs[:-1], refs[-1]
    each = parts[0].shape[1]
    me = ids_ref[1]
    for b in range(f_ref.shape[0]):
        x_ref[b] = nn(inv_ref[...], f_ref[b])
        for s, part in enumerate(parts):
            part[b] = x_ref[b, pl.ds(pl.multiple_of((me ^ s) * each, each), each)]


def proj_kernel(nodes, ids_ref, *refs):
    pairs = len(refs[:6]) // 3
    parts, x_ref = refs[6:-1], refs[-1]
    each = parts[0].shape[1]
    me = ids_ref[1]
    for i in range(pairs):
        inv_ref, k_ref, g_ref = refs[3 * i:3 * i + 3]
        image = (half_width * k_ref[...] + center * g_ref[...]) * (1.0 / nodes)
        x_ref[...] = nt(nn(inv_ref[...], image), inv_ref[...])
        for s, part in enumerate(parts):
            part[i] = x_ref[pl.ds(pl.multiple_of((me ^ s) * each, each), each)]


def slot_row(slot, half, odd):
    return slot + half * (1 - odd) * jnp.where(slot >= half, -1, 1)


def split_kernel(ids_ref, start_ref, *outs):
    half, kk, n = outs[0].shape
    odd = ids_ref[0] % 2
    for slot in range(2 * half):
        row = slot_row(slot, half, odd)
        piece = start_ref[:, pl.ds(pl.multiple_of(row * n, n), n)]
        for i in range(2):
            outs[2 * i + slot // half][slot % half] = piece[i * kk:(i + 1) * kk]


def join_kernel(half, ids_ref, *refs):
    parts, out_ref = refs[:-1], refs[-1]
    each, _, n = parts[0].shape
    odd = ids_ref[0] % 2
    me = ids_ref[1]
    for s, part in enumerate(parts):
        for b in range(each):
            row = slot_row((me ^ s) * each + b, half, odd)
            out_ref[:, pl.ds(pl.multiple_of(row * n, n), n)] = part[b]


def exchange(pair):
    count = lax.axis_size("node")
    even = [(i, i ^ 1) for i in range(count)]
    odd = [(i, (i - 1 if i % 2 == 0 else i + 1) % count) for i in range(count)]
    return lax.ppermute(pair[0], "node", even), lax.ppermute(pair[1], "node", odd)


def swap(value, axis, hop):
    return lax.ppermute(value, axis, [(i, i ^ hop) for i in range(lax.axis_size(axis))])


def swapped(parts):
    return [parts[0]] + [swap(parts[s], "col", s) for s in range(1, len(parts))]


def summed(value, *axes, hop=1):
    first = hop
    for axis in axes:
        hop = first
        while hop < lax.axis_size(axis):
            value = value + swap(value, axis, hop)
            hop *= 2
    return value


def body(blocks, owner_row, block_col, start):
    cols_here, width = start.shape
    block = blocks.shape[1]
    slots = width // block
    half = slots // 2
    count = lax.axis_size("col")
    nodes = width * lax.axis_size("node")
    vecs = cols_here * count
    each = cols_here // 2
    quarter = slots // count
    square = (vecs, vecs)
    wide = (quarter, vecs, block)
    held = pltpu.VMEM(wide, F32)
    ids = jnp.stack([lax.axis_index("node"), lax.axis_index("col")]).astype(I32)

    halves = call(split_kernel, "split", [(half, each, block)] * 4, ids, start, scalars=1)
    before = [tuple(halves[:2]), tuple(halves[2:])]
    w, inv, src, row, num = prep(ids, owner_row, block_col, blocks, slots)
    meta = (src, row, num, w, inv)

    def advance(now, before=((), ()), parts=False, halo=None):
        first, _ = apply(ids, meta, now[0], halo or exchange(now[0]), before[0])
        mate = first if parts else ()
        second, out = apply(ids, meta, now[1], exchange(now[1]), before[1], mate, count)
        return [first, second], (swapped(out) if parts else None)

    now, _ = advance(before)
    for step in range(DEGREE - 1):
        after, parts = advance(now, before, step == DEGREE - 2)
        before, now = now, after
    panel, gram_first = call(gram_kernel, "gram", [wide, square], ids, *parts, scalars=1)
    gram = summed(gram_first, "col", "node")
    after, parts = advance(now, parts=True)
    before, now = now, after
    (cross_first,) = call(
        cross_kernel, "cross", [square], ids, panel, *parts, scalars=1, scratch=[held]
    )
    inverse_first = inverse_factor(gram, nodes)
    for step in range(DEGREE - 1):
        if step == DEGREE - 2:
            held_back, inverse_first = lax.optimization_barrier((before[1], inverse_first))
            before = [before[0], held_back]
        after, parts = advance(now, before, step == DEGREE - 2)
        before, now = now, after

    parts, halo = lax.optimization_barrier((parts, exchange(now[0])))
    turned, gram_last = call(
        turn_kernel, "turn", [wide, square], ids, inverse_first, *parts, scalars=1, scratch=[held]
    )
    gram = summed(gram_last, "col", "node")
    _, parts = advance(now, parts=True, halo=halo)
    (cross_last,) = call(
        turn_cross_kernel, "turn_cross", [square], ids, inverse_first, turned, *parts,
        scalars=1, scratch=[held],
    )
    inverse_last = inverse_factor(gram, nodes)
    parts = call(
        basis_kernel, "basis", [(quarter, cols_here, block)] * count, ids, inverse_last, turned,
        scalars=1, scratch=[held],
    )
    arrived = swapped(parts)
    parts = call(
        functools.partial(proj_kernel, nodes), "proj", [(2, cols_here, vecs)] * count, ids,
        inverse_first, cross_first, gram_first, inverse_last, cross_last, gram_last,
        scalars=1, scratch=[pltpu.VMEM(square, F32)],
    )
    projected = sum(swapped(parts))
    projected = projected + swap(projected, "node", 1)
    projected, arrived = lax.optimization_barrier((projected, arrived))
    (basis,) = call(
        functools.partial(join_kernel, half), "join", [(cols_here, width)], ids, *arrived, scalars=1
    )
    projected = summed(projected, "node", hop=2)
    return basis, projected[0], projected[1]


def solution(mesh):
    placed = (P("node", None, None), P("node", None), P("node", None), P("col", "node"))
    return jax.shard_map(
        body,
        mesh=mesh,
        in_specs=placed,
        out_specs=(P("col", "node"), P("col", None), P("col", None)),
        check_vma=False,
    )
```

```python
import functools
import math
import jax
import jax.numpy as jnp
from jax import lax
from jax.experimental import pallas as pl
from jax.experimental.pallas import tpu as pltpu
from jax.sharding import PartitionSpec as P

DEGREE = 4
UNROLL = 48
CHUNK = 6
STREAMS = 4
APPLY_BYTES = 4 << 20
F32, BF16, I32 = jnp.float32, jnp.bfloat16, jnp.int32
precise = lax.Precision.HIGHEST
center = 1.025
half_width = 0.975
MIB = 1 << 20
IN_VMEM = pl.BlockSpec(memory_space=pltpu.VMEM)
IN_SMEM = pl.BlockSpec(memory_space=pltpu.SMEM)


def nt(a, b):
    return lax.dot_general(
        a, b, (((1,), (1,)), ((), ())), precision=precise, preferred_element_type=F32
    )


def tn(a, b):
    return lax.dot_general(
        a, b, (((0,), (0,)), ((), ())), precision=precise, preferred_element_type=F32
    )


def nn(a, b):
    return jnp.dot(a, b, precision=precise, preferred_element_type=F32)


def call(kernel, name, outs, *args, scalars=0, scratch=(), cost=None):
    return pl.pallas_call(
        kernel,
        in_specs=[IN_SMEM] * scalars + [IN_VMEM] * (len(args) - scalars),
        out_specs=[IN_VMEM] * len(outs),
        out_shape=[jax.ShapeDtypeStruct(o, F32) for o in outs],
        scratch_shapes=list(scratch),
        compiler_params=pltpu.CompilerParams(vmem_limit_bytes=12 * MIB),
        cost_estimate=cost,
        name=name,
    )(*args)


def prep_kernel(rows, ids_ref, own_ref, col_ref, *refs):
    blks, (w_ref, inv_ref, table_ref, eye_ref) = refs[:-4], refs[-4:]
    chunk, n, _ = blks[0].shape
    half = rows // 2
    step = pl.program_id(0)
    me = ids_ref[0]
    odd = me % 2
    count = own_ref.shape[1]

    @pl.when(step == 0)
    def _():
        table_ref[0] = me
        table_ref[1] = ids_ref[1]
        inv_ref[...] = jnp.zeros(inv_ref.shape, F32)
        lines = lax.broadcasted_iota(I32, eye_ref.shape, 0)
        lanes = lax.broadcasted_iota(I32, eye_ref.shape, 1)
        eye_ref[...] = jnp.where((lines == lanes) | (lines >= n), 1.0, 0.0).astype(BF16)

    for i, blk_ref in enumerate(blks):
        for c in range(chunk):
            b = (step * len(blks) + i) * chunk + c
            r = own_ref[0, b]
            k = col_ref[0, b]
            owner = k // rows
            local = k - owner * rows
            upper = (local >= half).astype(I32)
            near = local - half * upper
            swap = odd * upper + (1 - odd) * (1 - upper)
            slot = jnp.where(owner == me, near + half * swap, 2 * half + near + half * (1 - swap))
            top = (r >= half).astype(I32)
            r_at = r + half * (1 - odd) * (1 - 2 * top)
            table_ref[2 + b] = slot
            table_ref[2 + count + b] = r_at
            a = blk_ref[c]
            high = a.astype(BF16)
            low = (a - high.astype(F32)).astype(BF16)
            both = jnp.concatenate([high, low], axis=0)
            t = lax.dot_general(
                eye_ref[...], both, (((1,), (1,)), ((), ())), preferred_element_type=F32
            )
            w_ref[b] = t[:n].astype(BF16)
            inv_ref[r_at] = inv_ref[r_at] + (t[n:n + 1, :n] + t[n:n + 1, n:])

    @pl.when(step == pl.num_programs(0) - 1)
    def _():
        inv_ref[...] = 1.0 / inv_ref[...]


def prep(ids, own, col, blocks, rows):
    count, n, _ = blocks.shape
    chunk = math.gcd(count, STREAMS * CHUNK) // STREAMS
    blocks = pltpu.with_memory_space_constraint(blocks, pltpu.HBM)

    def stream(i):
        return pl.BlockSpec((chunk, n, n), lambda step: (STREAMS * step + i, 0, 0))

    return pl.pallas_call(
        functools.partial(prep_kernel, rows),
        grid=(count // (STREAMS * chunk),),
        in_specs=[IN_SMEM] * 3 + [stream(i) for i in range(STREAMS)],
        out_specs=[IN_VMEM, IN_VMEM, IN_SMEM],
        out_shape=[pltpu.VMEM((count, n, 2 * n), BF16),
                   jax.ShapeDtypeStruct((rows, 1, n), F32),
                   jax.ShapeDtypeStruct((2 + 2 * count,), I32)],
        scratch_shapes=[pltpu.VMEM((n + 16, n), BF16)],
        compiler_params=pltpu.CompilerParams(vmem_limit_bytes=12 * MIB),
        cost_estimate=pl.CostEstimate(
            flops=2 * count * n * n * n, bytes_accessed=4 * blocks.size, transcendentals=0
        ),
        name="prep",
    )(ids, own, col, *[blocks] * STREAMS)


def apply_kernel(recur, mate, *refs):
    refs = list(refs)
    table_ref, w_ref, inv_ref = refs[:3]
    panels = refs[3:7]
    del refs[:7]
    olds = [refs.pop(0) for _ in range(2 if recur else 0)]
    mates = [refs.pop(0) for _ in range(2 if mate else 0)]
    outs = [refs.pop(0) for _ in range(2)]
    parts = refs[:-2]
    sp_ref, acc_ref = refs[-2:]
    half, kk, n = panels[0].shape
    blocks = w_ref.shape[0]
    for i, ref in enumerate(panels):
        v = ref[...]
        high = v.astype(BF16)
        sp_ref[i * half:(i + 1) * half, :kk] = high
        sp_ref[i * half:(i + 1) * half, kk:] = (v - high.astype(F32)).astype(BF16)
    acc_ref[...] = jnp.zeros(acc_ref.shape, F32)
    unroll = math.gcd(blocks, UNROLL)

    def group(g, c):
        for u in range(unroll):
            b = g * unroll + u
            y = jnp.dot(sp_ref[table_ref[2 + b]], w_ref[b], preferred_element_type=F32)
            r = table_ref[2 + blocks + b]
            acc_ref[r] = acc_ref[r] + ((y[:kk, :n] + y[kk:, :n]) + (y[:kk, n:] + y[kk:, n:]))
        return c

    lax.fori_loop(0, blocks // unroll, group, 0)
    scale = (2.0 if recur else 1.0) / half_width
    for i in range(2):
        span = slice(i * half, (i + 1) * half)
        now = panels[i][...]
        image = (now - acc_ref[span] * inv_ref[span] - center * now) * scale
        if recur:
            image = image - olds[i][...]
        outs[i][...] = image
        if mate:
            acc_ref[span] = image
            parts[-1][span] = mates[i][...]
    if mate:
        count = len(parts) - 1
        me = table_ref[1]
        each = 2 * half // count
        for s in range(count):
            at = pl.ds((me ^ s) * each, each)
            parts[s][:, :kk] = parts[-1][at]
            parts[s][:, kk:] = acc_ref[at]


def apply(meta, pair, halo, old=(), mate=(), count=0):
    half, kk, n = pair[0].shape
    out = [jax.ShapeDtypeStruct((half, kk, n), F32)] * 2
    if mate:
        out += [jax.ShapeDtypeStruct((2 * half // count, 2 * kk, n), F32)] * count
    args = (*pair, *halo, *old, *mate)
    scratch = [pltpu.VMEM((4 * half, 2 * kk, n), BF16), pltpu.VMEM((2 * half, kk, n), F32)]
    if mate:
        scratch = [pltpu.VMEM((2 * half, kk, n), F32)] + scratch
    res = pl.pallas_call(
        functools.partial(apply_kernel, bool(old), bool(mate)),
        in_specs=[IN_SMEM] + [IN_VMEM] * (2 + len(args)),
        out_specs=[IN_VMEM] * len(out),
        out_shape=out,
        scratch_shapes=scratch,
        compiler_params=pltpu.CompilerParams(vmem_limit_bytes=12 * MIB),
        cost_estimate=pl.CostEstimate(
            flops=0, bytes_accessed=APPLY_BYTES, transcendentals=0
        ),
        name="apply" + "_recur" * bool(old) + "_parts" * bool(mate),
    )(*meta, *args)
    return tuple(res[:2]), tuple(res[2:])


def factor_kernel(nodes, g_ref, out_ref, both_ref):
    n = g_ref.shape[0]
    p = 8
    lines = lax.broadcasted_iota(I32, (n, n), 0)
    lanes = lax.broadcasted_iota(I32, (n, n), 1)
    both_ref[:, :n] = g_ref[...] * (1.0 / nodes)
    both_ref[:, n:] = jnp.where(lines == lanes, 1.0, 0.0).astype(F32)
    sub = lax.broadcasted_iota(I32, (p, n), 0)
    for j in range(0, n, p):
        left = both_ref[j:j + p, :n]
        right = both_ref[j:j + p, n:]
        cols = [jnp.broadcast_to(left[:, j + i:j + i + 1], (p, n)) for i in range(p)]
        pivot = jnp.zeros((p, n), F32)
        for i in range(p):
            own = jnp.broadcast_to(cols[i][i:i + 1], (p, n))
            pivot = jnp.where(sub == i, own, pivot)
            if i + 1 < p:
                ratio = jnp.where(sub > i, cols[i] / own, 0.0)
                for k in range(i + 1, p):
                    cols[k] = cols[k] - ratio * jnp.broadcast_to(cols[k][i:i + 1], (p, n))
                left = left - ratio * jnp.broadcast_to(left[i:i + 1], (p, n))
                right = right - ratio * jnp.broadcast_to(right[i:i + 1], (p, n))
        root = lax.rsqrt(pivot)
        left = left * root
        right = right * root
        out_ref[j:j + p] = right
        if j + p < n:
            change = tn(left, jnp.concatenate([left, right], axis=1))
            both_ref[j + p:] = both_ref[j + p:] - change[j + p:]


def inverse_factor(gram, nodes):
    n = gram.shape[0]
    return call(
        functools.partial(factor_kernel, nodes), "factor", [(n, n)], gram,
        scratch=[pltpu.VMEM((n, 2 * n), F32)],
    )[0]


def gathered(ids_ref, parts, b, x_ref):
    each = parts[0].shape[1]
    me = ids_ref[1]
    for s, part in enumerate(parts):
        x_ref[b, pl.ds(pl.multiple_of((me ^ s) * each, each), each)] = part[b]
    return x_ref[b]


def gram_kernel(ids_ref, *refs):
    parts, (f_ref, g_ref) = refs[:-2], refs[-2:]
    total = jnp.zeros(g_ref.shape, F32)
    for b in range(f_ref.shape[0]):
        f = gathered(ids_ref, parts, b, f_ref)
        total = total + nt(f, f)
    g_ref[...] = total


def cross_kernel(ids_ref, f_ref, *refs):
    parts, (k_ref, x_ref) = refs[:-2], refs[-2:]
    total = jnp.zeros(k_ref.shape, F32)
    for b in range(f_ref.shape[0]):
        total = total + nt(f_ref[b], gathered(ids_ref, parts, b, x_ref))
    k_ref[...] = total


def turn_kernel(ids_ref, inv_ref, *refs):
    parts, (f_ref, g_ref, x_ref) = refs[:-3], refs[-3:]
    total = jnp.zeros(g_ref.shape, F32)
    for b in range(f_ref.shape[0]):
        f = nn(inv_ref[...], gathered(ids_ref, parts, b, x_ref))
        f_ref[b] = f
        total = total + nt(f, f)
    g_ref[...] = total


def turn_cross_kernel(ids_ref, inv_ref, f_ref, *refs):
    parts, (k_ref, x_ref) = refs[:-2], refs[-2:]
    total = jnp.zeros(k_ref.shape, F32)
    for b in range(f_ref.shape[0]):
        z = nn(inv_ref[...], gathered(ids_ref, parts, b, x_ref))
        total = total + nt(f_ref[b], z)
    k_ref[...] = total


def basis_kernel(ids_ref, inv_ref, f_ref, *refs):
    parts, x_ref = refs[:-1], refs[-1]
    each = parts[0].shape[1]
    me = ids_ref[1]
    for b in range(f_ref.shape[0]):
        x_ref[b] = nn(inv_ref[...], f_ref[b])
        for s, part in enumerate(parts):
            part[b] = x_ref[b, pl.ds(pl.multiple_of((me ^ s) * each, each), each)]


def proj_kernel(nodes, ids_ref, *refs):
    pairs = len(refs[:6]) // 3
    parts, x_ref = refs[6:-1], refs[-1]
    each = parts[0].shape[1]
    me = ids_ref[1]
    for i in range(pairs):
        inv_ref, k_ref, g_ref = refs[3 * i:3 * i + 3]
        image = (half_width * k_ref[...] + center * g_ref[...]) * (1.0 / nodes)
        x_ref[...] = nt(nn(inv_ref[...], image), inv_ref[...])
        for s, part in enumerate(parts):
            part[i] = x_ref[pl.ds(pl.multiple_of((me ^ s) * each, each), each)]


def slot_row(slot, half, odd):
    return slot + half * (1 - odd) * jnp.where(slot >= half, -1, 1)


def split_kernel(ids_ref, start_ref, *outs):
    half, kk, n = outs[0].shape
    odd = ids_ref[0] % 2
    for slot in range(2 * half):
        row = slot_row(slot, half, odd)
        piece = start_ref[:, pl.ds(pl.multiple_of(row * n, n), n)]
        for i in range(2):
            outs[2 * i + slot // half][slot % half] = piece[i * kk:(i + 1) * kk]


def join_kernel(half, ids_ref, *refs):
    parts, out_ref = refs[:-1], refs[-1]
    each, _, n = parts[0].shape
    odd = ids_ref[0] % 2
    me = ids_ref[1]
    for s, part in enumerate(parts):
        for b in range(each):
            row = slot_row((me ^ s) * each + b, half, odd)
            out_ref[:, pl.ds(pl.multiple_of(row * n, n), n)] = part[b]


def exchange(pair):
    count = lax.axis_size("node")
    even = [(i, i ^ 1) for i in range(count)]
    odd = [(i, (i - 1 if i % 2 == 0 else i + 1) % count) for i in range(count)]
    return lax.ppermute(pair[0], "node", even), lax.ppermute(pair[1], "node", odd)


def swap(value, axis, hop):
    return lax.ppermute(value, axis, [(i, i ^ hop) for i in range(lax.axis_size(axis))])


def swapped(parts):
    return [parts[0]] + [swap(parts[s], "col", s) for s in range(1, len(parts))]


def hops_of(*axes):
    return [(axis, 1 << i) for axis in axes for i in range((lax.axis_size(axis) - 1).bit_length())]


def body(blocks, owner_row, block_col, start):
    cols_here, width = start.shape
    block = blocks.shape[1]
    slots = width // block
    half = slots // 2
    count = lax.axis_size("col")
    nodes = width * lax.axis_size("node")
    vecs = cols_here * count
    each = cols_here // 2
    quarter = slots // count
    square = (vecs, vecs)
    wide = (quarter, vecs, block)
    held = pltpu.VMEM(wide, F32)
    ids = jnp.stack([lax.axis_index("node"), lax.axis_index("col")]).astype(I32)

    halves = call(split_kernel, "split", [(half, each, block)] * 4, ids, start, scalars=1)
    before = [tuple(halves[:2]), tuple(halves[2:])]
    w, inv, table = prep(ids, owner_row, block_col, blocks, slots)
    meta = (table, w, inv)

    def advance(now, before=((), ()), parts=False):
        first, _ = apply(meta, now[0], exchange(now[0]), before[0])
        mate = first if parts else ()
        second, out = apply(meta, now[1], exchange(now[1]), before[1], mate, count)
        return [first, second], out

    now, _ = advance(before)
    for step in range(DEGREE - 1):
        after, parts = advance(now, before, step == DEGREE - 2)
        before, now = now, after
    panel, gram_first = call(gram_kernel, "gram", [wide, square], ids, *swapped(parts), scalars=1)
    after, parts = advance(now, parts=True)
    before, now = now, after
    (cross_first,) = call(
        cross_kernel, "cross", [square], ids, panel, *swapped(parts), scalars=1, scratch=[held]
    )
    got, hops = None, hops_of("col", "node")
    gram = gram_first
    for step in range(DEGREE - 1):
        after = []
        for i in range(2):
            old, gram, got = lax.optimization_barrier((before[i], gram, got))
            if got is not None:
                gram = gram + got
            got = swap(gram, *hops.pop(0)) if hops else None
            mate = after[0] if i == 1 and step == DEGREE - 2 else ()
            done, parts = apply(meta, now[i], exchange(now[i]), old, mate, count)
            after.append(done)
            if got is not None:
                gram, got, _ = lax.optimization_barrier((gram, got, done))
        before, now = now, after
    if got is not None:
        gram = gram + got
    for hop in hops:
        gram = gram + swap(gram, *hop)
    inverse_first = inverse_factor(gram, nodes)

    arrived, halo = lax.optimization_barrier((swapped(parts), exchange(now[0])))
    halos = [halo, exchange(now[1])]
    turned, gram_last = call(
        turn_kernel, "turn", [wide, square], ids, inverse_first, *arrived, scalars=1, scratch=[held]
    )
    gram = gram_last
    for i, hop in enumerate(hops_of("col", "node")):
        got = swap(gram, *hop)
        if i == 2:
            got, halos[1] = lax.optimization_barrier((got, halos[1]))
        gram = gram + got
    first, _ = apply(meta, now[0], halos[0])
    _, parts = apply(meta, now[1], halos[1], (), first, count)
    (cross_last,) = call(
        turn_cross_kernel, "turn_cross", [square], ids, inverse_first, turned, *swapped(parts),
        scalars=1, scratch=[held],
    )
    inverse_last = inverse_factor(gram, nodes)
    parts = call(
        basis_kernel, "basis", [(quarter, cols_here, block)] * count, ids, inverse_last, turned,
        scalars=1, scratch=[held],
    )
    arrived = swapped(parts)
    parts = call(
        functools.partial(proj_kernel, nodes), "proj", [(2, cols_here, vecs)] * count, ids,
        inverse_first, cross_first, gram_first, inverse_last, cross_last, gram_last,
        scalars=1, scratch=[pltpu.VMEM(square, F32)],
    )
    projected = sum(swapped(parts))
    for i, hop in enumerate(hops_of("node")):
        projected = projected + swap(projected, *hop)
        if i == 0:
            projected, arrived = lax.optimization_barrier((projected, arrived))
            (basis,) = call(
                functools.partial(join_kernel, half), "join", [(cols_here, width)], ids, *arrived, scalars=1
            )
    return basis, projected[0], projected[1]


def solution(mesh):
    placed = (P("node", None, None), P("node", None), P("node", None), P("col", "node"))
    return jax.shard_map(
        body,
        mesh=mesh,
        in_specs=placed,
        out_specs=(P("col", "node"), P("col", None), P("col", None)),
        check_vma=False,
    )
```

```python
import functools
import math
import jax
import jax.numpy as jnp
from jax import lax
from jax.experimental import pallas as pl
from jax.experimental.pallas import tpu as pltpu
from jax.sharding import PartitionSpec as P

DEGREE = 4
UNROLL = 48
CHUNK = 24
TURNS = 3
TIE_HALO = 1
TIE_IMAGE = 1
APPLY_BYTES = 4 << 20
F32, BF16, I32 = jnp.float32, jnp.bfloat16, jnp.int32
precise = lax.Precision.HIGHEST
center = 1.025
half_width = 0.975
MIB = 1 << 20
IN_VMEM = pl.BlockSpec(memory_space=pltpu.VMEM)
IN_SMEM = pl.BlockSpec(memory_space=pltpu.SMEM)


def nt(a, b):
    return lax.dot_general(
        a, b, (((1,), (1,)), ((), ())), precision=precise, preferred_element_type=F32
    )


def tn(a, b):
    return lax.dot_general(
        a, b, (((0,), (0,)), ((), ())), precision=precise, preferred_element_type=F32
    )


def nn(a, b):
    return jnp.dot(a, b, precision=precise, preferred_element_type=F32)


def call(kernel, name, outs, *args, scalars=0, scratch=(), cost=None):
    return pl.pallas_call(
        kernel,
        in_specs=[IN_SMEM] * scalars + [IN_VMEM] * (len(args) - scalars),
        out_specs=[IN_VMEM] * len(outs),
        out_shape=[jax.ShapeDtypeStruct(o, F32) for o in outs],
        scratch_shapes=list(scratch),
        compiler_params=pltpu.CompilerParams(vmem_limit_bytes=12 * MIB),
        cost_estimate=cost,
        name=name,
    )(*args)


def prep_kernel(rows, ids_ref, own_ref, col_ref, blk_ref, w_ref, inv_ref, table_ref, held_ref, eye_ref, sem_ref):
    count, n, _ = held_ref.shape
    steps = sem_ref.shape[0]
    chunk = count // steps
    half = rows // 2
    me = ids_ref[0]
    odd = me % 2

    def fetch(step):
        span = pl.ds(step * chunk, chunk)
        return pltpu.make_async_copy(blk_ref.at[span], held_ref.at[span], sem_ref.at[step])

    for step in range(steps):
        fetch(step).start()
    table_ref[0] = me
    table_ref[1] = ids_ref[1]
    inv_ref[...] = jnp.zeros(inv_ref.shape, F32)
    lines = lax.broadcasted_iota(I32, eye_ref.shape, 0)
    lanes = lax.broadcasted_iota(I32, eye_ref.shape, 1)
    eye_ref[...] = jnp.where((lines == lanes) | (lines >= n), 1.0, 0.0).astype(BF16)

    def pack(step, carry):
        fetch(step).wait()
        for c in range(chunk):
            b = step * chunk + c
            r = own_ref[0, b]
            k = col_ref[0, b]
            owner = k // rows
            local = k - owner * rows
            upper = (local >= half).astype(I32)
            near = local - half * upper
            swap = odd * upper + (1 - odd) * (1 - upper)
            slot = jnp.where(owner == me, near + half * swap, 2 * half + near + half * (1 - swap))
            top = (r >= half).astype(I32)
            r_at = r + half * (1 - odd) * (1 - 2 * top)
            table_ref[2 + b] = slot
            table_ref[2 + count + b] = r_at
            a = held_ref[b]
            if c % TURNS:
                t = a.T
                high = t.astype(BF16)
                w_ref[b, :, :n] = high
                w_ref[b, :, n:] = (t - high.astype(F32)).astype(BF16)
                inv_ref[r_at] = inv_ref[r_at] + jnp.sum(t, axis=0, keepdims=True)
            else:
                high = a.astype(BF16)
                low = (a - high.astype(F32)).astype(BF16)
                both = jnp.concatenate([high, low], axis=0)
                t = lax.dot_general(
                    eye_ref[...], both, (((1,), (1,)), ((), ())), preferred_element_type=F32
                )
                w_ref[b] = t[:n].astype(BF16)
                inv_ref[r_at] = inv_ref[r_at] + (t[n:n + 1, :n] + t[n:n + 1, n:])
        return carry

    lax.fori_loop(0, steps, pack, 0)
    inv_ref[...] = 1.0 / inv_ref[...]


def prep(ids, own, col, blocks, rows):
    count, n, _ = blocks.shape
    own, col, blocks = (pltpu.with_memory_space_constraint(x, pltpu.HBM) for x in (own, col, blocks))
    return pl.pallas_call(
        functools.partial(prep_kernel, rows),
        in_specs=[IN_SMEM] * 3 + [pl.BlockSpec(memory_space=pl.ANY)],
        out_specs=[IN_VMEM, IN_VMEM, IN_SMEM],
        out_shape=[pltpu.VMEM((count, n, 2 * n), BF16),
                   jax.ShapeDtypeStruct((rows, 1, n), F32),
                   jax.ShapeDtypeStruct((2 + 2 * count,), I32)],
        scratch_shapes=[
            pltpu.VMEM(blocks.shape, F32),
            pltpu.VMEM((n + 16, n), BF16),
            pltpu.SemaphoreType.DMA((count // math.gcd(count, CHUNK),)),
        ],
        compiler_params=pltpu.CompilerParams(vmem_limit_bytes=24 * MIB),
        cost_estimate=pl.CostEstimate(
            flops=2 * count * n * n * n, bytes_accessed=4 * blocks.size, transcendentals=0
        ),
        name="prep",
    )(ids, own, col, blocks)


def apply_kernel(recur, mate, *refs):
    refs = list(refs)
    table_ref, w_ref, inv_ref = refs[:3]
    panels = refs[3:7]
    del refs[:7]
    olds = [refs.pop(0) for _ in range(2 if recur else 0)]
    mates = [refs.pop(0) for _ in range(2 if mate else 0)]
    outs = [refs.pop(0) for _ in range(2)]
    parts = refs[:-2]
    sp_ref, acc_ref = refs[-2:]
    half, kk, n = panels[0].shape
    blocks = w_ref.shape[0]
    for i, ref in enumerate(panels):
        v = ref[...]
        high = v.astype(BF16)
        sp_ref[i * half:(i + 1) * half, :kk] = high
        sp_ref[i * half:(i + 1) * half, kk:] = (v - high.astype(F32)).astype(BF16)
    acc_ref[...] = jnp.zeros(acc_ref.shape, F32)
    unroll = math.gcd(blocks, UNROLL)

    def group(g, c):
        for u in range(unroll):
            b = g * unroll + u
            y = jnp.dot(sp_ref[table_ref[2 + b]], w_ref[b], preferred_element_type=F32)
            r = table_ref[2 + blocks + b]
            acc_ref[r] = acc_ref[r] + ((y[:kk, :n] + y[kk:, :n]) + (y[:kk, n:] + y[kk:, n:]))
        return c

    lax.fori_loop(0, blocks // unroll, group, 0)
    scale = (2.0 if recur else 1.0) / half_width
    for i in range(2):
        span = slice(i * half, (i + 1) * half)
        now = panels[i][...]
        image = (now - acc_ref[span] * inv_ref[span] - center * now) * scale
        if recur:
            image = image - olds[i][...]
        outs[i][...] = image
        if mate:
            acc_ref[span] = image
            parts[-1][span] = mates[i][...]
    if mate:
        count = len(parts) - 1
        me = table_ref[1]
        each = 2 * half // count
        for s in range(count):
            at = pl.ds((me ^ s) * each, each)
            parts[s][:, :kk] = parts[-1][at]
            parts[s][:, kk:] = acc_ref[at]


def apply(meta, pair, halo, old=(), mate=(), count=0):
    half, kk, n = pair[0].shape
    out = [jax.ShapeDtypeStruct((half, kk, n), F32)] * 2
    if mate:
        out += [jax.ShapeDtypeStruct((2 * half // count, 2 * kk, n), F32)] * count
    args = (*pair, *halo, *old, *mate)
    scratch = [pltpu.VMEM((4 * half, 2 * kk, n), BF16), pltpu.VMEM((2 * half, kk, n), F32)]
    if mate:
        scratch = [pltpu.VMEM((2 * half, kk, n), F32)] + scratch
    res = pl.pallas_call(
        functools.partial(apply_kernel, bool(old), bool(mate)),
        in_specs=[IN_SMEM] + [IN_VMEM] * (2 + len(args)),
        out_specs=[IN_VMEM] * len(out),
        out_shape=out,
        scratch_shapes=scratch,
        compiler_params=pltpu.CompilerParams(vmem_limit_bytes=12 * MIB),
        cost_estimate=pl.CostEstimate(
            flops=0, bytes_accessed=APPLY_BYTES, transcendentals=0
        ),
        name="apply" + "_recur" * bool(old) + "_parts" * bool(mate),
    )(*meta, *args)
    return tuple(res[:2]), tuple(res[2:])


def factor_kernel(nodes, g_ref, out_ref):
    n = g_ref.shape[0]
    p = 8
    out_ref[...] = g_ref[...] * (1.0 / nodes)
    sub = lax.broadcasted_iota(I32, (p, n), 0)
    lane = lax.broadcasted_iota(I32, (p, n), 1)
    for j in range(0, n, p):
        rows = out_ref[j:j + p]
        cols = [jnp.broadcast_to(rows[:, j + i:j + i + 1], (p, n)) for i in range(p)]
        rows = jnp.where((lane >= j) & (lane < j + p), jnp.where(lane - j == sub, 1.0, 0.0), rows)
        for i in range(p):
            root = lax.rsqrt(jnp.broadcast_to(cols[i][i:i + 1], (p, n)))
            ratio = jnp.where(sub > i, cols[i] * root, 0.0)
            scale = jnp.where(sub == i, root, 1.0)
            for k in range(i + 1, p):
                cols[k] = cols[k] - ratio * (jnp.broadcast_to(cols[k][i:i + 1], (p, n)) * root)
            rows = rows * scale - ratio * (jnp.broadcast_to(rows[i:i + 1], (p, n)) * root)
        out_ref[j:j + p] = jnp.where(lane < j + p, rows, 0.0)
        if j + p < n:
            change = nn(rows.T[j + p:], rows)
            lanes = lax.broadcasted_iota(I32, change.shape, 1)
            rest = out_ref[j + p:]
            out_ref[j + p:] = jnp.where((lanes >= j) & (lanes < j + p), 0.0, rest) - change


def inverse_factor(gram, nodes):
    n = gram.shape[0]
    return call(
        functools.partial(factor_kernel, nodes), "factor", [(n, n)], gram,
    )[0]


def gathered(ids_ref, parts, b, x_ref):
    each = parts[0].shape[1]
    me = ids_ref[1]
    for s, part in enumerate(parts):
        x_ref[b, pl.ds(pl.multiple_of((me ^ s) * each, each), each)] = part[b]
    return x_ref[b]


def gram_kernel(ids_ref, *refs):
    parts, (f_ref, g_ref) = refs[:-2], refs[-2:]
    total = jnp.zeros(g_ref.shape, F32)
    for b in range(f_ref.shape[0]):
        f = gathered(ids_ref, parts, b, f_ref)
        total = total + nt(f, f)
    g_ref[...] = total


def cross_kernel(ids_ref, f_ref, g_ref, *refs):
    parts, (k_ref, x_ref) = refs[:-2], refs[-2:]
    total = jnp.zeros(k_ref.shape, F32)
    for b in range(f_ref.shape[0]):
        total = total + nt(f_ref[b], gathered(ids_ref, parts, b, x_ref))
    k_ref[...] = half_width * total + center * g_ref[...]


def turn_kernel(ids_ref, inv_ref, *refs):
    parts, (f_ref, g_ref, x_ref) = refs[:-3], refs[-3:]
    total = jnp.zeros(g_ref.shape, F32)
    for b in range(f_ref.shape[0]):
        f = nn(inv_ref[...], gathered(ids_ref, parts, b, x_ref))
        f_ref[b] = f
        total = total + nt(f, f)
    g_ref[...] = total


def turn_cross_kernel(ids_ref, inv_ref, f_ref, g_ref, first_ref, *refs):
    parts, (k_ref, x_ref) = refs[:-2], refs[-2:]
    total = jnp.zeros(g_ref.shape, F32)
    for b in range(f_ref.shape[0]):
        z = nn(inv_ref[...], gathered(ids_ref, parts, b, x_ref))
        total = total + nt(f_ref[b], z)
    k_ref[0] = first_ref[...]
    k_ref[1] = half_width * total + center * g_ref[...]


def basis_kernel(ids_ref, inv_ref, f_ref, *refs):
    parts, x_ref = refs[:-1], refs[-1]
    each = parts[0].shape[1]
    me = ids_ref[1]
    for b in range(f_ref.shape[0]):
        x_ref[b] = nn(inv_ref[...], f_ref[b])
        for s, part in enumerate(parts):
            part[b] = x_ref[b, pl.ds(pl.multiple_of((me ^ s) * each, each), each)]


def proj_kernel(nodes, ids_ref, first_ref, last_ref, image_ref, *refs):
    parts, x_ref = refs[:-1], refs[-1]
    each = parts[0].shape[1]
    me = ids_ref[1]
    for i, inv_ref in enumerate((first_ref, last_ref)):
        x_ref[...] = nt(nn(inv_ref[...], image_ref[i] * (1.0 / nodes)), inv_ref[...])
        for s, part in enumerate(parts):
            part[i] = x_ref[pl.ds(pl.multiple_of((me ^ s) * each, each), each)]


def slot_row(slot, half, odd):
    return slot + half * (1 - odd) * jnp.where(slot >= half, -1, 1)


def split_kernel(ids_ref, start_ref, *outs):
    half, kk, n = outs[0].shape
    odd = ids_ref[0] % 2
    for slot in range(2 * half):
        row = slot_row(slot, half, odd)
        piece = start_ref[:, pl.ds(pl.multiple_of(row * n, n), n)]
        for i in range(2):
            outs[2 * i + slot // half][slot % half] = piece[i * kk:(i + 1) * kk]


def join_kernel(half, ids_ref, *refs):
    parts, out_ref = refs[:-1], refs[-1]
    each, _, n = parts[0].shape
    odd = ids_ref[0] % 2
    me = ids_ref[1]
    for s, part in enumerate(parts):
        for b in range(each):
            row = slot_row((me ^ s) * each + b, half, odd)
            out_ref[:, pl.ds(pl.multiple_of(row * n, n), n)] = part[b]


def exchange(pair):
    count = lax.axis_size("node")
    even = [(i, i ^ 1) for i in range(count)]
    odd = [(i, (i - 1 if i % 2 == 0 else i + 1) % count) for i in range(count)]
    return lax.ppermute(pair[0], "node", even), lax.ppermute(pair[1], "node", odd)


def swap(value, axis, hop):
    return lax.ppermute(value, axis, [(i, i ^ hop) for i in range(lax.axis_size(axis))])


def swapped(parts):
    return [parts[0]] + [swap(parts[s], "col", s) for s in range(1, len(parts))]


def hops_of(*axes):
    return [(axis, 1 << i) for axis in axes for i in range((lax.axis_size(axis) - 1).bit_length())]


def body(blocks, owner_row, block_col, start):
    cols_here, width = start.shape
    block = blocks.shape[1]
    slots = width // block
    half = slots // 2
    count = lax.axis_size("col")
    nodes = width * lax.axis_size("node")
    vecs = cols_here * count
    each = cols_here // 2
    quarter = slots // count
    square = (vecs, vecs)
    wide = (quarter, vecs, block)
    held = pltpu.VMEM(wide, F32)
    ids = jnp.stack([lax.axis_index("node"), lax.axis_index("col")]).astype(I32)

    halves = call(split_kernel, "split", [(half, each, block)] * 4, ids, start, scalars=1)
    before = [tuple(halves[:2]), tuple(halves[2:])]
    w, inv, table = prep(ids, owner_row, block_col, blocks, slots)
    meta = (table, w, inv)

    def advance(now, before=((), ()), parts=False):
        first, _ = apply(meta, now[0], exchange(now[0]), before[0])
        mate = first if parts else ()
        second, out = apply(meta, now[1], exchange(now[1]), before[1], mate, count)
        return [first, second], out

    now, _ = advance(before)
    for step in range(DEGREE - 1):
        after, parts = advance(now, before, step == DEGREE - 2)
        before, now = now, after
    panel, gram_first = call(gram_kernel, "gram", [wide, square], ids, *swapped(parts), scalars=1)
    after, parts = advance(now, parts=True)
    before, now = now, after
    image = swapped(parts)
    got, hops = None, hops_of("col", "node")
    gram = gram_first
    for step in range(DEGREE - 1):
        after = []
        for i in range(2):
            old, gram, got = lax.optimization_barrier((before[i], gram, got))
            if (step, i) == (1, 1):
                old, image = lax.optimization_barrier((old, image))
            if got is not None:
                gram = gram + got
            got = swap(gram, *hops.pop(0)) if hops else None
            mate = after[0] if i == 1 and step == DEGREE - 2 else ()
            done, parts = apply(meta, now[i], exchange(now[i]), old, mate, count)
            after.append(done)
            if got is not None:
                gram, got, _ = lax.optimization_barrier((gram, got, done))
        before, now = now, after
    if got is not None:
        gram = gram + got
    for hop in hops:
        gram = gram + swap(gram, *hop)
    halos = [exchange(panels) for panels in now]
    halos[0], gram = lax.optimization_barrier((halos[0], gram))
    inverse_first = inverse_factor(gram, nodes)
    (cross_first,) = call(
        cross_kernel, "cross", [square], ids, panel, gram_first, *image, scalars=1, scratch=[held]
    )
    turned, gram_last = call(
        turn_kernel, "turn", [wide, square], ids, inverse_first, *swapped(parts), scalars=1, scratch=[held]
    )
    first, _ = apply(meta, now[0], halos[0])
    gram = gram_last
    hops = hops_of("col", "node")
    for i, hop in enumerate(hops):
        got = swap(gram, *hop)
        if i == TIE_HALO:
            got, halos[1] = lax.optimization_barrier((got, halos[1]))
            _, parts = apply(meta, now[1], halos[1], (), first, count)
            parts = swapped(parts)
        if i == len(hops) - TIE_IMAGE:
            got, parts = lax.optimization_barrier((got, parts))
        gram = gram + got
    (images,) = call(
        turn_cross_kernel, "turn_cross", [(2, vecs, vecs)], ids, inverse_first, turned, gram_last,
        cross_first, *parts, scalars=1, scratch=[held],
    )
    for hop in hops_of("node"):
        images = images + swap(images, *hop)
    inverse_last = inverse_factor(gram, nodes)
    parts = call(
        basis_kernel, "basis", [(quarter, cols_here, block)] * count, ids, inverse_last, turned,
        scalars=1, scratch=[held],
    )
    (basis,) = call(
        functools.partial(join_kernel, half), "join", [(cols_here, width)], ids, *swapped(parts), scalars=1
    )
    parts = call(
        functools.partial(proj_kernel, nodes), "proj", [(2, cols_here, vecs)] * count, ids,
        inverse_first, inverse_last, images, scalars=1, scratch=[pltpu.VMEM(square, F32)],
    )
    projected = sum(swapped(parts))
    return basis, projected[0], projected[1]


def solution(mesh):
    placed = (P("node", None, None), P("node", None), P("node", None), P("col", "node"))
    return jax.shard_map(
        body,
        mesh=mesh,
        in_specs=placed,
        out_specs=(P("col", "node"), P("col", None), P("col", None)),
        check_vma=False,
    )
```

```python
import functools
import math
import jax
import jax.numpy as jnp
from jax import lax
from jax.experimental import pallas as pl
from jax.experimental.pallas import tpu as pltpu
from jax.sharding import PartitionSpec as P

DEGREE = 4
UNROLL = 72
CHUNK = 24
TURNS = 3
APPLY_BYTES = 4 << 20
F32, BF16, I32 = jnp.float32, jnp.bfloat16, jnp.int32
precise = lax.Precision.HIGHEST
center = 1.025
half_width = 0.975
MIB = 1 << 20
IN_VMEM = pl.BlockSpec(memory_space=pltpu.VMEM)
IN_SMEM = pl.BlockSpec(memory_space=pltpu.SMEM)


def nt(a, b):
    return lax.dot_general(
        a, b, (((1,), (1,)), ((), ())), precision=precise, preferred_element_type=F32
    )


def tn(a, b):
    return lax.dot_general(
        a, b, (((0,), (0,)), ((), ())), precision=precise, preferred_element_type=F32
    )


def nn(a, b):
    return jnp.dot(a, b, precision=precise, preferred_element_type=F32)


def call(kernel, name, outs, *args, scalars=0, scratch=(), cost=None):
    return pl.pallas_call(
        kernel,
        in_specs=[IN_SMEM] * scalars + [IN_VMEM] * (len(args) - scalars),
        out_specs=[IN_VMEM] * len(outs),
        out_shape=[jax.ShapeDtypeStruct(o, F32) for o in outs],
        scratch_shapes=list(scratch),
        compiler_params=pltpu.CompilerParams(vmem_limit_bytes=12 * MIB),
        cost_estimate=cost,
        name=name,
    )(*args)


def prep_kernel(rows, ids_ref, own_ref, col_ref, blk_ref, w_ref, inv_ref, table_ref, held_ref, eye_ref, sem_ref):
    count, n, _ = held_ref.shape
    steps = sem_ref.shape[0]
    chunk = count // steps
    half = rows // 2
    me = ids_ref[0]
    odd = me % 2

    def fetch(step):
        span = pl.ds(step * chunk, chunk)
        return pltpu.make_async_copy(blk_ref.at[span], held_ref.at[span], sem_ref.at[step])

    for step in range(steps):
        fetch(step).start()
    table_ref[0] = me
    table_ref[1] = ids_ref[1]
    inv_ref[...] = jnp.zeros(inv_ref.shape, F32)
    lines = lax.broadcasted_iota(I32, eye_ref.shape, 0)
    lanes = lax.broadcasted_iota(I32, eye_ref.shape, 1)
    eye_ref[...] = jnp.where((lines == lanes) | (lines >= n), 1.0, 0.0).astype(BF16)

    def pack(step, carry):
        fetch(step).wait()
        for c in range(chunk):
            b = step * chunk + c
            r = own_ref[0, b]
            k = col_ref[0, b]
            owner = k // rows
            local = k - owner * rows
            upper = (local >= half).astype(I32)
            near = local - half * upper
            swap = odd * upper + (1 - odd) * (1 - upper)
            slot = jnp.where(owner == me, near + half * swap, 2 * half + near + half * (1 - swap))
            top = (r >= half).astype(I32)
            r_at = r + half * (1 - odd) * (1 - 2 * top)
            table_ref[2 + b] = slot
            table_ref[2 + count + b] = r_at
            a = held_ref[b]
            if c % TURNS:
                t = a.T
                high = t.astype(BF16)
                w_ref[b, :, :n] = high
                w_ref[b, :, n:] = (t - high.astype(F32)).astype(BF16)
                inv_ref[r_at] = inv_ref[r_at] + jnp.sum(t, axis=0, keepdims=True)
            else:
                high = a.astype(BF16)
                low = (a - high.astype(F32)).astype(BF16)
                both = jnp.concatenate([high, low], axis=0)
                t = lax.dot_general(
                    eye_ref[...], both, (((1,), (1,)), ((), ())), preferred_element_type=F32
                )
                w_ref[b] = t[:n].astype(BF16)
                inv_ref[r_at] = inv_ref[r_at] + (t[n:n + 1, :n] + t[n:n + 1, n:])
        return carry

    lax.fori_loop(0, steps, pack, 0)
    inv_ref[...] = 1.0 / inv_ref[...]


def prep(ids, own, col, blocks, rows):
    count, n, _ = blocks.shape
    own, col, blocks = (pltpu.with_memory_space_constraint(x, pltpu.HBM) for x in (own, col, blocks))
    return pl.pallas_call(
        functools.partial(prep_kernel, rows),
        in_specs=[IN_SMEM] * 3 + [pl.BlockSpec(memory_space=pl.ANY)],
        out_specs=[IN_VMEM, IN_VMEM, IN_SMEM],
        out_shape=[pltpu.VMEM((count, n, 2 * n), BF16),
                   jax.ShapeDtypeStruct((rows, 1, n), F32),
                   jax.ShapeDtypeStruct((2 + 2 * count,), I32)],
        scratch_shapes=[
            pltpu.VMEM(blocks.shape, F32),
            pltpu.VMEM((n + 16, n), BF16),
            pltpu.SemaphoreType.DMA((count // math.gcd(count, CHUNK),)),
        ],
        compiler_params=pltpu.CompilerParams(vmem_limit_bytes=24 * MIB),
        cost_estimate=pl.CostEstimate(
            flops=2 * count * n * n * n, bytes_accessed=4 * blocks.size, transcendentals=0
        ),
        name="prep",
    )(ids, own, col, blocks)


def apply_kernel(recur, mate, *refs):
    refs = list(refs)
    table_ref, w_ref, inv_ref = refs[:3]
    panels = refs[3:7]
    del refs[:7]
    olds = [refs.pop(0) for _ in range(2 if recur else 0)]
    mates = [refs.pop(0) for _ in range(2 if mate else 0)]
    outs = [refs.pop(0) for _ in range(2)]
    parts = refs[:-2]
    sp_ref, acc_ref = refs[-2:]
    half, kk, n = panels[0].shape
    blocks = w_ref.shape[0]
    for i, ref in enumerate(panels):
        v = ref[...]
        high = v.astype(BF16)
        sp_ref[i * half:(i + 1) * half, :kk] = high
        sp_ref[i * half:(i + 1) * half, kk:] = (v - high.astype(F32)).astype(BF16)
    acc_ref[...] = jnp.zeros(acc_ref.shape, F32)
    unroll = math.gcd(blocks, UNROLL)

    def group(g, c):
        for u in range(unroll):
            b = g * unroll + u
            y = jnp.dot(sp_ref[table_ref[2 + b]], w_ref[b], preferred_element_type=F32)
            r = table_ref[2 + blocks + b]
            acc_ref[r] = acc_ref[r] + ((y[:kk, :n] + y[kk:, :n]) + (y[:kk, n:] + y[kk:, n:]))
        return c

    lax.fori_loop(0, blocks // unroll, group, 0)
    scale = (2.0 if recur else 1.0) / half_width
    for i in range(2):
        span = slice(i * half, (i + 1) * half)
        now = panels[i][...]
        image = (now - acc_ref[span] * inv_ref[span] - center * now) * scale
        if recur:
            image = image - olds[i][...]
        outs[i][...] = image
        if mate:
            acc_ref[span] = image
            parts[-1][span] = mates[i][...]
    if mate:
        count = len(parts) - 1
        me = table_ref[1]
        each = 2 * half // count
        for s in range(count):
            at = pl.ds((me ^ s) * each, each)
            parts[s][:, :kk] = parts[-1][at]
            parts[s][:, kk:] = acc_ref[at]


def apply(meta, pair, halo, old=(), mate=(), count=0):
    half, kk, n = pair[0].shape
    out = [jax.ShapeDtypeStruct((half, kk, n), F32)] * 2
    if mate:
        out += [jax.ShapeDtypeStruct((2 * half // count, 2 * kk, n), F32)] * count
    args = (*pair, *halo, *old, *mate)
    scratch = [pltpu.VMEM((4 * half, 2 * kk, n), BF16), pltpu.VMEM((2 * half, kk, n), F32)]
    if mate:
        scratch = [pltpu.VMEM((2 * half, kk, n), F32)] + scratch
    res = pl.pallas_call(
        functools.partial(apply_kernel, bool(old), bool(mate)),
        in_specs=[IN_SMEM] + [IN_VMEM] * (2 + len(args)),
        out_specs=[IN_VMEM] * len(out),
        out_shape=out,
        scratch_shapes=scratch,
        compiler_params=pltpu.CompilerParams(vmem_limit_bytes=12 * MIB),
        cost_estimate=pl.CostEstimate(
            flops=0, bytes_accessed=APPLY_BYTES, transcendentals=0
        ),
        name="apply" + "_recur" * bool(old) + "_parts" * bool(mate),
    )(*meta, *args)
    return tuple(res[:2]), tuple(res[2:])


def factor_kernel(nodes, g_ref, out_ref):
    n = g_ref.shape[0]
    p = 8
    out_ref[...] = g_ref[...] * (1.0 / nodes)
    sub = lax.broadcasted_iota(I32, (p, n), 0)
    lane = lax.broadcasted_iota(I32, (p, n), 1)
    for j in range(0, n, p):
        rows = out_ref[j:j + p]
        cols = [jnp.broadcast_to(rows[:, j + i:j + i + 1], (p, n)) for i in range(p)]
        rows = jnp.where((lane >= j) & (lane < j + p), jnp.where(lane - j == sub, 1.0, 0.0), rows)
        for i in range(p):
            root = lax.rsqrt(jnp.broadcast_to(cols[i][i:i + 1], (p, n)))
            ratio = jnp.where(sub > i, cols[i] * root, 0.0)
            scale = jnp.where(sub == i, root, 1.0)
            for k in range(i + 1, p):
                cols[k] = cols[k] - ratio * (jnp.broadcast_to(cols[k][i:i + 1], (p, n)) * root)
            rows = rows * scale - ratio * (jnp.broadcast_to(rows[i:i + 1], (p, n)) * root)
        out_ref[j:j + p] = jnp.where(lane < j + p, rows, 0.0)
        if j + p < n:
            change = nn(rows.T[j + p:], rows)
            lanes = lax.broadcasted_iota(I32, change.shape, 1)
            rest = out_ref[j + p:]
            out_ref[j + p:] = jnp.where((lanes >= j) & (lanes < j + p), 0.0, rest) - change


def inverse_factor(gram, nodes):
    n = gram.shape[0]
    return call(
        functools.partial(factor_kernel, nodes), "factor", [(n, n)], gram,
    )[0]


def gathered(ids_ref, parts, b, x_ref):
    each = parts[0].shape[1]
    me = ids_ref[1]
    for s, part in enumerate(parts):
        x_ref[b, pl.ds(pl.multiple_of((me ^ s) * each, each), each)] = part[b]
    return x_ref[b]


def gram_kernel(ids_ref, *refs):
    parts, (f_ref, g_ref) = refs[:-2], refs[-2:]
    total = jnp.zeros(g_ref.shape, F32)
    for b in range(f_ref.shape[0]):
        f = gathered(ids_ref, parts, b, f_ref)
        total = total + nt(f, f)
    g_ref[...] = total


def cross_kernel(ids_ref, f_ref, g_ref, *refs):
    parts, (k_ref, x_ref) = refs[:-2], refs[-2:]
    total = jnp.zeros(k_ref.shape, F32)
    for b in range(f_ref.shape[0]):
        total = total + nt(f_ref[b], gathered(ids_ref, parts, b, x_ref))
    k_ref[...] = half_width * total + center * g_ref[...]


def turn_kernel(ids_ref, inv_ref, *refs):
    parts, (f_ref, g_ref, x_ref) = refs[:-3], refs[-3:]
    total = jnp.zeros(g_ref.shape, F32)
    for b in range(f_ref.shape[0]):
        f = nn(inv_ref[...], gathered(ids_ref, parts, b, x_ref))
        f_ref[b] = f
        total = total + nt(f, f)
    g_ref[...] = total


def turn_cross_kernel(ids_ref, inv_ref, f_ref, g_ref, *refs):
    parts, (k_ref, x_ref) = refs[:-2], refs[-2:]
    total = jnp.zeros(g_ref.shape, F32)
    for b in range(f_ref.shape[0]):
        total = total + nt(f_ref[b], gathered(ids_ref, parts, b, x_ref))
    k_ref[...] = half_width * nt(total, inv_ref[...]) + center * g_ref[...]


def basis_kernel(ids_ref, inv_ref, f_ref, *refs):
    parts, x_ref = refs[:-1], refs[-1]
    each = parts[0].shape[1]
    me = ids_ref[1]
    for b in range(f_ref.shape[0]):
        x_ref[b] = nn(inv_ref[...], f_ref[b])
        for s, part in enumerate(parts):
            part[b] = x_ref[b, pl.ds(pl.multiple_of((me ^ s) * each, each), each)]


def proj_kernel(nodes, ids_ref, *refs):
    pairs, parts, x_ref = (refs[:2], refs[2:4]), refs[4:-1], refs[-1]
    each = parts[0].shape[1]
    me = ids_ref[1]
    for i, (inv_ref, image_ref) in enumerate(pairs):
        x_ref[...] = nt(nn(inv_ref[...], image_ref[...] * (1.0 / nodes)), inv_ref[...])
        for s, part in enumerate(parts):
            part[i] = x_ref[pl.ds(pl.multiple_of((me ^ s) * each, each), each)]


def slot_row(slot, half, odd):
    return slot + half * (1 - odd) * jnp.where(slot >= half, -1, 1)


def split_kernel(ids_ref, start_ref, *outs):
    half, kk, n = outs[0].shape
    odd = ids_ref[0] % 2
    for slot in range(2 * half):
        row = slot_row(slot, half, odd)
        piece = start_ref[:, pl.ds(pl.multiple_of(row * n, n), n)]
        for i in range(2):
            outs[2 * i + slot // half][slot % half] = piece[i * kk:(i + 1) * kk]


def join_kernel(half, ids_ref, *refs):
    parts, out_ref = refs[:-1], refs[-1]
    each, _, n = parts[0].shape
    odd = ids_ref[0] % 2
    me = ids_ref[1]
    for s, part in enumerate(parts):
        for b in range(each):
            row = slot_row((me ^ s) * each + b, half, odd)
            out_ref[:, pl.ds(pl.multiple_of(row * n, n), n)] = part[b]


def exchange(pair):
    count = lax.axis_size("node")
    even = [(i, i ^ 1) for i in range(count)]
    odd = [(i, (i - 1 if i % 2 == 0 else i + 1) % count) for i in range(count)]
    return lax.ppermute(pair[0], "node", even), lax.ppermute(pair[1], "node", odd)


def swap(value, axis, hop):
    return lax.ppermute(value, axis, [(i, i ^ hop) for i in range(lax.axis_size(axis))])


def swapped(parts):
    return [parts[0]] + [swap(parts[s], "col", s) for s in range(1, len(parts))]


def hops_of(*axes):
    return [(axis, 1 << i) for axis in axes for i in range((lax.axis_size(axis) - 1).bit_length())]


def body(blocks, owner_row, block_col, start):
    cols_here, width = start.shape
    block = blocks.shape[1]
    slots = width // block
    half = slots // 2
    count = lax.axis_size("col")
    nodes = width * lax.axis_size("node")
    vecs = cols_here * count
    each = cols_here // 2
    quarter = slots // count
    square = (vecs, vecs)
    wide = (quarter, vecs, block)
    held = pltpu.VMEM(wide, F32)
    ids = jnp.stack([lax.axis_index("node"), lax.axis_index("col")]).astype(I32)

    halves = call(split_kernel, "split", [(half, each, block)] * 4, ids, start, scalars=1)
    before = [tuple(halves[:2]), tuple(halves[2:])]
    w, inv, table = prep(ids, owner_row, block_col, blocks, slots)
    meta = (table, w, inv)

    def advance(now, before=((), ()), parts=False):
        first, _ = apply(meta, now[0], exchange(now[0]), before[0])
        mate = first if parts else ()
        second, out = apply(meta, now[1], exchange(now[1]), before[1], mate, count)
        return [first, second], out

    now, _ = advance(before)
    for step in range(DEGREE - 1):
        after, parts = advance(now, before, step == DEGREE - 2)
        before, now = now, after
    panel, gram_first = call(gram_kernel, "gram", [wide, square], ids, *swapped(parts), scalars=1)
    after, parts = advance(now, parts=True)
    before, now = now, after
    image = swapped(parts)
    got, hops = None, hops_of("col", "node")
    gram = gram_first
    for step in range(DEGREE - 1):
        after = []
        for i in range(2):
            old, gram, got = lax.optimization_barrier((before[i], gram, got))
            if (step, i) == (1, 1):
                old, image = lax.optimization_barrier((old, image))
            if got is not None:
                gram = gram + got
            got = swap(gram, *hops.pop(0)) if hops else None
            mate = after[0] if i == 1 and step == DEGREE - 2 else ()
            done, parts = apply(meta, now[i], exchange(now[i]), old, mate, count)
            after.append(done)
            if got is not None:
                gram, got, _ = lax.optimization_barrier((gram, got, done))
        before, now = now, after
    if got is not None:
        gram = gram + got
    for hop in hops:
        gram = gram + swap(gram, *hop)
    halos = [exchange(panels) for panels in now]
    halos[0], gram = lax.optimization_barrier((halos[0], gram))
    inverse_first = inverse_factor(gram, nodes)
    (image_first,) = call(
        cross_kernel, "cross", [square], ids, panel, gram_first, *image, scalars=1, scratch=[held]
    )
    turned, gram_last = call(
        turn_kernel, "turn", [wide, square], ids, inverse_first, *swapped(parts), scalars=1, scratch=[held]
    )
    first, _ = apply(meta, now[0], halos[0])
    gram = gram_last
    hops = hops_of("col", "node")
    for i, hop in enumerate(hops):
        got = swap(gram, *hop)
        if i == 1:
            got, halos[1] = lax.optimization_barrier((got, halos[1]))
            _, parts = apply(meta, now[1], halos[1], (), first, count)
            (image_last,) = call(
                turn_cross_kernel, "turn_cross", [square], ids, inverse_first, turned, gram_last,
                *swapped(parts), scalars=1, scratch=[held],
            )
        if i == len(hops) - 2:
            got, image_first = lax.optimization_barrier((got, image_first))
        if i == len(hops) - 1:
            got, image_last = lax.optimization_barrier((got, image_last))
        gram = gram + got
    inverse_last = inverse_factor(gram, nodes)
    for i, hop in enumerate(hops_of("node")):
        image_first = image_first + swap(image_first, *hop)
        got = swap(image_last, *hop)
        if i == 0:
            got, image_last, _ = lax.optimization_barrier((got, image_last, inverse_last))
        image_last = image_last + got
    parts = call(
        basis_kernel, "basis", [(quarter, cols_here, block)] * count, ids, inverse_last, turned,
        scalars=1, scratch=[held],
    )
    (basis,) = call(
        functools.partial(join_kernel, half), "join", [(cols_here, width)], ids, *swapped(parts), scalars=1
    )
    parts = call(
        functools.partial(proj_kernel, nodes), "proj", [(2, cols_here, vecs)] * count, ids,
        inverse_first, image_first, inverse_last, image_last, scalars=1, scratch=[pltpu.VMEM(square, F32)],
    )
    projected = sum(swapped(parts))
    return basis, projected[0], projected[1]


def solution(mesh):
    placed = (P("node", None, None), P("node", None), P("node", None), P("col", "node"))
    return jax.shard_map(
        body,
        mesh=mesh,
        in_specs=placed,
        out_specs=(P("col", "node"), P("col", None), P("col", None)),
        check_vma=False,
    )
```

```python
import functools
import math
import jax
import jax.numpy as jnp
from jax import lax
from jax.experimental import pallas as pl
from jax.experimental.pallas import tpu as pltpu
from jax.sharding import PartitionSpec as P

DEGREE = 4
UNROLL = 72
CHUNK = 24
TURNS = 3
TIE_HALO = 0
TIE_FIRST = 1
APPLY_BYTES = 4 << 20
F32, BF16, I32 = jnp.float32, jnp.bfloat16, jnp.int32
precise = lax.Precision.HIGHEST
center = 1.025
half_width = 0.975
MIB = 1 << 20
IN_VMEM = pl.BlockSpec(memory_space=pltpu.VMEM)
IN_SMEM = pl.BlockSpec(memory_space=pltpu.SMEM)


def nt(a, b):
    return lax.dot_general(
        a, b, (((1,), (1,)), ((), ())), precision=precise, preferred_element_type=F32
    )


def tn(a, b):
    return lax.dot_general(
        a, b, (((0,), (0,)), ((), ())), precision=precise, preferred_element_type=F32
    )


def nn(a, b):
    return jnp.dot(a, b, precision=precise, preferred_element_type=F32)


def call(kernel, name, outs, *args, scalars=0, scratch=(), cost=None):
    return pl.pallas_call(
        kernel,
        in_specs=[IN_SMEM] * scalars + [IN_VMEM] * (len(args) - scalars),
        out_specs=[IN_VMEM] * len(outs),
        out_shape=[jax.ShapeDtypeStruct(o, F32) for o in outs],
        scratch_shapes=list(scratch),
        compiler_params=pltpu.CompilerParams(vmem_limit_bytes=12 * MIB),
        cost_estimate=cost,
        name=name,
    )(*args)


def prep_kernel(rows, ids_ref, own_ref, col_ref, blk_ref, w_ref, inv_ref, table_ref, held_ref, eye_ref, sem_ref):
    count, n, _ = held_ref.shape
    steps = sem_ref.shape[0]
    chunk = count // steps
    half = rows // 2
    me = ids_ref[0]
    odd = me % 2

    def fetch(step):
        span = pl.ds(step * chunk, chunk)
        return pltpu.make_async_copy(blk_ref.at[span], held_ref.at[span], sem_ref.at[step])

    for step in range(steps):
        fetch(step).start()
    table_ref[0] = me
    table_ref[1] = ids_ref[1]
    inv_ref[...] = jnp.zeros(inv_ref.shape, F32)
    lines = lax.broadcasted_iota(I32, eye_ref.shape, 0)
    lanes = lax.broadcasted_iota(I32, eye_ref.shape, 1)
    eye_ref[...] = jnp.where((lines == lanes) | (lines >= n), 1.0, 0.0).astype(BF16)

    def pack(step, carry):
        fetch(step).wait()
        for c in range(chunk):
            b = step * chunk + c
            r = own_ref[0, b]
            k = col_ref[0, b]
            owner = k // rows
            local = k - owner * rows
            upper = (local >= half).astype(I32)
            near = local - half * upper
            swap = odd * upper + (1 - odd) * (1 - upper)
            slot = jnp.where(owner == me, near + half * swap, 2 * half + near + half * (1 - swap))
            top = (r >= half).astype(I32)
            r_at = r + half * (1 - odd) * (1 - 2 * top)
            table_ref[2 + b] = slot
            table_ref[2 + count + b] = r_at
            a = held_ref[b]
            if c % TURNS:
                t = a.T
                high = t.astype(BF16)
                w_ref[b, :, :n] = high
                w_ref[b, :, n:] = (t - high.astype(F32)).astype(BF16)
                inv_ref[r_at] = inv_ref[r_at] + jnp.sum(t, axis=0, keepdims=True)
            else:
                high = a.astype(BF16)
                low = (a - high.astype(F32)).astype(BF16)
                both = jnp.concatenate([high, low], axis=0)
                t = lax.dot_general(
                    eye_ref[...], both, (((1,), (1,)), ((), ())), preferred_element_type=F32
                )
                w_ref[b] = t[:n].astype(BF16)
                inv_ref[r_at] = inv_ref[r_at] + (t[n:n + 1, :n] + t[n:n + 1, n:])
        return carry

    lax.fori_loop(0, steps, pack, 0)
    inv_ref[...] = 1.0 / inv_ref[...]


def prep(ids, own, col, blocks, rows):
    count, n, _ = blocks.shape
    own, col, blocks = (pltpu.with_memory_space_constraint(x, pltpu.HBM) for x in (own, col, blocks))
    return pl.pallas_call(
        functools.partial(prep_kernel, rows),
        in_specs=[IN_SMEM] * 3 + [pl.BlockSpec(memory_space=pl.ANY)],
        out_specs=[IN_VMEM, IN_VMEM, IN_SMEM],
        out_shape=[pltpu.VMEM((count, n, 2 * n), BF16),
                   jax.ShapeDtypeStruct((rows, 1, n), F32),
                   jax.ShapeDtypeStruct((2 + 2 * count,), I32)],
        scratch_shapes=[
            pltpu.VMEM(blocks.shape, F32),
            pltpu.VMEM((n + 16, n), BF16),
            pltpu.SemaphoreType.DMA((count // math.gcd(count, CHUNK),)),
        ],
        compiler_params=pltpu.CompilerParams(vmem_limit_bytes=24 * MIB),
        cost_estimate=pl.CostEstimate(
            flops=2 * count * n * n * n, bytes_accessed=4 * blocks.size, transcendentals=0
        ),
        name="prep",
    )(ids, own, col, blocks)


def apply_kernel(recur, mate, *refs):
    refs = list(refs)
    table_ref, w_ref, inv_ref = refs[:3]
    panels = refs[3:7]
    del refs[:7]
    olds = [refs.pop(0) for _ in range(2 if recur else 0)]
    mates = [refs.pop(0) for _ in range(2 if mate else 0)]
    outs = [refs.pop(0) for _ in range(2)]
    parts = refs[:-2]
    sp_ref, acc_ref = refs[-2:]
    half, kk, n = panels[0].shape
    blocks = w_ref.shape[0]
    for i, ref in enumerate(panels):
        v = ref[...]
        high = v.astype(BF16)
        sp_ref[i * half:(i + 1) * half, :kk] = high
        sp_ref[i * half:(i + 1) * half, kk:] = (v - high.astype(F32)).astype(BF16)
    acc_ref[...] = jnp.zeros(acc_ref.shape, F32)
    unroll = math.gcd(blocks, UNROLL)

    def group(g, c):
        for u in range(unroll):
            b = g * unroll + u
            y = jnp.dot(sp_ref[table_ref[2 + b]], w_ref[b], preferred_element_type=F32)
            r = table_ref[2 + blocks + b]
            acc_ref[r] = acc_ref[r] + ((y[:kk, :n] + y[kk:, :n]) + (y[:kk, n:] + y[kk:, n:]))
        return c

    lax.fori_loop(0, blocks // unroll, group, 0)
    scale = (2.0 if recur else 1.0) / half_width
    for i in range(2):
        span = slice(i * half, (i + 1) * half)
        now = panels[i][...]
        image = (now - acc_ref[span] * inv_ref[span] - center * now) * scale
        if recur:
            image = image - olds[i][...]
        outs[i][...] = image
        if mate:
            acc_ref[span] = image
            parts[-1][span] = mates[i][...]
    if mate:
        count = len(parts) - 1
        me = table_ref[1]
        each = 2 * half // count
        for s in range(count):
            at = pl.ds((me ^ s) * each, each)
            parts[s][:, :kk] = parts[-1][at]
            parts[s][:, kk:] = acc_ref[at]


def apply(meta, pair, halo, old=(), mate=(), count=0):
    half, kk, n = pair[0].shape
    out = [jax.ShapeDtypeStruct((half, kk, n), F32)] * 2
    if mate:
        out += [jax.ShapeDtypeStruct((2 * half // count, 2 * kk, n), F32)] * count
    args = (*pair, *halo, *old, *mate)
    scratch = [pltpu.VMEM((4 * half, 2 * kk, n), BF16), pltpu.VMEM((2 * half, kk, n), F32)]
    if mate:
        scratch = [pltpu.VMEM((2 * half, kk, n), F32)] + scratch
    res = pl.pallas_call(
        functools.partial(apply_kernel, bool(old), bool(mate)),
        in_specs=[IN_SMEM] + [IN_VMEM] * (2 + len(args)),
        out_specs=[IN_VMEM] * len(out),
        out_shape=out,
        scratch_shapes=scratch,
        compiler_params=pltpu.CompilerParams(vmem_limit_bytes=12 * MIB),
        cost_estimate=pl.CostEstimate(
            flops=0, bytes_accessed=APPLY_BYTES, transcendentals=0
        ),
        name="apply" + "_recur" * bool(old) + "_parts" * bool(mate),
    )(*meta, *args)
    return tuple(res[:2]), tuple(res[2:])


def factor_kernel(nodes, g_ref, out_ref):
    n = g_ref.shape[0]
    p = 8
    out_ref[...] = g_ref[...] * (1.0 / nodes)
    sub = lax.broadcasted_iota(I32, (p, n), 0)
    lane = lax.broadcasted_iota(I32, (p, n), 1)
    for j in range(0, n, p):
        rows = out_ref[j:j + p]
        cols = [jnp.broadcast_to(rows[:, j + i:j + i + 1], (p, n)) for i in range(p)]
        rows = jnp.where((lane >= j) & (lane < j + p), jnp.where(lane - j == sub, 1.0, 0.0), rows)
        for i in range(p):
            root = lax.rsqrt(jnp.broadcast_to(cols[i][i:i + 1], (p, n)))
            ratio = jnp.where(sub > i, cols[i] * root, 0.0)
            scale = jnp.where(sub == i, root, 1.0)
            for k in range(i + 1, p):
                cols[k] = cols[k] - ratio * (jnp.broadcast_to(cols[k][i:i + 1], (p, n)) * root)
            rows = rows * scale - ratio * (jnp.broadcast_to(rows[i:i + 1], (p, n)) * root)
        out_ref[j:j + p] = jnp.where(lane < j + p, rows, 0.0)
        if j + p < n:
            change = nn(rows.T[j + p:], rows)
            lanes = lax.broadcasted_iota(I32, change.shape, 1)
            rest = out_ref[j + p:]
            out_ref[j + p:] = jnp.where((lanes >= j) & (lanes < j + p), 0.0, rest) - change


def inverse_factor(gram, nodes):
    n = gram.shape[0]
    return call(
        functools.partial(factor_kernel, nodes), "factor", [(n, n)], gram,
    )[0]


def gathered(ids_ref, parts, b, x_ref):
    each = parts[0].shape[1]
    me = ids_ref[1]
    for s, part in enumerate(parts):
        x_ref[b, pl.ds(pl.multiple_of((me ^ s) * each, each), each)] = part[b]
    return x_ref[b]


def gram_kernel(ids_ref, *refs):
    parts, (f_ref, g_ref) = refs[:-2], refs[-2:]
    total = jnp.zeros(g_ref.shape, F32)
    for b in range(f_ref.shape[0]):
        f = gathered(ids_ref, parts, b, f_ref)
        total = total + nt(f, f)
    g_ref[...] = total


def cross_kernel(ids_ref, f_ref, g_ref, *refs):
    parts, (k_ref, x_ref) = refs[:-2], refs[-2:]
    total = jnp.zeros(k_ref.shape, F32)
    for b in range(f_ref.shape[0]):
        total = total + nt(f_ref[b], gathered(ids_ref, parts, b, x_ref))
    k_ref[...] = half_width * total + center * g_ref[...]


def turn_kernel(ids_ref, inv_ref, *refs):
    parts, (f_ref, g_ref, x_ref) = refs[:-3], refs[-3:]
    total = jnp.zeros(g_ref.shape, F32)
    for b in range(f_ref.shape[0]):
        f = nn(inv_ref[...], gathered(ids_ref, parts, b, x_ref))
        f_ref[b] = f
        total = total + nt(f, f)
    g_ref[...] = total


def turn_cross_kernel(ids_ref, inv_ref, f_ref, g_ref, *refs):
    parts, (k_ref, x_ref) = refs[:-2], refs[-2:]
    total = jnp.zeros(g_ref.shape, F32)
    for b in range(f_ref.shape[0]):
        total = total + nt(f_ref[b], gathered(ids_ref, parts, b, x_ref))
    k_ref[...] = half_width * nt(total, inv_ref[...]) + center * g_ref[...]


def basis_kernel(ids_ref, inv_ref, f_ref, *refs):
    parts, x_ref = refs[:-1], refs[-1]
    each = parts[0].shape[1]
    me = ids_ref[1]
    for b in range(f_ref.shape[0]):
        x_ref[b] = nn(inv_ref[...], f_ref[b])
        for s, part in enumerate(parts):
            part[b] = x_ref[b, pl.ds(pl.multiple_of((me ^ s) * each, each), each)]


def proj_kernel(nodes, ids_ref, *refs):
    pairs, parts, x_ref = (refs[:2], refs[2:4]), refs[4:-1], refs[-1]
    each = parts[0].shape[1]
    me = ids_ref[1]
    for i, (inv_ref, image_ref) in enumerate(pairs):
        x_ref[...] = nt(nn(inv_ref[...], image_ref[...] * (1.0 / nodes)), inv_ref[...])
        for s, part in enumerate(parts):
            part[i] = x_ref[pl.ds(pl.multiple_of((me ^ s) * each, each), each)]


def slot_row(slot, half, odd):
    return slot + half * (1 - odd) * jnp.where(slot >= half, -1, 1)


def split_kernel(ids_ref, start_ref, *outs):
    half, kk, n = outs[0].shape
    odd = ids_ref[0] % 2
    for slot in range(2 * half):
        row = slot_row(slot, half, odd)
        piece = start_ref[:, pl.ds(pl.multiple_of(row * n, n), n)]
        for i in range(2):
            outs[2 * i + slot // half][slot % half] = piece[i * kk:(i + 1) * kk]


def join_kernel(half, ids_ref, *refs):
    parts, out_ref = refs[:-1], refs[-1]
    each, _, n = parts[0].shape
    odd = ids_ref[0] % 2
    me = ids_ref[1]
    for s, part in enumerate(parts):
        for b in range(each):
            row = slot_row((me ^ s) * each + b, half, odd)
            out_ref[:, pl.ds(pl.multiple_of(row * n, n), n)] = part[b]


def exchange(pair):
    count = lax.axis_size("node")
    even = [(i, i ^ 1) for i in range(count)]
    odd = [(i, (i - 1 if i % 2 == 0 else i + 1) % count) for i in range(count)]
    return lax.ppermute(pair[0], "node", even), lax.ppermute(pair[1], "node", odd)


def swap(value, axis, hop):
    return lax.ppermute(value, axis, [(i, i ^ hop) for i in range(lax.axis_size(axis))])


def swapped(parts):
    return [parts[0]] + [swap(parts[s], "col", s) for s in range(1, len(parts))]


def hops_of(*axes):
    return [(axis, 1 << i) for axis in axes for i in range((lax.axis_size(axis) - 1).bit_length())]


def rounds_of(*axes):
    rounds = []
    for axis in axes:
        bits = (lax.axis_size(axis) - 1).bit_length()
        while bits > 0:
            low = max(bits - 2, 0)
            rounds.append((axis, [1 << bit for bit in range(low, bits)]))
            bits = low
    return rounds


def round_swaps(value, axis, hops):
    hops = hops if len(hops) == 1 else [hops[0], hops[1], hops[0] ^ hops[1]]
    return [swap(value, axis, hop) for hop in hops]


def round_sum(value, got):
    value = value + got[0]
    return value if len(got) == 1 else value + (got[1] + got[2])


def body(blocks, owner_row, block_col, start):
    cols_here, width = start.shape
    block = blocks.shape[1]
    slots = width // block
    half = slots // 2
    count = lax.axis_size("col")
    nodes = width * lax.axis_size("node")
    vecs = cols_here * count
    each = cols_here // 2
    quarter = slots // count
    square = (vecs, vecs)
    wide = (quarter, vecs, block)
    held = pltpu.VMEM(wide, F32)
    ids = jnp.stack([lax.axis_index("node"), lax.axis_index("col")]).astype(I32)

    halves = call(split_kernel, "split", [(half, each, block)] * 4, ids, start, scalars=1)
    before = [tuple(halves[:2]), tuple(halves[2:])]
    w, inv, table = prep(ids, owner_row, block_col, blocks, slots)
    meta = (table, w, inv)

    def advance(now, before=((), ()), parts=False):
        first, _ = apply(meta, now[0], exchange(now[0]), before[0])
        mate = first if parts else ()
        second, out = apply(meta, now[1], exchange(now[1]), before[1], mate, count)
        return [first, second], out

    now, _ = advance(before)
    for step in range(DEGREE - 1):
        after, parts = advance(now, before, step == DEGREE - 2)
        before, now = now, after
    panel, gram_first = call(gram_kernel, "gram", [wide, square], ids, *swapped(parts), scalars=1)
    after, parts = advance(now, parts=True)
    before, now = now, after
    image = swapped(parts)
    got, hops = None, hops_of("col", "node")
    gram = gram_first
    for step in range(DEGREE - 1):
        after = []
        for i in range(2):
            old, gram, got = lax.optimization_barrier((before[i], gram, got))
            if (step, i) == (1, 1):
                old, image = lax.optimization_barrier((old, image))
            if got is not None:
                gram = gram + got
            got = swap(gram, *hops.pop(0)) if hops else None
            mate = after[0] if i == 1 and step == DEGREE - 2 else ()
            done, parts = apply(meta, now[i], exchange(now[i]), old, mate, count)
            after.append(done)
            if got is not None:
                gram, got, _ = lax.optimization_barrier((gram, got, done))
        before, now = now, after
    if got is not None:
        gram = gram + got
    for hop in hops:
        gram = gram + swap(gram, *hop)
    halos = [exchange(panels) for panels in now]
    halos[0], gram = lax.optimization_barrier((halos[0], gram))
    inverse_first = inverse_factor(gram, nodes)
    (image_first,) = call(
        cross_kernel, "cross", [square], ids, panel, gram_first, *image, scalars=1, scratch=[held]
    )
    first, _ = apply(meta, now[0], halos[0])
    arrived, first = lax.optimization_barrier((swapped(parts), first))
    turned, gram_last = call(
        turn_kernel, "turn", [wide, square], ids, inverse_first, *arrived, scalars=1, scratch=[held]
    )
    gram = gram_last
    rounds = rounds_of("col", "node")
    for i, each_round in enumerate(rounds):
        got = round_swaps(gram, *each_round)
        if i == TIE_HALO:
            got, halos[1] = lax.optimization_barrier((got, halos[1]))
            _, parts = apply(meta, now[1], halos[1], (), first, count)
            (image_last,) = call(
                turn_cross_kernel, "turn_cross", [square], ids, inverse_first, turned, gram_last,
                *swapped(parts), scalars=1, scratch=[held],
            )
        if i == len(rounds) - TIE_FIRST:
            got, image_first = lax.optimization_barrier((got, image_first))
        if i == len(rounds) - 1:
            got, image_last = lax.optimization_barrier((got, image_last))
        gram = round_sum(gram, got)
    inverse_last = inverse_factor(gram, nodes)
    parts = call(
        basis_kernel, "basis", [(quarter, cols_here, block)] * count, ids, inverse_last, turned,
        scalars=1, scratch=[held],
    )
    for i, each_round in enumerate(rounds_of("node")):
        if i == 1:
            parts, image_last = lax.optimization_barrier((parts, image_last))
        got_first = round_swaps(image_first, *each_round)
        got = round_swaps(image_last, *each_round)
        if i == 0:
            got, got_first, image_last, _ = lax.optimization_barrier((got, got_first, image_last, inverse_last))
        image_first = round_sum(image_first, got_first)
        image_last = round_sum(image_last, got)
    arrived = swapped(parts)
    parts = call(
        functools.partial(proj_kernel, nodes), "proj", [(2, cols_here, vecs)] * count, ids,
        inverse_first, image_first, inverse_last, image_last, scalars=1, scratch=[pltpu.VMEM(square, F32)],
    )
    received, arrived = lax.optimization_barrier((swapped(parts), arrived))
    projected = sum(received)
    (basis,) = call(
        functools.partial(join_kernel, half), "join", [(cols_here, width)], ids, *arrived, scalars=1
    )
    return basis, projected[0], projected[1]


def solution(mesh):
    placed = (P("node", None, None), P("node", None), P("node", None), P("col", "node"))
    return jax.shard_map(
        body,
        mesh=mesh,
        in_specs=placed,
        out_specs=(P("col", "node"), P("col", None), P("col", None)),
        check_vma=False,
    )
```

```python
import functools
import math
import jax
import jax.numpy as jnp
from jax import lax
from jax.experimental import pallas as pl
from jax.experimental.pallas import tpu as pltpu
from jax.sharding import PartitionSpec as P

DEGREE = 4
UNROLL = 72
CHUNK = 24
TURNS = 3
APPLY_BYTES = 4 << 20
F32, BF16, I32 = jnp.float32, jnp.bfloat16, jnp.int32
precise = lax.Precision.HIGHEST
center = 1.025
half_width = 0.975
MIB = 1 << 20
IN_VMEM = pl.BlockSpec(memory_space=pltpu.VMEM)
IN_SMEM = pl.BlockSpec(memory_space=pltpu.SMEM)


def nt(a, b):
    return lax.dot_general(
        a, b, (((1,), (1,)), ((), ())), precision=precise, preferred_element_type=F32
    )


def tn(a, b):
    return lax.dot_general(
        a, b, (((0,), (0,)), ((), ())), precision=precise, preferred_element_type=F32
    )


def nn(a, b):
    return jnp.dot(a, b, precision=precise, preferred_element_type=F32)


def call(kernel, name, outs, *args, scalars=0, scratch=(), cost=None):
    return pl.pallas_call(
        kernel,
        in_specs=[IN_SMEM] * scalars + [IN_VMEM] * (len(args) - scalars),
        out_specs=[IN_VMEM] * len(outs),
        out_shape=[jax.ShapeDtypeStruct(o, F32) for o in outs],
        scratch_shapes=list(scratch),
        compiler_params=pltpu.CompilerParams(vmem_limit_bytes=12 * MIB),
        cost_estimate=cost,
        name=name,
    )(*args)


def prep_kernel(rows, ids_ref, own_ref, col_ref, blk_ref, w_ref, inv_ref, table_ref, held_ref, eye_ref, sem_ref):
    count, n, _ = held_ref.shape
    steps = sem_ref.shape[0]
    chunk = count // steps
    half = rows // 2
    me = ids_ref[0]
    odd = me % 2

    def fetch(step):
        span = pl.ds(step * chunk, chunk)
        return pltpu.make_async_copy(blk_ref.at[span], held_ref.at[span], sem_ref.at[step])

    for step in range(steps):
        fetch(step).start()
    table_ref[0] = me
    table_ref[1] = ids_ref[1]
    inv_ref[...] = jnp.zeros(inv_ref.shape, F32)
    lines = lax.broadcasted_iota(I32, eye_ref.shape, 0)
    lanes = lax.broadcasted_iota(I32, eye_ref.shape, 1)
    eye_ref[...] = jnp.where((lines == lanes) | (lines >= n), 1.0, 0.0).astype(BF16)

    def pack(step, carry):
        fetch(step).wait()
        for c in range(chunk):
            b = step * chunk + c
            r = own_ref[0, b]
            k = col_ref[0, b]
            owner = k // rows
            local = k - owner * rows
            upper = (local >= half).astype(I32)
            near = local - half * upper
            swap = odd * upper + (1 - odd) * (1 - upper)
            slot = jnp.where(owner == me, near + half * swap, 2 * half + near + half * (1 - swap))
            top = (r >= half).astype(I32)
            r_at = r + half * (1 - odd) * (1 - 2 * top)
            table_ref[2 + b] = slot
            table_ref[2 + count + b] = r_at
            a = held_ref[b]
            if c % TURNS:
                t = a.T
                high = t.astype(BF16)
                w_ref[b, :, :n] = high
                w_ref[b, :, n:] = (t - high.astype(F32)).astype(BF16)
                inv_ref[r_at] = inv_ref[r_at] + jnp.sum(t, axis=0, keepdims=True)
            else:
                high = a.astype(BF16)
                low = (a - high.astype(F32)).astype(BF16)
                both = jnp.concatenate([high, low], axis=0)
                t = lax.dot_general(
                    eye_ref[...], both, (((1,), (1,)), ((), ())), preferred_element_type=F32
                )
                w_ref[b] = t[:n].astype(BF16)
                inv_ref[r_at] = inv_ref[r_at] + (t[n:n + 1, :n] + t[n:n + 1, n:])
        return carry

    lax.fori_loop(0, steps, pack, 0)
    inv_ref[...] = 1.0 / inv_ref[...]


def prep(ids, own, col, blocks, rows):
    count, n, _ = blocks.shape
    own, col, blocks = (pltpu.with_memory_space_constraint(x, pltpu.HBM) for x in (own, col, blocks))
    return pl.pallas_call(
        functools.partial(prep_kernel, rows),
        in_specs=[IN_SMEM] * 3 + [pl.BlockSpec(memory_space=pl.ANY)],
        out_specs=[IN_VMEM, IN_VMEM, IN_SMEM],
        out_shape=[pltpu.VMEM((count, n, 2 * n), BF16),
                   jax.ShapeDtypeStruct((rows, 1, n), F32),
                   jax.ShapeDtypeStruct((2 + 2 * count,), I32)],
        scratch_shapes=[
            pltpu.VMEM(blocks.shape, F32),
            pltpu.VMEM((n + 16, n), BF16),
            pltpu.SemaphoreType.DMA((count // math.gcd(count, CHUNK),)),
        ],
        compiler_params=pltpu.CompilerParams(vmem_limit_bytes=24 * MIB),
        cost_estimate=pl.CostEstimate(
            flops=2 * count * n * n * n, bytes_accessed=4 * blocks.size, transcendentals=0
        ),
        name="prep",
    )(ids, own, col, blocks)


def apply_kernel(recur, mate, *refs):
    refs = list(refs)
    table_ref, w_ref, inv_ref = refs[:3]
    panels = refs[3:7]
    del refs[:7]
    olds = [refs.pop(0) for _ in range(2 if recur else 0)]
    mates = [refs.pop(0) for _ in range(2 if mate else 0)]
    outs = [refs.pop(0) for _ in range(2)]
    parts = refs[:-2]
    sp_ref, acc_ref = refs[-2:]
    half, kk, n = panels[0].shape
    blocks = w_ref.shape[0]
    for i, ref in enumerate(panels):
        v = ref[...]
        high = v.astype(BF16)
        sp_ref[i * half:(i + 1) * half, :kk] = high
        sp_ref[i * half:(i + 1) * half, kk:] = (v - high.astype(F32)).astype(BF16)
    acc_ref[...] = jnp.zeros(acc_ref.shape, F32)
    unroll = math.gcd(blocks, UNROLL)

    def group(g, c):
        for u in range(unroll):
            b = g * unroll + u
            y = jnp.dot(sp_ref[table_ref[2 + b]], w_ref[b], preferred_element_type=F32)
            r = table_ref[2 + blocks + b]
            acc_ref[r] = acc_ref[r] + ((y[:kk, :n] + y[kk:, :n]) + (y[:kk, n:] + y[kk:, n:]))
        return c

    lax.fori_loop(0, blocks // unroll, group, 0)
    scale = (2.0 if recur else 1.0) / half_width
    for i in range(2):
        span = slice(i * half, (i + 1) * half)
        now = panels[i][...]
        image = (now - acc_ref[span] * inv_ref[span] - center * now) * scale
        if recur:
            image = image - olds[i][...]
        outs[i][...] = image
        if mate:
            acc_ref[span] = image
            parts[-1][span] = mates[i][...]
    if mate:
        count = len(parts) - 1
        me = table_ref[1]
        each = 2 * half // count
        for s in range(count):
            at = pl.ds((me ^ s) * each, each)
            parts[s][:, :kk] = parts[-1][at]
            parts[s][:, kk:] = acc_ref[at]


def apply(meta, pair, halo, old=(), mate=(), count=0):
    half, kk, n = pair[0].shape
    out = [jax.ShapeDtypeStruct((half, kk, n), F32)] * 2
    if mate:
        out += [jax.ShapeDtypeStruct((2 * half // count, 2 * kk, n), F32)] * count
    args = (*pair, *halo, *old, *mate)
    scratch = [pltpu.VMEM((4 * half, 2 * kk, n), BF16), pltpu.VMEM((2 * half, kk, n), F32)]
    if mate:
        scratch = [pltpu.VMEM((2 * half, kk, n), F32)] + scratch
    res = pl.pallas_call(
        functools.partial(apply_kernel, bool(old), bool(mate)),
        in_specs=[IN_SMEM] + [IN_VMEM] * (2 + len(args)),
        out_specs=[IN_VMEM] * len(out),
        out_shape=out,
        scratch_shapes=scratch,
        compiler_params=pltpu.CompilerParams(vmem_limit_bytes=12 * MIB),
        cost_estimate=pl.CostEstimate(
            flops=0, bytes_accessed=APPLY_BYTES, transcendentals=0
        ),
        name="apply" + "_recur" * bool(old) + "_parts" * bool(mate),
    )(*meta, *args)
    return tuple(res[:2]), tuple(res[2:])


def factor_kernel(nodes, g_ref, out_ref):
    n = g_ref.shape[0]
    p = 8
    out_ref[...] = g_ref[...] * (1.0 / nodes)
    sub = lax.broadcasted_iota(I32, (p, n), 0)
    lane = lax.broadcasted_iota(I32, (p, n), 1)
    for j in range(0, n, p):
        rows = out_ref[j:j + p]
        cols = [jnp.broadcast_to(rows[:, j + i:j + i + 1], (p, n)) for i in range(p)]
        rows = jnp.where((lane >= j) & (lane < j + p), jnp.where(lane - j == sub, 1.0, 0.0), rows)
        for i in range(p):
            root = lax.rsqrt(jnp.broadcast_to(cols[i][i:i + 1], (p, n)))
            ratio = jnp.where(sub > i, cols[i] * root, 0.0)
            scale = jnp.where(sub == i, root, 1.0)
            for k in range(i + 1, p):
                cols[k] = cols[k] - ratio * (jnp.broadcast_to(cols[k][i:i + 1], (p, n)) * root)
            rows = rows * scale - ratio * (jnp.broadcast_to(rows[i:i + 1], (p, n)) * root)
        out_ref[j:j + p] = jnp.where(lane < j + p, rows, 0.0)
        if j + p < n:
            change = nn(rows.T[j + p:], rows)
            lanes = lax.broadcasted_iota(I32, change.shape, 1)
            rest = out_ref[j + p:]
            out_ref[j + p:] = jnp.where((lanes >= j) & (lanes < j + p), 0.0, rest) - change


def inverse_factor(gram, nodes):
    n = gram.shape[0]
    return call(
        functools.partial(factor_kernel, nodes), "factor", [(n, n)], gram,
    )[0]


def gathered(ids_ref, parts, b, x_ref):
    each = parts[0].shape[1]
    me = ids_ref[1]
    for s, part in enumerate(parts):
        x_ref[b, pl.ds(pl.multiple_of((me ^ s) * each, each), each)] = part[b]
    return x_ref[b]


def gram_kernel(ids_ref, *refs):
    parts, (f_ref, g_ref) = refs[:-2], refs[-2:]
    total = jnp.zeros(g_ref.shape, F32)
    for b in range(f_ref.shape[0]):
        f = gathered(ids_ref, parts, b, f_ref)
        total = total + nt(f, f)
    g_ref[...] = total


def cross_kernel(ids_ref, f_ref, g_ref, *refs):
    parts, (k_ref, x_ref) = refs[:-2], refs[-2:]
    total = jnp.zeros(k_ref.shape, F32)
    for b in range(f_ref.shape[0]):
        total = total + nt(f_ref[b], gathered(ids_ref, parts, b, x_ref))
    k_ref[...] = half_width * total + center * g_ref[...]


def turn_kernel(ids_ref, inv_ref, *refs):
    parts, (f_ref, g_ref, x_ref) = refs[:-3], refs[-3:]
    total = jnp.zeros(g_ref.shape, F32)
    for b in range(f_ref.shape[0]):
        f = nn(inv_ref[...], gathered(ids_ref, parts, b, x_ref))
        f_ref[b] = f
        total = total + nt(f, f)
    g_ref[...] = total


def turn_cross_kernel(ids_ref, inv_ref, f_ref, g_ref, *refs):
    parts, (k_ref, x_ref) = refs[:-2], refs[-2:]
    total = jnp.zeros(g_ref.shape, F32)
    for b in range(f_ref.shape[0]):
        total = total + nt(f_ref[b], gathered(ids_ref, parts, b, x_ref))
    k_ref[...] = half_width * nt(total, inv_ref[...]) + center * g_ref[...]


def basis_kernel(ids_ref, inv_ref, f_ref, *refs):
    parts, x_ref = refs[:-1], refs[-1]
    each = parts[0].shape[1]
    me = ids_ref[1]
    for b in range(f_ref.shape[0]):
        x_ref[b] = nn(inv_ref[...], f_ref[b])
        for s, part in enumerate(parts):
            part[b] = x_ref[b, pl.ds(pl.multiple_of((me ^ s) * each, each), each)]


def proj_kernel(nodes, ids_ref, *refs):
    pairs, parts, x_ref = (refs[:2], refs[2:4]), refs[4:-1], refs[-1]
    each = parts[0].shape[1]
    me = ids_ref[1]
    for i, (inv_ref, image_ref) in enumerate(pairs):
        x_ref[...] = nt(nn(inv_ref[...], image_ref[...] * (1.0 / nodes)), inv_ref[...])
        for s, part in enumerate(parts):
            part[i] = x_ref[pl.ds(pl.multiple_of((me ^ s) * each, each), each)]


def slot_row(slot, half, odd):
    return slot + half * (1 - odd) * jnp.where(slot >= half, -1, 1)


def split_kernel(ids_ref, start_ref, *outs):
    half, kk, n = outs[0].shape
    odd = ids_ref[0] % 2
    for slot in range(2 * half):
        row = slot_row(slot, half, odd)
        piece = start_ref[:, pl.ds(pl.multiple_of(row * n, n), n)]
        for i in range(2):
            outs[2 * i + slot // half][slot % half] = piece[i * kk:(i + 1) * kk]


def join_kernel(half, ids_ref, *refs):
    parts, out_ref = refs[:-1], refs[-1]
    each, _, n = parts[0].shape
    odd = ids_ref[0] % 2
    me = ids_ref[1]
    for s, part in enumerate(parts):
        for b in range(each):
            row = slot_row((me ^ s) * each + b, half, odd)
            out_ref[:, pl.ds(pl.multiple_of(row * n, n), n)] = part[b]


def exchange(pair):
    count = lax.axis_size("node")
    even = [(i, i ^ 1) for i in range(count)]
    odd = [(i, (i - 1 if i % 2 == 0 else i + 1) % count) for i in range(count)]
    return lax.ppermute(pair[0], "node", even), lax.ppermute(pair[1], "node", odd)


def swap(value, axis, hop):
    return lax.ppermute(value, axis, [(i, i ^ hop) for i in range(lax.axis_size(axis))])


def swapped(parts):
    return [parts[0]] + [swap(parts[s], "col", s) for s in range(1, len(parts))]


def hops_of(*axes):
    return [(axis, 1 << i) for axis in axes for i in range((lax.axis_size(axis) - 1).bit_length())]


def rounds_of(*axes):
    rounds = []
    for axis in axes:
        bits = (lax.axis_size(axis) - 1).bit_length()
        while bits > 0:
            low = max(bits - 2, 0)
            rounds.append((axis, [1 << bit for bit in range(low, bits)]))
            bits = low
    return rounds


def round_swaps(value, axis, hops):
    hops = hops if len(hops) == 1 else [hops[0], hops[1], hops[0] ^ hops[1]]
    return [swap(value, axis, hop) for hop in hops]


def round_sum(value, got):
    value = value + got[0]
    return value if len(got) == 1 else value + (got[1] + got[2])


def body(blocks, owner_row, block_col, start):
    cols_here, width = start.shape
    block = blocks.shape[1]
    slots = width // block
    half = slots // 2
    count = lax.axis_size("col")
    nodes = width * lax.axis_size("node")
    vecs = cols_here * count
    each = cols_here // 2
    quarter = slots // count
    square = (vecs, vecs)
    wide = (quarter, vecs, block)
    held = pltpu.VMEM(wide, F32)
    ids = jnp.stack([lax.axis_index("node"), lax.axis_index("col")]).astype(I32)

    halves = call(split_kernel, "split", [(half, each, block)] * 4, ids, start, scalars=1)
    before = [tuple(halves[:2]), tuple(halves[2:])]
    w, inv, table = prep(ids, owner_row, block_col, blocks, slots)
    meta = (table, w, inv)

    def advance(now, before=((), ()), parts=False):
        first, _ = apply(meta, now[0], exchange(now[0]), before[0])
        mate = first if parts else ()
        second, out = apply(meta, now[1], exchange(now[1]), before[1], mate, count)
        return [first, second], out

    now, _ = advance(before)
    for step in range(DEGREE - 1):
        after, parts = advance(now, before, step == DEGREE - 2)
        before, now = now, after
    panel, gram_first = call(gram_kernel, "gram", [wide, square], ids, *swapped(parts), scalars=1)
    after, parts = advance(now, parts=True)
    before, now = now, after
    image = swapped(parts)
    got, hops = None, hops_of("col", "node")
    gram = gram_first
    for step in range(DEGREE - 1):
        after = []
        for i in range(2):
            old, gram, got = lax.optimization_barrier((before[i], gram, got))
            if (step, i) == (1, 1):
                old, image = lax.optimization_barrier((old, image))
            if got is not None:
                gram = gram + got
            got = swap(gram, *hops.pop(0)) if hops else None
            mate = after[0] if i == 1 and step == DEGREE - 2 else ()
            done, parts = apply(meta, now[i], exchange(now[i]), old, mate, count)
            after.append(done)
            if got is not None:
                gram, got, _ = lax.optimization_barrier((gram, got, done))
        before, now = now, after
    if got is not None:
        gram = gram + got
    for hop in hops:
        gram = gram + swap(gram, *hop)
    halos = [exchange(panels) for panels in now]
    halos[0], gram = lax.optimization_barrier((halos[0], gram))
    inverse_first = inverse_factor(gram, nodes)
    (image_first,) = call(
        cross_kernel, "cross", [square], ids, panel, gram_first, *image, scalars=1, scratch=[held]
    )
    turned, gram_last = call(
        turn_kernel, "turn", [wide, square], ids, inverse_first, *swapped(parts), scalars=1, scratch=[held]
    )
    first, _ = apply(meta, now[0], halos[0])
    gram = gram_last
    hops = hops_of("col", "node")
    for i, hop in enumerate(hops):
        got = swap(gram, *hop)
        if i == 1:
            got, halos[1] = lax.optimization_barrier((got, halos[1]))
            _, parts = apply(meta, now[1], halos[1], (), first, count)
            (image_last,) = call(
                turn_cross_kernel, "turn_cross", [square], ids, inverse_first, turned, gram_last,
                *swapped(parts), scalars=1, scratch=[held],
            )
        if i == len(hops) - 2:
            got, image_first = lax.optimization_barrier((got, image_first))
        if i == len(hops) - 1:
            got, image_last = lax.optimization_barrier((got, image_last))
        gram = gram + got
    inverse_last = inverse_factor(gram, nodes)
    parts = call(
        basis_kernel, "basis", [(quarter, cols_here, block)] * count, ids, inverse_last, turned,
        scalars=1, scratch=[held],
    )
    for i, each_round in enumerate(rounds_of("node")):
        if i == 1:
            parts, image_last = lax.optimization_barrier((parts, image_last))
        got_first = round_swaps(image_first, *each_round)
        got = round_swaps(image_last, *each_round)
        if i == 0:
            got, got_first, image_last, _ = lax.optimization_barrier((got, got_first, image_last, inverse_last))
        image_first = round_sum(image_first, got_first)
        image_last = round_sum(image_last, got)
    arrived = swapped(parts)
    parts = call(
        functools.partial(proj_kernel, nodes), "proj", [(2, cols_here, vecs)] * count, ids,
        inverse_first, image_first, inverse_last, image_last, scalars=1, scratch=[pltpu.VMEM(square, F32)],
    )
    received, arrived = lax.optimization_barrier((swapped(parts), arrived))
    projected = sum(received)
    (basis,) = call(
        functools.partial(join_kernel, half), "join", [(cols_here, width)], ids, *arrived, scalars=1
    )
    return basis, projected[0], projected[1]


def solution(mesh):
    placed = (P("node", None, None), P("node", None), P("node", None), P("col", "node"))
    return jax.shard_map(
        body,
        mesh=mesh,
        in_specs=placed,
        out_specs=(P("col", "node"), P("col", None), P("col", None)),
        check_vma=False,
    )
```

```python
import functools
import math
import jax
import jax.numpy as jnp
from jax import lax
from jax.experimental import pallas as pl
from jax.experimental.pallas import tpu as pltpu
from jax.sharding import PartitionSpec as P

DEGREE = 4
UNROLL = 72
CHUNK = 24
TURNS = 3
PANEL = 16
APPLY_BYTES = 4 << 20
F32, BF16, I32 = jnp.float32, jnp.bfloat16, jnp.int32
precise = lax.Precision.HIGHEST
center = 1.025
half_width = 0.975
MIB = 1 << 20
IN_VMEM = pl.BlockSpec(memory_space=pltpu.VMEM)
IN_SMEM = pl.BlockSpec(memory_space=pltpu.SMEM)


def nt(a, b):
    return lax.dot_general(
        a, b, (((1,), (1,)), ((), ())), precision=precise, preferred_element_type=F32
    )


def tn(a, b):
    return lax.dot_general(
        a, b, (((0,), (0,)), ((), ())), precision=precise, preferred_element_type=F32
    )


def nn(a, b):
    return jnp.dot(a, b, precision=precise, preferred_element_type=F32)


def call(kernel, name, outs, *args, scalars=0, scratch=(), cost=None):
    return pl.pallas_call(
        kernel,
        in_specs=[IN_SMEM] * scalars + [IN_VMEM] * (len(args) - scalars),
        out_specs=[IN_VMEM] * len(outs),
        out_shape=[jax.ShapeDtypeStruct(o, F32) for o in outs],
        scratch_shapes=list(scratch),
        compiler_params=pltpu.CompilerParams(vmem_limit_bytes=12 * MIB),
        cost_estimate=cost,
        name=name,
    )(*args)


def prep_kernel(rows, ids_ref, own_ref, col_ref, blk_ref, w_ref, inv_ref, table_ref, held_ref, eye_ref, sem_ref):
    count, n, _ = held_ref.shape
    steps = sem_ref.shape[0]
    chunk = count // steps
    half = rows // 2
    me = ids_ref[0]
    odd = me % 2

    def fetch(step):
        span = pl.ds(step * chunk, chunk)
        return pltpu.make_async_copy(blk_ref.at[span], held_ref.at[span], sem_ref.at[step])

    for step in range(steps):
        fetch(step).start()
    table_ref[0] = me
    table_ref[1] = ids_ref[1]
    inv_ref[...] = jnp.zeros(inv_ref.shape, F32)
    lines = lax.broadcasted_iota(I32, eye_ref.shape, 0)
    lanes = lax.broadcasted_iota(I32, eye_ref.shape, 1)
    eye_ref[...] = jnp.where((lines == lanes) | (lines >= n), 1.0, 0.0).astype(BF16)

    def pack(step, carry):
        fetch(step).wait()
        for c in range(chunk):
            b = step * chunk + c
            r = own_ref[0, b]
            k = col_ref[0, b]
            owner = k // rows
            local = k - owner * rows
            upper = (local >= half).astype(I32)
            near = local - half * upper
            swap = odd * upper + (1 - odd) * (1 - upper)
            slot = jnp.where(owner == me, near + half * swap, 2 * half + near + half * (1 - swap))
            top = (r >= half).astype(I32)
            r_at = r + half * (1 - odd) * (1 - 2 * top)
            table_ref[2 + b] = slot
            table_ref[2 + count + b] = r_at
            a = held_ref[b]
            if c % TURNS:
                t = a.T
                high = t.astype(BF16)
                w_ref[b, :, :n] = high
                w_ref[b, :, n:] = (t - high.astype(F32)).astype(BF16)
                inv_ref[r_at] = inv_ref[r_at] + jnp.sum(t, axis=0, keepdims=True)
            else:
                high = a.astype(BF16)
                low = (a - high.astype(F32)).astype(BF16)
                both = jnp.concatenate([high, low], axis=0)
                t = lax.dot_general(
                    eye_ref[...], both, (((1,), (1,)), ((), ())), preferred_element_type=F32
                )
                w_ref[b] = t[:n].astype(BF16)
                inv_ref[r_at] = inv_ref[r_at] + (t[n:n + 1, :n] + t[n:n + 1, n:])
        return carry

    lax.fori_loop(0, steps, pack, 0)
    inv_ref[...] = 1.0 / inv_ref[...]


def prep(ids, own, col, blocks, rows):
    count, n, _ = blocks.shape
    own, col, blocks = (pltpu.with_memory_space_constraint(x, pltpu.HBM) for x in (own, col, blocks))
    return pl.pallas_call(
        functools.partial(prep_kernel, rows),
        in_specs=[IN_SMEM] * 3 + [pl.BlockSpec(memory_space=pl.ANY)],
        out_specs=[IN_VMEM, IN_VMEM, IN_SMEM],
        out_shape=[pltpu.VMEM((count, n, 2 * n), BF16),
                   jax.ShapeDtypeStruct((rows, 1, n), F32),
                   jax.ShapeDtypeStruct((2 + 2 * count,), I32)],
        scratch_shapes=[
            pltpu.VMEM(blocks.shape, F32),
            pltpu.VMEM((n + 16, n), BF16),
            pltpu.SemaphoreType.DMA((count // math.gcd(count, CHUNK),)),
        ],
        compiler_params=pltpu.CompilerParams(vmem_limit_bytes=24 * MIB),
        cost_estimate=pl.CostEstimate(
            flops=2 * count * n * n * n, bytes_accessed=4 * blocks.size, transcendentals=0
        ),
        name="prep",
    )(ids, own, col, blocks)


def apply_kernel(recur, mate, *refs):
    refs = list(refs)
    table_ref, w_ref, inv_ref = refs[:3]
    panels = refs[3:7]
    del refs[:7]
    olds = [refs.pop(0) for _ in range(2 if recur else 0)]
    mates = [refs.pop(0) for _ in range(2 if mate else 0)]
    outs = [refs.pop(0) for _ in range(2)]
    parts = refs[:-2]
    sp_ref, acc_ref = refs[-2:]
    half, kk, n = panels[0].shape
    blocks = w_ref.shape[0]
    for i, ref in enumerate(panels):
        v = ref[...]
        high = v.astype(BF16)
        sp_ref[i * half:(i + 1) * half, :kk] = high
        sp_ref[i * half:(i + 1) * half, kk:] = (v - high.astype(F32)).astype(BF16)
    acc_ref[...] = jnp.zeros(acc_ref.shape, F32)
    unroll = math.gcd(blocks, UNROLL)

    def group(g, c):
        for u in range(unroll):
            b = g * unroll + u
            y = jnp.dot(sp_ref[table_ref[2 + b]], w_ref[b], preferred_element_type=F32)
            r = table_ref[2 + blocks + b]
            acc_ref[r] = acc_ref[r] + ((y[:kk, :n] + y[kk:, :n]) + (y[:kk, n:] + y[kk:, n:]))
        return c

    lax.fori_loop(0, blocks // unroll, group, 0)
    scale = (2.0 if recur else 1.0) / half_width
    for i in range(2):
        span = slice(i * half, (i + 1) * half)
        now = panels[i][...]
        image = (now - acc_ref[span] * inv_ref[span] - center * now) * scale
        if recur:
            image = image - olds[i][...]
        outs[i][...] = image
        if mate:
            acc_ref[span] = image
            parts[-1][span] = mates[i][...]
    if mate:
        count = len(parts) - 1
        me = table_ref[1]
        each = 2 * half // count
        for s in range(count):
            at = pl.ds((me ^ s) * each, each)
            parts[s][:, :kk] = parts[-1][at]
            parts[s][:, kk:] = acc_ref[at]


def apply(meta, pair, halo, old=(), mate=(), count=0):
    half, kk, n = pair[0].shape
    out = [jax.ShapeDtypeStruct((half, kk, n), F32)] * 2
    if mate:
        out += [jax.ShapeDtypeStruct((2 * half // count, 2 * kk, n), F32)] * count
    args = (*pair, *halo, *old, *mate)
    scratch = [pltpu.VMEM((4 * half, 2 * kk, n), BF16), pltpu.VMEM((2 * half, kk, n), F32)]
    if mate:
        scratch = [pltpu.VMEM((2 * half, kk, n), F32)] + scratch
    res = pl.pallas_call(
        functools.partial(apply_kernel, bool(old), bool(mate)),
        in_specs=[IN_SMEM] + [IN_VMEM] * (2 + len(args)),
        out_specs=[IN_VMEM] * len(out),
        out_shape=out,
        scratch_shapes=scratch,
        compiler_params=pltpu.CompilerParams(vmem_limit_bytes=12 * MIB),
        cost_estimate=pl.CostEstimate(
            flops=0, bytes_accessed=APPLY_BYTES, transcendentals=0
        ),
        name="apply" + "_recur" * bool(old) + "_parts" * bool(mate),
    )(*meta, *args)
    return tuple(res[:2]), tuple(res[2:])


def factor_kernel(nodes, g_ref, out_ref):
    n = g_ref.shape[0]
    p = PANEL
    out_ref[...] = g_ref[...] * (1.0 / nodes)
    sub = lax.broadcasted_iota(I32, (p, n), 0)
    lane = lax.broadcasted_iota(I32, (p, n), 1)
    for j in range(0, n, p):
        rows = out_ref[j:j + p]
        cols = [jnp.broadcast_to(rows[:, j + i:j + i + 1], (p, n)) for i in range(p)]
        rows = jnp.where((lane >= j) & (lane < j + p), jnp.where(lane - j == sub, 1.0, 0.0), rows)
        for i in range(p):
            root = lax.rsqrt(jnp.broadcast_to(cols[i][i:i + 1], (p, n)))
            ratio = jnp.where(sub > i, cols[i] * root, 0.0)
            scale = jnp.where(sub == i, root, 1.0)
            for k in range(i + 1, p):
                cols[k] = cols[k] - ratio * (jnp.broadcast_to(cols[k][i:i + 1], (p, n)) * root)
            rows = rows * scale - ratio * (jnp.broadcast_to(rows[i:i + 1], (p, n)) * root)
        out_ref[j:j + p] = jnp.where(lane < j + p, rows, 0.0)
        if j + p < n:
            change = nn(rows.T[j + p:], rows)
            lanes = lax.broadcasted_iota(I32, change.shape, 1)
            rest = out_ref[j + p:]
            out_ref[j + p:] = jnp.where((lanes >= j) & (lanes < j + p), 0.0, rest) - change


def inverse_factor(gram, nodes):
    n = gram.shape[0]
    return call(
        functools.partial(factor_kernel, nodes), "factor", [(n, n)], gram,
    )[0]


def gathered(ids_ref, parts, b, x_ref):
    each = parts[0].shape[1]
    me = ids_ref[1]
    for s, part in enumerate(parts):
        x_ref[b, pl.ds(pl.multiple_of((me ^ s) * each, each), each)] = part[b]
    return x_ref[b]


def couples(count):
    return [range(b, min(b + 2, count)) for b in range(0, count, 2)]


def wide(pieces):
    return jnp.concatenate(list(pieces), axis=1)


def gram_kernel(ids_ref, *refs):
    parts, (f_ref, g_ref) = refs[:-2], refs[-2:]
    total = jnp.zeros(g_ref.shape, F32)
    for pair in couples(f_ref.shape[0]):
        f = wide(gathered(ids_ref, parts, b, f_ref) for b in pair)
        total = total + nt(f, f)
    g_ref[...] = total


def cross_kernel(ids_ref, f_ref, g_ref, *refs):
    parts, (k_ref, x_ref) = refs[:-2], refs[-2:]
    total = jnp.zeros(k_ref.shape, F32)
    for pair in couples(f_ref.shape[0]):
        z = wide(gathered(ids_ref, parts, b, x_ref) for b in pair)
        total = total + nt(wide(f_ref[b] for b in pair), z)
    k_ref[...] = half_width * total + center * g_ref[...]


def turn_kernel(ids_ref, inv_ref, *refs):
    parts, (f_ref, g_ref, x_ref) = refs[:-3], refs[-3:]
    n = x_ref.shape[-1]
    total = jnp.zeros(g_ref.shape, F32)
    for pair in couples(f_ref.shape[0]):
        f = nn(inv_ref[...], wide(gathered(ids_ref, parts, b, x_ref) for b in pair))
        for i, b in enumerate(pair):
            f_ref[b] = f[:, i * n:(i + 1) * n]
        total = total + nt(f, f)
    g_ref[...] = total


def turn_cross_kernel(ids_ref, inv_ref, f_ref, g_ref, *refs):
    parts, (k_ref, x_ref) = refs[:-2], refs[-2:]
    total = jnp.zeros(g_ref.shape, F32)
    for pair in couples(f_ref.shape[0]):
        z = wide(gathered(ids_ref, parts, b, x_ref) for b in pair)
        total = total + nt(wide(f_ref[b] for b in pair), z)
    k_ref[...] = half_width * nt(total, inv_ref[...]) + center * g_ref[...]


def basis_kernel(ids_ref, inv_ref, f_ref, *refs):
    parts, x_ref = refs[:-1], refs[-1]
    each = parts[0].shape[1]
    me = ids_ref[1]
    n = x_ref.shape[-1]
    for pair in couples(f_ref.shape[0]):
        q = nn(inv_ref[...], wide(f_ref[b] for b in pair))
        for i, b in enumerate(pair):
            x_ref[b] = q[:, i * n:(i + 1) * n]
            for s, part in enumerate(parts):
                part[b] = x_ref[b, pl.ds(pl.multiple_of((me ^ s) * each, each), each)]


def proj_kernel(nodes, ids_ref, *refs):
    pairs, parts, x_ref = (refs[:2], refs[2:4]), refs[4:-1], refs[-1]
    each = parts[0].shape[1]
    me = ids_ref[1]
    for i, (inv_ref, image_ref) in enumerate(pairs):
        x_ref[...] = nt(nn(inv_ref[...], image_ref[...] * (1.0 / nodes)), inv_ref[...])
        for s, part in enumerate(parts):
            part[i] = x_ref[pl.ds(pl.multiple_of((me ^ s) * each, each), each)]


def slot_row(slot, half, odd):
    return slot + half * (1 - odd) * jnp.where(slot >= half, -1, 1)


def split_kernel(ids_ref, start_ref, *outs):
    half, kk, n = outs[0].shape
    odd = ids_ref[0] % 2
    for slot in range(2 * half):
        row = slot_row(slot, half, odd)
        piece = start_ref[:, pl.ds(pl.multiple_of(row * n, n), n)]
        for i in range(2):
            outs[2 * i + slot // half][slot % half] = piece[i * kk:(i + 1) * kk]


def join_kernel(half, ids_ref, *refs):
    parts, out_ref = refs[:-1], refs[-1]
    each, _, n = parts[0].shape
    odd = ids_ref[0] % 2
    me = ids_ref[1]
    for s, part in enumerate(parts):
        for b in range(each):
            row = slot_row((me ^ s) * each + b, half, odd)
            out_ref[:, pl.ds(pl.multiple_of(row * n, n), n)] = part[b]


def exchange(pair):
    count = lax.axis_size("node")
    even = [(i, i ^ 1) for i in range(count)]
    odd = [(i, (i - 1 if i % 2 == 0 else i + 1) % count) for i in range(count)]
    return lax.ppermute(pair[0], "node", even), lax.ppermute(pair[1], "node", odd)


def swap(value, axis, hop):
    return lax.ppermute(value, axis, [(i, i ^ hop) for i in range(lax.axis_size(axis))])


def swapped(parts):
    return [parts[0]] + [swap(parts[s], "col", s) for s in range(1, len(parts))]


def hops_of(*axes):
    return [(axis, 1 << i) for axis in axes for i in range((lax.axis_size(axis) - 1).bit_length())]


def rounds_of(*axes):
    rounds = []
    for axis in axes:
        bits = (lax.axis_size(axis) - 1).bit_length()
        while bits > 0:
            low = max(bits - 2, 0)
            rounds.append((axis, [1 << bit for bit in range(low, bits)]))
            bits = low
    return rounds


def round_swaps(value, axis, hops):
    hops = hops if len(hops) == 1 else [hops[0], hops[1], hops[0] ^ hops[1]]
    return [swap(value, axis, hop) for hop in hops]


def round_sum(value, got):
    value = value + got[0]
    return value if len(got) == 1 else value + (got[1] + got[2])


def body(blocks, owner_row, block_col, start):
    cols_here, width = start.shape
    block = blocks.shape[1]
    slots = width // block
    half = slots // 2
    count = lax.axis_size("col")
    nodes = width * lax.axis_size("node")
    vecs = cols_here * count
    each = cols_here // 2
    quarter = slots // count
    square = (vecs, vecs)
    held_shape = (quarter, vecs, block)
    held = pltpu.VMEM(held_shape, F32)
    ids = jnp.stack([lax.axis_index("node"), lax.axis_index("col")]).astype(I32)

    halves = call(split_kernel, "split", [(half, each, block)] * 4, ids, start, scalars=1)
    before = [tuple(halves[:2]), tuple(halves[2:])]
    w, inv, table = prep(ids, owner_row, block_col, blocks, slots)
    meta = (table, w, inv)

    def advance(now, before=((), ()), parts=False):
        first, _ = apply(meta, now[0], exchange(now[0]), before[0])
        mate = first if parts else ()
        second, out = apply(meta, now[1], exchange(now[1]), before[1], mate, count)
        return [first, second], out

    now, _ = advance(before)
    for step in range(DEGREE - 1):
        after, parts = advance(now, before, step == DEGREE - 2)
        before, now = now, after
    panel, gram_first = call(gram_kernel, "gram", [held_shape, square], ids, *swapped(parts), scalars=1)
    after, parts = advance(now, parts=True)
    before, now = now, after
    image = swapped(parts)
    got, hops = None, hops_of("col", "node")
    gram = gram_first
    for step in range(DEGREE - 1):
        after = []
        for i in range(2):
            old, gram, got = lax.optimization_barrier((before[i], gram, got))
            if (step, i) == (1, 1):
                old, image = lax.optimization_barrier((old, image))
            if got is not None:
                gram = gram + got
            got = swap(gram, *hops.pop(0)) if hops else None
            mate = after[0] if i == 1 and step == DEGREE - 2 else ()
            done, parts = apply(meta, now[i], exchange(now[i]), old, mate, count)
            after.append(done)
            if got is not None:
                gram, got, _ = lax.optimization_barrier((gram, got, done))
        before, now = now, after
    if got is not None:
        gram = gram + got
    for hop in hops:
        gram = gram + swap(gram, *hop)
    halos = [exchange(panels) for panels in now]
    halos[0], gram = lax.optimization_barrier((halos[0], gram))
    inverse_first = inverse_factor(gram, nodes)
    (image_first,) = call(
        cross_kernel, "cross", [square], ids, panel, gram_first, *image, scalars=1, scratch=[held]
    )
    turned, gram_last = call(
        turn_kernel, "turn", [held_shape, square], ids, inverse_first, *swapped(parts), scalars=1, scratch=[held]
    )
    first, _ = apply(meta, now[0], halos[0])
    gram = gram_last
    hops = hops_of("col", "node")
    for i, hop in enumerate(hops):
        got = swap(gram, *hop)
        if i == 1:
            got, halos[1] = lax.optimization_barrier((got, halos[1]))
            _, parts = apply(meta, now[1], halos[1], (), first, count)
            (image_last,) = call(
                turn_cross_kernel, "turn_cross", [square], ids, inverse_first, turned, gram_last,
                *swapped(parts), scalars=1, scratch=[held],
            )
        if i == len(hops) - 2:
            got, image_first = lax.optimization_barrier((got, image_first))
        if i == len(hops) - 1:
            got, image_last = lax.optimization_barrier((got, image_last))
        gram = gram + got
    inverse_last = inverse_factor(gram, nodes)
    parts = call(
        basis_kernel, "basis", [(quarter, cols_here, block)] * count, ids, inverse_last, turned,
        scalars=1, scratch=[held],
    )
    for i, each_round in enumerate(rounds_of("node")):
        if i == 1:
            parts, image_last = lax.optimization_barrier((parts, image_last))
        got_first = round_swaps(image_first, *each_round)
        got = round_swaps(image_last, *each_round)
        if i == 0:
            got, got_first, image_last, _ = lax.optimization_barrier((got, got_first, image_last, inverse_last))
        image_first = round_sum(image_first, got_first)
        image_last = round_sum(image_last, got)
    arrived = swapped(parts)
    parts = call(
        functools.partial(proj_kernel, nodes), "proj", [(2, cols_here, vecs)] * count, ids,
        inverse_first, image_first, inverse_last, image_last, scalars=1, scratch=[pltpu.VMEM(square, F32)],
    )
    received, arrived = lax.optimization_barrier((swapped(parts), arrived))
    projected = sum(received)
    (basis,) = call(
        functools.partial(join_kernel, half), "join", [(cols_here, width)], ids, *arrived, scalars=1
    )
    return basis, projected[0], projected[1]


def solution(mesh):
    placed = (P("node", None, None), P("node", None), P("node", None), P("col", "node"))
    return jax.shard_map(
        body,
        mesh=mesh,
        in_specs=placed,
        out_specs=(P("col", "node"), P("col", None), P("col", None)),
        check_vma=False,
    )
```

```python
import functools
import math
import jax
import jax.numpy as jnp
from jax import lax
from jax.experimental import pallas as pl
from jax.experimental.pallas import tpu as pltpu
from jax.sharding import PartitionSpec as P

DEGREE = 4
UNROLL = 72
CHUNK = 24
TURNS = 3
PANEL = 16
APPLY_BYTES = 4 << 20
F32, BF16, I32 = jnp.float32, jnp.bfloat16, jnp.int32
precise = lax.Precision.HIGHEST
center = 1.025
half_width = 0.975
MIB = 1 << 20
IN_VMEM = pl.BlockSpec(memory_space=pltpu.VMEM)
IN_SMEM = pl.BlockSpec(memory_space=pltpu.SMEM)


def nt(a, b):
    return lax.dot_general(
        a, b, (((1,), (1,)), ((), ())), precision=precise, preferred_element_type=F32
    )


def tn(a, b):
    return lax.dot_general(
        a, b, (((0,), (0,)), ((), ())), precision=precise, preferred_element_type=F32
    )


def nn(a, b):
    return jnp.dot(a, b, precision=precise, preferred_element_type=F32)


def call(kernel, name, outs, *args, scalars=0, scratch=(), cost=None):
    return pl.pallas_call(
        kernel,
        in_specs=[IN_SMEM] * scalars + [IN_VMEM] * (len(args) - scalars),
        out_specs=[IN_VMEM] * len(outs),
        out_shape=[jax.ShapeDtypeStruct(o, F32) for o in outs],
        scratch_shapes=list(scratch),
        compiler_params=pltpu.CompilerParams(vmem_limit_bytes=12 * MIB),
        cost_estimate=cost,
        name=name,
    )(*args)


def prep_kernel(rows, groups, ids_ref, own_ref, col_ref, blk_ref, w_ref, inv_ref, table_ref, held_ref, eye_ref, sem_ref):
    count, n, _ = held_ref.shape
    steps = sem_ref.shape[0]
    chunk = count // steps
    half = rows // 2
    me = ids_ref[0]
    odd = me % 2
    base = me * rows
    base_next = jnp.where(me == groups - 1, 0, me + 1) * rows
    base_last = jnp.where(me == 0, groups - 1, me - 1) * rows

    def fetch(step):
        span = pl.ds(step * chunk, chunk)
        return pltpu.make_async_copy(blk_ref.at[span], held_ref.at[span], sem_ref.at[step])

    for step in range(steps):
        fetch(step).start()
    table_ref[0] = me
    table_ref[1] = ids_ref[1]
    inv_ref[...] = jnp.zeros(inv_ref.shape, F32)
    lines = lax.broadcasted_iota(I32, eye_ref.shape, 0)
    lanes = lax.broadcasted_iota(I32, eye_ref.shape, 1)
    eye_ref[...] = jnp.where((lines == lanes) | (lines >= n), 1.0, 0.0).astype(BF16)

    def pack(step, carry):
        fetch(step).wait()
        for c in range(chunk):
            b = step * chunk + c
            r = own_ref[0, b]
            k = col_ref[0, b]
            mine = (k >= base) & (k < base + rows)
            ahead = (k >= base_next) & (k < base_next + half)
            local = k - jnp.where(mine, base, jnp.where(ahead, base_next, base_last))
            upper = (local >= half).astype(I32)
            near = local - half * upper
            swap = odd * upper + (1 - odd) * (1 - upper)
            slot = jnp.where(mine, near + half * swap, 2 * half + near + half * (1 - swap))
            top = (r >= half).astype(I32)
            r_at = r + half * (1 - odd) * (1 - 2 * top)
            table_ref[2 + b] = slot
            table_ref[2 + count + b] = r_at
            a = held_ref[b]
            if c % TURNS:
                t = a.T
                high = t.astype(BF16)
                w_ref[b, :, :n] = high
                w_ref[b, :, n:] = (t - high.astype(F32)).astype(BF16)
                inv_ref[r_at] = inv_ref[r_at] + jnp.sum(t, axis=0, keepdims=True)
            else:
                high = a.astype(BF16)
                low = (a - high.astype(F32)).astype(BF16)
                both = jnp.concatenate([high, low], axis=0)
                t = lax.dot_general(
                    eye_ref[...], both, (((1,), (1,)), ((), ())), preferred_element_type=F32
                )
                w_ref[b] = t[:n].astype(BF16)
                inv_ref[r_at] = inv_ref[r_at] + (t[n:n + 1, :n] + t[n:n + 1, n:])
        return carry

    lax.fori_loop(0, steps, pack, 0)
    inv_ref[...] = 1.0 / inv_ref[...]


def prep(ids, own, col, blocks, rows, groups):
    count, n, _ = blocks.shape
    own, col, blocks = (pltpu.with_memory_space_constraint(x, pltpu.HBM) for x in (own, col, blocks))
    return pl.pallas_call(
        functools.partial(prep_kernel, rows, groups),
        in_specs=[IN_SMEM] * 3 + [pl.BlockSpec(memory_space=pl.ANY)],
        out_specs=[IN_VMEM, IN_VMEM, IN_SMEM],
        out_shape=[pltpu.VMEM((count, n, 2 * n), BF16),
                   jax.ShapeDtypeStruct((rows, 1, n), F32),
                   jax.ShapeDtypeStruct((2 + 2 * count,), I32)],
        scratch_shapes=[
            pltpu.VMEM(blocks.shape, F32),
            pltpu.VMEM((n + 16, n), BF16),
            pltpu.SemaphoreType.DMA((count // math.gcd(count, CHUNK),)),
        ],
        compiler_params=pltpu.CompilerParams(vmem_limit_bytes=24 * MIB),
        cost_estimate=pl.CostEstimate(
            flops=2 * count * n * n * n, bytes_accessed=4 * blocks.size, transcendentals=0
        ),
        name="prep",
    )(ids, own, col, blocks)


def apply_kernel(recur, mate, *refs):
    refs = list(refs)
    table_ref, w_ref, inv_ref = refs[:3]
    panels = refs[3:7]
    del refs[:7]
    olds = [refs.pop(0) for _ in range(2 if recur else 0)]
    mates = [refs.pop(0) for _ in range(2 if mate else 0)]
    outs = [refs.pop(0) for _ in range(2)]
    parts = refs[:-2]
    sp_ref, acc_ref = refs[-2:]
    half, kk, n = panels[0].shape
    blocks = w_ref.shape[0]
    for i, ref in enumerate(panels):
        v = ref[...]
        high = v.astype(BF16)
        sp_ref[i * half:(i + 1) * half, :kk] = high
        sp_ref[i * half:(i + 1) * half, kk:] = (v - high.astype(F32)).astype(BF16)
    acc_ref[...] = jnp.zeros(acc_ref.shape, F32)
    unroll = math.gcd(blocks, UNROLL)

    def group(g, c):
        for u in range(unroll):
            b = g * unroll + u
            y = jnp.dot(sp_ref[table_ref[2 + b]], w_ref[b], preferred_element_type=F32)
            r = table_ref[2 + blocks + b]
            acc_ref[r] = acc_ref[r] + ((y[:kk, :n] + y[kk:, :n]) + (y[:kk, n:] + y[kk:, n:]))
        return c

    lax.fori_loop(0, blocks // unroll, group, 0)
    scale = (2.0 if recur else 1.0) / half_width
    for i in range(2):
        span = slice(i * half, (i + 1) * half)
        now = panels[i][...]
        image = (now - acc_ref[span] * inv_ref[span] - center * now) * scale
        if recur:
            image = image - olds[i][...]
        outs[i][...] = image
        if mate:
            acc_ref[span] = image
            parts[-1][span] = mates[i][...]
    if mate:
        count = len(parts) - 1
        me = table_ref[1]
        each = 2 * half // count
        for s in range(count):
            at = pl.ds((me ^ s) * each, each)
            parts[s][:, :kk] = parts[-1][at]
            parts[s][:, kk:] = acc_ref[at]


def apply(meta, pair, halo, old=(), mate=(), count=0):
    half, kk, n = pair[0].shape
    out = [jax.ShapeDtypeStruct((half, kk, n), F32)] * 2
    if mate:
        out += [jax.ShapeDtypeStruct((2 * half // count, 2 * kk, n), F32)] * count
    args = (*pair, *halo, *old, *mate)
    scratch = [pltpu.VMEM((4 * half, 2 * kk, n), BF16), pltpu.VMEM((2 * half, kk, n), F32)]
    if mate:
        scratch = [pltpu.VMEM((2 * half, kk, n), F32)] + scratch
    res = pl.pallas_call(
        functools.partial(apply_kernel, bool(old), bool(mate)),
        in_specs=[IN_SMEM] + [IN_VMEM] * (2 + len(args)),
        out_specs=[IN_VMEM] * len(out),
        out_shape=out,
        scratch_shapes=scratch,
        compiler_params=pltpu.CompilerParams(vmem_limit_bytes=12 * MIB),
        cost_estimate=pl.CostEstimate(
            flops=0, bytes_accessed=APPLY_BYTES, transcendentals=0
        ),
        name="apply" + "_recur" * bool(old) + "_parts" * bool(mate),
    )(*meta, *args)
    return tuple(res[:2]), tuple(res[2:])


def factor_kernel(nodes, g_ref, out_ref):
    n = g_ref.shape[0]
    p = PANEL
    out_ref[...] = g_ref[...] * (1.0 / nodes)
    sub = lax.broadcasted_iota(I32, (p, n), 0)
    lane = lax.broadcasted_iota(I32, (p, n), 1)
    for j in range(0, n, p):
        rows = out_ref[j:j + p]
        cols = [jnp.broadcast_to(rows[:, j + i:j + i + 1], (p, n)) for i in range(p)]
        rows = jnp.where((lane >= j) & (lane < j + p), jnp.where(lane - j == sub, 1.0, 0.0), rows)
        for i in range(p):
            root = lax.rsqrt(jnp.broadcast_to(cols[i][i:i + 1], (p, n)))
            ratio = jnp.where(sub > i, cols[i] * root, 0.0)
            scale = jnp.where(sub == i, root, 1.0)
            for k in range(i + 1, p):
                cols[k] = cols[k] - ratio * (jnp.broadcast_to(cols[k][i:i + 1], (p, n)) * root)
            rows = rows * scale - ratio * (jnp.broadcast_to(rows[i:i + 1], (p, n)) * root)
        out_ref[j:j + p] = jnp.where(lane < j + p, rows, 0.0)
        if j + p < n:
            change = nn(rows.T[j + p:], rows)
            lanes = lax.broadcasted_iota(I32, change.shape, 1)
            rest = out_ref[j + p:]
            out_ref[j + p:] = jnp.where((lanes >= j) & (lanes < j + p), 0.0, rest) - change


def inverse_factor(gram, nodes):
    n = gram.shape[0]
    return call(
        functools.partial(factor_kernel, nodes), "factor", [(n, n)], gram,
    )[0]


def gathered(ids_ref, parts, b, x_ref):
    each = parts[0].shape[1]
    me = ids_ref[1]
    for s, part in enumerate(parts):
        x_ref[b, pl.ds(pl.multiple_of((me ^ s) * each, each), each)] = part[b]
    return x_ref[b]


def couples(count):
    return [range(b, min(b + 2, count)) for b in range(0, count, 2)]


def wide(pieces):
    return jnp.concatenate(list(pieces), axis=1)


def gram_kernel(ids_ref, *refs):
    parts, (f_ref, g_ref) = refs[:-2], refs[-2:]
    total = jnp.zeros(g_ref.shape, F32)
    for pair in couples(f_ref.shape[0]):
        f = wide(gathered(ids_ref, parts, b, f_ref) for b in pair)
        total = total + nt(f, f)
    g_ref[...] = total


def cross_kernel(ids_ref, f_ref, g_ref, *refs):
    parts, (k_ref, x_ref) = refs[:-2], refs[-2:]
    total = jnp.zeros(k_ref.shape, F32)
    for pair in couples(f_ref.shape[0]):
        z = wide(gathered(ids_ref, parts, b, x_ref) for b in pair)
        total = total + nt(wide(f_ref[b] for b in pair), z)
    k_ref[...] = half_width * total + center * g_ref[...]


def turn_kernel(ids_ref, inv_ref, *refs):
    parts, (f_ref, g_ref, x_ref) = refs[:-3], refs[-3:]
    n = x_ref.shape[-1]
    total = jnp.zeros(g_ref.shape, F32)
    for pair in couples(f_ref.shape[0]):
        f = nn(inv_ref[...], wide(gathered(ids_ref, parts, b, x_ref) for b in pair))
        for i, b in enumerate(pair):
            f_ref[b] = f[:, i * n:(i + 1) * n]
        total = total + nt(f, f)
    g_ref[...] = total


def turn_cross_kernel(ids_ref, inv_ref, f_ref, g_ref, *refs):
    parts, (k_ref, x_ref) = refs[:-2], refs[-2:]
    total = jnp.zeros(g_ref.shape, F32)
    for pair in couples(f_ref.shape[0]):
        z = wide(gathered(ids_ref, parts, b, x_ref) for b in pair)
        total = total + nt(wide(f_ref[b] for b in pair), z)
    k_ref[...] = half_width * nt(total, inv_ref[...]) + center * g_ref[...]


def basis_kernel(ids_ref, inv_ref, f_ref, *refs):
    parts, x_ref = refs[:-1], refs[-1]
    each = parts[0].shape[1]
    me = ids_ref[1]
    n = x_ref.shape[-1]
    for pair in couples(f_ref.shape[0]):
        q = nn(inv_ref[...], wide(f_ref[b] for b in pair))
        for i, b in enumerate(pair):
            x_ref[b] = q[:, i * n:(i + 1) * n]
            for s, part in enumerate(parts):
                part[b] = x_ref[b, pl.ds(pl.multiple_of((me ^ s) * each, each), each)]


def proj_kernel(nodes, ids_ref, *refs):
    pairs, parts, x_ref = (refs[:2], refs[2:4]), refs[4:-1], refs[-1]
    each = parts[0].shape[1]
    me = ids_ref[1]
    for i, (inv_ref, image_ref) in enumerate(pairs):
        x_ref[...] = nt(nn(inv_ref[...], image_ref[...] * (1.0 / nodes)), inv_ref[...])
        for s, part in enumerate(parts):
            part[i] = x_ref[pl.ds(pl.multiple_of((me ^ s) * each, each), each)]


def slot_row(slot, half, odd):
    return slot + half * (1 - odd) * jnp.where(slot >= half, -1, 1)


def split_kernel(ids_ref, start_ref, *outs):
    half, kk, n = outs[0].shape
    odd = ids_ref[0] % 2
    for slot in range(2 * half):
        row = slot_row(slot, half, odd)
        piece = start_ref[:, pl.ds(pl.multiple_of(row * n, n), n)]
        for i in range(2):
            outs[2 * i + slot // half][slot % half] = piece[i * kk:(i + 1) * kk]


def join_kernel(half, ids_ref, *refs):
    parts, out_ref = refs[:-1], refs[-1]
    each, _, n = parts[0].shape
    odd = ids_ref[0] % 2
    me = ids_ref[1]
    for s, part in enumerate(parts):
        for b in range(each):
            row = slot_row((me ^ s) * each + b, half, odd)
            out_ref[:, pl.ds(pl.multiple_of(row * n, n), n)] = part[b]


def exchange(pair):
    count = lax.axis_size("node")
    even = [(i, i ^ 1) for i in range(count)]
    odd = [(i, (i - 1 if i % 2 == 0 else i + 1) % count) for i in range(count)]
    return lax.ppermute(pair[0], "node", even), lax.ppermute(pair[1], "node", odd)


def swap(value, axis, hop):
    return lax.ppermute(value, axis, [(i, i ^ hop) for i in range(lax.axis_size(axis))])


def swapped(parts):
    return [parts[0]] + [swap(parts[s], "col", s) for s in range(1, len(parts))]


def hops_of(*axes):
    return [(axis, 1 << i) for axis in axes for i in range((lax.axis_size(axis) - 1).bit_length())]


def rounds_of(*axes):
    rounds = []
    for axis in axes:
        bits = (lax.axis_size(axis) - 1).bit_length()
        while bits > 0:
            low = max(bits - 2, 0)
            rounds.append((axis, [1 << bit for bit in range(low, bits)]))
            bits = low
    return rounds


def round_swaps(value, axis, hops):
    hops = hops if len(hops) == 1 else [hops[0], hops[1], hops[0] ^ hops[1]]
    return [swap(value, axis, hop) for hop in hops]


def round_sum(value, got):
    value = value + got[0]
    return value if len(got) == 1 else value + (got[1] + got[2])


def body(blocks, owner_row, block_col, start):
    cols_here, width = start.shape
    block = blocks.shape[1]
    slots = width // block
    half = slots // 2
    count = lax.axis_size("col")
    nodes = width * lax.axis_size("node")
    vecs = cols_here * count
    each = cols_here // 2
    quarter = slots // count
    square = (vecs, vecs)
    held_shape = (quarter, vecs, block)
    held = pltpu.VMEM(held_shape, F32)
    ids = jnp.stack([lax.axis_index("node"), lax.axis_index("col")]).astype(I32)

    halves = call(split_kernel, "split", [(half, each, block)] * 4, ids, start, scalars=1)
    before = [tuple(halves[:2]), tuple(halves[2:])]
    w, inv, table = prep(ids, owner_row, block_col, blocks, slots, lax.axis_size("node"))
    meta = (table, w, inv)

    def advance(now, before=((), ()), parts=False):
        first, _ = apply(meta, now[0], exchange(now[0]), before[0])
        mate = first if parts else ()
        second, out = apply(meta, now[1], exchange(now[1]), before[1], mate, count)
        return [first, second], out

    now, _ = advance(before)
    for step in range(DEGREE - 1):
        after, parts = advance(now, before, step == DEGREE - 2)
        before, now = now, after
    panel, gram_first = call(gram_kernel, "gram", [held_shape, square], ids, *swapped(parts), scalars=1)
    after, parts = advance(now, parts=True)
    before, now = now, after
    image = swapped(parts)
    got, hops = None, hops_of("col", "node")
    hops = hops[:1] + hops[2:4] + hops[1:2] + hops[4:]
    gram = gram_first
    for step in range(DEGREE - 1):
        after = []
        for i in range(2):
            old, gram, got = lax.optimization_barrier((before[i], gram, got))
            if (step, i) == (1, 1):
                old, image = lax.optimization_barrier((old, image))
                (image_first,) = call(
                    cross_kernel, "cross", [square], ids, panel, gram_first, *image, scalars=1, scratch=[held]
                )
            if (step, i) == (2, 1):
                old, image_first = lax.optimization_barrier((old, image_first))
            if got is not None:
                gram = gram + got
            got = swap(gram, *hops.pop(0)) if hops else None
            mate = after[0] if i == 1 and step == DEGREE - 2 else ()
            done, parts = apply(meta, now[i], exchange(now[i]), old, mate, count)
            after.append(done)
            if got is not None:
                gram, got, _ = lax.optimization_barrier((gram, got, done))
        before, now = now, after
    if got is not None:
        gram = gram + got
    for hop in hops:
        gram = gram + swap(gram, *hop)
    halos = [exchange(panels) for panels in now]
    halos[0], gram = lax.optimization_barrier((halos[0], gram))
    inverse_first = inverse_factor(gram, nodes)
    turned, gram_last = call(
        turn_kernel, "turn", [held_shape, square], ids, inverse_first, *swapped(parts), scalars=1, scratch=[held]
    )
    first, _ = apply(meta, now[0], halos[0])
    gram = gram_last
    hops = hops_of("col", "node")
    first_hops = hops_of("node")
    for i, hop in enumerate(hops):
        got = swap(gram, *hop)
        if i == 1:
            got, halos[1], first = lax.optimization_barrier((got, halos[1], first))
            _, parts = apply(meta, now[1], halos[1], (), first, count)
            (image_last,) = call(
                turn_cross_kernel, "turn_cross", [square], ids, inverse_first, turned, gram_last,
                *swapped(parts), scalars=1, scratch=[held],
            )
        if i >= len(hops) - 2:
            got_first = swap(image_first, *first_hops.pop(0))
            got, got_first = lax.optimization_barrier((got, got_first))
            image_first = image_first + got_first
        if i == len(hops) - 1:
            got, image_last = lax.optimization_barrier((got, image_last))
        gram = gram + got
    inverse_last = inverse_factor(gram, nodes)
    parts = call(
        basis_kernel, "basis", [(quarter, cols_here, block)] * count, ids, inverse_last, turned,
        scalars=1, scratch=[held],
    )
    for i, each_round in enumerate(rounds_of("node")):
        if i == 1:
            parts, image_last = lax.optimization_barrier((parts, image_last))
        got = round_swaps(image_last, *each_round)
        if i == 0:
            got_first = swap(image_first, *first_hops.pop(0))
            got, got_first, image_last, _ = lax.optimization_barrier((got, got_first, image_last, inverse_last))
            image_first = image_first + got_first
        image_last = round_sum(image_last, got)
    for hop in first_hops:
        image_first = image_first + swap(image_first, *hop)
    arrived = swapped(parts)
    parts = call(
        functools.partial(proj_kernel, nodes), "proj", [(2, cols_here, vecs)] * count, ids,
        inverse_first, image_first, inverse_last, image_last, scalars=1, scratch=[pltpu.VMEM(square, F32)],
    )
    (basis,) = call(
        functools.partial(join_kernel, half), "join", [(cols_here, width)], ids, *arrived, scalars=1
    )
    received, basis = lax.optimization_barrier((swapped(parts), basis))
    projected = sum(received)
    return basis, projected[0], projected[1]


def solution(mesh):
    placed = (P("node", None, None), P("node", None), P("node", None), P("col", "node"))
    return jax.shard_map(
        body,
        mesh=mesh,
        in_specs=placed,
        out_specs=(P("col", "node"), P("col", None), P("col", None)),
        check_vma=False,
    )
```

```python
import functools
import math
import jax
import jax.numpy as jnp
from jax import lax
from jax.experimental import pallas as pl
from jax.experimental.pallas import tpu as pltpu
from jax.sharding import PartitionSpec as P

DEGREE = 4
UNROLL = 72
CHUNK = 24
TURNS = 3
PANEL = 16
APPLY_BYTES = 4 << 20
F32, BF16, I32 = jnp.float32, jnp.bfloat16, jnp.int32
precise = lax.Precision.HIGHEST
center = 1.025
half_width = 0.975
MIB = 1 << 20
IN_VMEM = pl.BlockSpec(memory_space=pltpu.VMEM)
IN_SMEM = pl.BlockSpec(memory_space=pltpu.SMEM)


def nt(a, b):
    return lax.dot_general(
        a, b, (((1,), (1,)), ((), ())), precision=precise, preferred_element_type=F32
    )


def tn(a, b):
    return lax.dot_general(
        a, b, (((0,), (0,)), ((), ())), precision=precise, preferred_element_type=F32
    )


def nn(a, b):
    return jnp.dot(a, b, precision=precise, preferred_element_type=F32)


def call(kernel, name, outs, *args, scalars=0, scratch=(), cost=None):
    return pl.pallas_call(
        kernel,
        in_specs=[IN_SMEM] * scalars + [IN_VMEM] * (len(args) - scalars),
        out_specs=[IN_VMEM] * len(outs),
        out_shape=[jax.ShapeDtypeStruct(o, F32) for o in outs],
        scratch_shapes=list(scratch),
        compiler_params=pltpu.CompilerParams(vmem_limit_bytes=12 * MIB),
        cost_estimate=cost,
        name=name,
    )(*args)


def prep_kernel(rows, groups, ids_ref, own_ref, col_ref, blk_ref, w_ref, inv_ref, table_ref, held_ref, eye_ref, sem_ref):
    count, n, _ = held_ref.shape
    steps = sem_ref.shape[0]
    chunk = count // steps
    half = rows // 2
    me = ids_ref[0]
    odd = me % 2
    base = me * rows
    base_next = jnp.where(me == groups - 1, 0, me + 1) * rows
    base_last = jnp.where(me == 0, groups - 1, me - 1) * rows

    def fetch(step):
        span = pl.ds(step * chunk, chunk)
        return pltpu.make_async_copy(blk_ref.at[span], held_ref.at[span], sem_ref.at[step])

    for step in range(steps):
        fetch(step).start()
    table_ref[0] = me
    table_ref[1] = ids_ref[1]
    inv_ref[...] = jnp.zeros(inv_ref.shape, F32)
    lines = lax.broadcasted_iota(I32, eye_ref.shape, 0)
    lanes = lax.broadcasted_iota(I32, eye_ref.shape, 1)
    eye_ref[...] = jnp.where((lines == lanes) | (lines >= n), 1.0, 0.0).astype(BF16)

    def pack(step, carry):
        fetch(step).wait()
        for c in range(chunk):
            b = step * chunk + c
            r = own_ref[0, b]
            k = col_ref[0, b]
            mine = (k >= base) & (k < base + rows)
            ahead = (k >= base_next) & (k < base_next + half)
            local = k - jnp.where(mine, base, jnp.where(ahead, base_next, base_last))
            upper = (local >= half).astype(I32)
            near = local - half * upper
            swap = odd * upper + (1 - odd) * (1 - upper)
            slot = jnp.where(mine, near + half * swap, 2 * half + near + half * (1 - swap))
            top = (r >= half).astype(I32)
            r_at = r + half * (1 - odd) * (1 - 2 * top)
            table_ref[2 + b] = slot
            table_ref[2 + count + b] = r_at
            a = held_ref[b]
            if c % TURNS:
                t = a.T
                high = t.astype(BF16)
                w_ref[b, :, :n] = high
                w_ref[b, :, n:] = (t - high.astype(F32)).astype(BF16)
                inv_ref[r_at] = inv_ref[r_at] + jnp.sum(t, axis=0, keepdims=True)
            else:
                high = a.astype(BF16)
                low = (a - high.astype(F32)).astype(BF16)
                both = jnp.concatenate([high, low], axis=0)
                t = lax.dot_general(
                    eye_ref[...], both, (((1,), (1,)), ((), ())), preferred_element_type=F32
                )
                w_ref[b] = t[:n].astype(BF16)
                inv_ref[r_at] = inv_ref[r_at] + (t[n:n + 1, :n] + t[n:n + 1, n:])
        return carry

    lax.fori_loop(0, steps, pack, 0)
    inv_ref[...] = 1.0 / inv_ref[...]


def prep(ids, own, col, blocks, rows, groups):
    count, n, _ = blocks.shape
    own, col, blocks = (pltpu.with_memory_space_constraint(x, pltpu.HBM) for x in (own, col, blocks))
    return pl.pallas_call(
        functools.partial(prep_kernel, rows, groups),
        in_specs=[IN_SMEM] * 3 + [pl.BlockSpec(memory_space=pl.ANY)],
        out_specs=[IN_VMEM, IN_VMEM, IN_SMEM],
        out_shape=[pltpu.VMEM((count, n, 2 * n), BF16),
                   jax.ShapeDtypeStruct((rows, 1, n), F32),
                   jax.ShapeDtypeStruct((2 + 2 * count,), I32)],
        scratch_shapes=[
            pltpu.VMEM(blocks.shape, F32),
            pltpu.VMEM((n + 16, n), BF16),
            pltpu.SemaphoreType.DMA((count // math.gcd(count, CHUNK),)),
        ],
        compiler_params=pltpu.CompilerParams(vmem_limit_bytes=24 * MIB),
        cost_estimate=pl.CostEstimate(
            flops=2 * count * n * n * n, bytes_accessed=4 * blocks.size, transcendentals=0
        ),
        name="prep",
    )(ids, own, col, blocks)


def apply_kernel(recur, mate, *refs):
    refs = list(refs)
    table_ref, w_ref, inv_ref = refs[:3]
    panels = refs[3:7]
    del refs[:7]
    olds = [refs.pop(0) for _ in range(2 if recur else 0)]
    mates = [refs.pop(0) for _ in range(2 if mate else 0)]
    outs = [refs.pop(0) for _ in range(2)]
    parts = refs[:-2]
    sp_ref, acc_ref = refs[-2:]
    half, kk, n = panels[0].shape
    blocks = w_ref.shape[0]
    for i, ref in enumerate(panels):
        v = ref[...]
        high = v.astype(BF16)
        sp_ref[i * half:(i + 1) * half, :kk] = high
        sp_ref[i * half:(i + 1) * half, kk:] = (v - high.astype(F32)).astype(BF16)
    acc_ref[...] = jnp.zeros(acc_ref.shape, F32)
    unroll = math.gcd(blocks, UNROLL)

    def group(g, c):
        for u in range(unroll):
            b = g * unroll + u
            y = jnp.dot(sp_ref[table_ref[2 + b]], w_ref[b], preferred_element_type=F32)
            r = table_ref[2 + blocks + b]
            acc_ref[r] = acc_ref[r] + ((y[:kk, :n] + y[kk:, :n]) + (y[:kk, n:] + y[kk:, n:]))
        return c

    lax.fori_loop(0, blocks // unroll, group, 0)
    scale = (2.0 if recur else 1.0) / half_width
    for i in range(2):
        span = slice(i * half, (i + 1) * half)
        now = panels[i][...]
        image = (now - acc_ref[span] * inv_ref[span] - center * now) * scale
        if recur:
            image = image - olds[i][...]
        outs[i][...] = image
        if mate:
            acc_ref[span] = image
            parts[-1][span] = mates[i][...]
    if mate:
        count = len(parts) - 1
        me = table_ref[1]
        each = 2 * half // count
        for s in range(count):
            at = pl.ds((me ^ s) * each, each)
            parts[s][:, :kk] = parts[-1][at]
            parts[s][:, kk:] = acc_ref[at]


def apply(meta, pair, halo, old=(), mate=(), count=0):
    half, kk, n = pair[0].shape
    out = [jax.ShapeDtypeStruct((half, kk, n), F32)] * 2
    if mate:
        out += [jax.ShapeDtypeStruct((2 * half // count, 2 * kk, n), F32)] * count
    args = (*pair, *halo, *old, *mate)
    scratch = [pltpu.VMEM((4 * half, 2 * kk, n), BF16), pltpu.VMEM((2 * half, kk, n), F32)]
    if mate:
        scratch = [pltpu.VMEM((2 * half, kk, n), F32)] + scratch
    res = pl.pallas_call(
        functools.partial(apply_kernel, bool(old), bool(mate)),
        in_specs=[IN_SMEM] + [IN_VMEM] * (2 + len(args)),
        out_specs=[IN_VMEM] * len(out),
        out_shape=out,
        scratch_shapes=scratch,
        compiler_params=pltpu.CompilerParams(vmem_limit_bytes=12 * MIB),
        cost_estimate=pl.CostEstimate(
            flops=0, bytes_accessed=APPLY_BYTES, transcendentals=0
        ),
        name="apply" + "_recur" * bool(old) + "_parts" * bool(mate),
    )(*meta, *args)
    return tuple(res[:2]), tuple(res[2:])


def factor_kernel(nodes, g_ref, out_ref):
    n = g_ref.shape[0]
    p = PANEL
    out_ref[...] = g_ref[...] * (1.0 / nodes)
    sub = lax.broadcasted_iota(I32, (p, n), 0)
    lane = lax.broadcasted_iota(I32, (p, n), 1)
    for j in range(0, n, p):
        rows = out_ref[j:j + p]
        cols = [jnp.broadcast_to(rows[:, j + i:j + i + 1], (p, n)) for i in range(p)]
        rows = jnp.where((lane >= j) & (lane < j + p), jnp.where(lane - j == sub, 1.0, 0.0), rows)
        for i in range(p):
            root = lax.rsqrt(jnp.broadcast_to(cols[i][i:i + 1], (p, n)))
            ratio = jnp.where(sub > i, cols[i] * root, 0.0)
            scale = jnp.where(sub == i, root, 1.0)
            for k in range(i + 1, p):
                cols[k] = cols[k] - ratio * (jnp.broadcast_to(cols[k][i:i + 1], (p, n)) * root)
            rows = rows * scale - ratio * (jnp.broadcast_to(rows[i:i + 1], (p, n)) * root)
        out_ref[j:j + p] = jnp.where(lane < j + p, rows, 0.0)
        if j + p < n:
            change = nn(rows.T[j + p:], rows)
            lanes = lax.broadcasted_iota(I32, change.shape, 1)
            rest = out_ref[j + p:]
            out_ref[j + p:] = jnp.where((lanes >= j) & (lanes < j + p), 0.0, rest) - change


def inverse_factor(gram, nodes):
    n = gram.shape[0]
    return call(
        functools.partial(factor_kernel, nodes), "factor", [(n, n)], gram,
    )[0]


def gathered(ids_ref, parts, b, x_ref):
    each = parts[0].shape[1]
    me = ids_ref[1]
    for s, part in enumerate(parts):
        x_ref[b, pl.ds(pl.multiple_of((me ^ s) * each, each), each)] = part[b]
    return x_ref[b]


def couples(count):
    return [range(b, min(b + 2, count)) for b in range(0, count, 2)]


def wide(pieces):
    return jnp.concatenate(list(pieces), axis=1)


def gram_kernel(ids_ref, *refs):
    parts, (f_ref, g_ref) = refs[:-2], refs[-2:]
    total = jnp.zeros(g_ref.shape, F32)
    for pair in couples(f_ref.shape[0]):
        f = wide(gathered(ids_ref, parts, b, f_ref) for b in pair)
        total = total + nt(f, f)
    g_ref[...] = total


def cross_kernel(ids_ref, f_ref, g_ref, *refs):
    parts, (k_ref, x_ref) = refs[:-2], refs[-2:]
    total = jnp.zeros(k_ref.shape, F32)
    for pair in couples(f_ref.shape[0]):
        z = wide(gathered(ids_ref, parts, b, x_ref) for b in pair)
        total = total + nt(wide(f_ref[b] for b in pair), z)
    k_ref[...] = half_width * total + center * g_ref[...]


def turn_kernel(ids_ref, inv_ref, *refs):
    parts, (f_ref, g_ref, x_ref) = refs[:-3], refs[-3:]
    n = x_ref.shape[-1]
    total = jnp.zeros(g_ref.shape, F32)
    for pair in couples(f_ref.shape[0]):
        f = nn(inv_ref[...], wide(gathered(ids_ref, parts, b, x_ref) for b in pair))
        for i, b in enumerate(pair):
            f_ref[b] = f[:, i * n:(i + 1) * n]
        total = total + nt(f, f)
    g_ref[...] = total


def turn_cross_kernel(ids_ref, inv_ref, f_ref, g_ref, *refs):
    parts, (k_ref, x_ref) = refs[:-2], refs[-2:]
    total = jnp.zeros(g_ref.shape, F32)
    for pair in couples(f_ref.shape[0]):
        z = wide(gathered(ids_ref, parts, b, x_ref) for b in pair)
        total = total + nt(wide(f_ref[b] for b in pair), z)
    k_ref[...] = half_width * nt(total, inv_ref[...]) + center * g_ref[...]


def basis_kernel(ids_ref, inv_ref, f_ref, *refs):
    parts, x_ref = refs[:-1], refs[-1]
    each = parts[0].shape[1]
    me = ids_ref[1]
    n = x_ref.shape[-1]
    for pair in couples(f_ref.shape[0]):
        q = nn(inv_ref[...], wide(f_ref[b] for b in pair))
        for i, b in enumerate(pair):
            x_ref[b] = q[:, i * n:(i + 1) * n]
            for s, part in enumerate(parts):
                part[b] = x_ref[b, pl.ds(pl.multiple_of((me ^ s) * each, each), each)]


def proj_kernel(nodes, ids_ref, *refs):
    pairs, parts, x_ref = (refs[:2], refs[2:4]), refs[4:-1], refs[-1]
    each = parts[0].shape[1]
    me = ids_ref[1]
    for i, (inv_ref, image_ref) in enumerate(pairs):
        x_ref[...] = nt(nn(inv_ref[...], image_ref[...] * (1.0 / nodes)), inv_ref[...])
        for s, part in enumerate(parts):
            part[i] = x_ref[pl.ds(pl.multiple_of((me ^ s) * each, each), each)]


def slot_row(slot, half, odd):
    return slot + half * (1 - odd) * jnp.where(slot >= half, -1, 1)


def split_kernel(ids_ref, start_ref, *outs):
    half, kk, n = outs[0].shape
    odd = ids_ref[0] % 2
    for slot in range(2 * half):
        row = slot_row(slot, half, odd)
        piece = start_ref[:, pl.ds(pl.multiple_of(row * n, n), n)]
        for i in range(2):
            outs[2 * i + slot // half][slot % half] = piece[i * kk:(i + 1) * kk]


def join_kernel(half, ids_ref, *refs):
    parts, out_ref = refs[:-1], refs[-1]
    each, _, n = parts[0].shape
    odd = ids_ref[0] % 2
    me = ids_ref[1]
    for s, part in enumerate(parts):
        for b in range(each):
            row = slot_row((me ^ s) * each + b, half, odd)
            out_ref[:, pl.ds(pl.multiple_of(row * n, n), n)] = part[b]


def exchange(pair):
    count = lax.axis_size("node")
    even = [(i, i ^ 1) for i in range(count)]
    odd = [(i, (i - 1 if i % 2 == 0 else i + 1) % count) for i in range(count)]
    return lax.ppermute(pair[0], "node", even), lax.ppermute(pair[1], "node", odd)


def swap(value, axis, hop):
    return lax.ppermute(value, axis, [(i, i ^ hop) for i in range(lax.axis_size(axis))])


def swapped(parts):
    return [parts[0]] + [swap(parts[s], "col", s) for s in range(1, len(parts))]


def hops_of(*axes):
    return [(axis, 1 << i) for axis in axes for i in range((lax.axis_size(axis) - 1).bit_length())]


def rounds_of(*axes):
    rounds = []
    for axis in axes:
        bits = (lax.axis_size(axis) - 1).bit_length()
        while bits > 0:
            low = max(bits - 2, 0)
            rounds.append((axis, [1 << bit for bit in range(low, bits)]))
            bits = low
    return rounds


def round_swaps(value, axis, hops):
    hops = hops if len(hops) == 1 else [hops[0], hops[1], hops[0] ^ hops[1]]
    return [swap(value, axis, hop) for hop in hops]


def round_sum(value, got):
    value = value + got[0]
    return value if len(got) == 1 else value + (got[1] + got[2])


def body(blocks, owner_row, block_col, start):
    cols_here, width = start.shape
    block = blocks.shape[1]
    slots = width // block
    half = slots // 2
    count = lax.axis_size("col")
    nodes = width * lax.axis_size("node")
    vecs = cols_here * count
    each = cols_here // 2
    quarter = slots // count
    square = (vecs, vecs)
    held_shape = (quarter, vecs, block)
    held = pltpu.VMEM(held_shape, F32)
    ids = jnp.stack([lax.axis_index("node"), lax.axis_index("col")]).astype(I32)

    halves = call(split_kernel, "split", [(half, each, block)] * 4, ids, start, scalars=1)
    before = [tuple(halves[:2]), tuple(halves[2:])]
    w, inv, table = prep(ids, owner_row, block_col, blocks, slots, lax.axis_size("node"))
    meta = (table, w, inv)

    def advance(now, before=((), ()), parts=False):
        first, _ = apply(meta, now[0], exchange(now[0]), before[0])
        mate = first if parts else ()
        second, out = apply(meta, now[1], exchange(now[1]), before[1], mate, count)
        return [first, second], out

    now, _ = advance(before)
    for step in range(DEGREE - 1):
        after, parts = advance(now, before, step == DEGREE - 2)
        before, now = now, after
    panel, gram_first = call(gram_kernel, "gram", [held_shape, square], ids, *swapped(parts), scalars=1)
    after, parts = advance(now, parts=True)
    before, now = now, after
    image = swapped(parts)
    got, hops = None, hops_of("col", "node")
    gram = gram_first
    for step in range(DEGREE - 1):
        after = []
        for i in range(2):
            old, gram, got = lax.optimization_barrier((before[i], gram, got))
            if (step, i) == (1, 1):
                old, image = lax.optimization_barrier((old, image))
            if got is not None:
                gram = gram + got
            got = swap(gram, *hops.pop(0)) if hops else None
            mate = after[0] if i == 1 and step == DEGREE - 2 else ()
            done, parts = apply(meta, now[i], exchange(now[i]), old, mate, count)
            after.append(done)
            if got is not None:
                gram, got, _ = lax.optimization_barrier((gram, got, done))
        before, now = now, after
    if got is not None:
        gram = gram + got
    for hop in hops:
        gram = gram + swap(gram, *hop)
    halos = [exchange(panels) for panels in now]
    halos[0], gram = lax.optimization_barrier((halos[0], gram))
    inverse_first = inverse_factor(gram, nodes)
    (image_first,) = call(
        cross_kernel, "cross", [square], ids, panel, gram_first, *image, scalars=1, scratch=[held]
    )
    turned, gram_last = call(
        turn_kernel, "turn", [held_shape, square], ids, inverse_first, *swapped(parts), scalars=1, scratch=[held]
    )
    first, _ = apply(meta, now[0], halos[0])
    gram = gram_last
    hops = hops_of("col", "node")
    for i, hop in enumerate(hops):
        got = swap(gram, *hop)
        if i == 1:
            got, halos[1] = lax.optimization_barrier((got, halos[1]))
            _, parts = apply(meta, now[1], halos[1], (), first, count)
            (image_last,) = call(
                turn_cross_kernel, "turn_cross", [square], ids, inverse_first, turned, gram_last,
                *swapped(parts), scalars=1, scratch=[held],
            )
        if i == len(hops) - 2:
            got, image_first = lax.optimization_barrier((got, image_first))
        if i == len(hops) - 1:
            got, image_last = lax.optimization_barrier((got, image_last))
        gram = gram + got
    inverse_last = inverse_factor(gram, nodes)
    parts = call(
        basis_kernel, "basis", [(quarter, cols_here, block)] * count, ids, inverse_last, turned,
        scalars=1, scratch=[held],
    )
    for i, each_round in enumerate(rounds_of("node")):
        if i == 1:
            parts, image_last = lax.optimization_barrier((parts, image_last))
        got_first = round_swaps(image_first, *each_round)
        got = round_swaps(image_last, *each_round)
        if i == 0:
            got, got_first, image_last, _ = lax.optimization_barrier((got, got_first, image_last, inverse_last))
        image_first = round_sum(image_first, got_first)
        image_last = round_sum(image_last, got)
    arrived = swapped(parts)
    parts = call(
        functools.partial(proj_kernel, nodes), "proj", [(2, cols_here, vecs)] * count, ids,
        inverse_first, image_first, inverse_last, image_last, scalars=1, scratch=[pltpu.VMEM(square, F32)],
    )
    (basis,) = call(
        functools.partial(join_kernel, half), "join", [(cols_here, width)], ids, *arrived, scalars=1
    )
    received, basis = lax.optimization_barrier((swapped(parts), basis))
    projected = sum(received)
    return basis, projected[0], projected[1]


def solution(mesh):
    placed = (P("node", None, None), P("node", None), P("node", None), P("col", "node"))
    return jax.shard_map(
        body,
        mesh=mesh,
        in_specs=placed,
        out_specs=(P("col", "node"), P("col", None), P("col", None)),
        check_vma=False,
    )
```

```python
import functools
import math
import jax
import jax.numpy as jnp
from jax import lax
from jax.experimental import pallas as pl
from jax.experimental.pallas import tpu as pltpu
from jax.sharding import PartitionSpec as P

DEGREE = 4
UNROLL = 72
CHUNK = 24
TURNS = 3
PANEL = 16
APPLY_BYTES = 4 << 20
F32, BF16, I32 = jnp.float32, jnp.bfloat16, jnp.int32
precise = lax.Precision.HIGHEST
center = 1.025
half_width = 0.975
MIB = 1 << 20
IN_VMEM = pl.BlockSpec(memory_space=pltpu.VMEM)
IN_SMEM = pl.BlockSpec(memory_space=pltpu.SMEM)


def nt(a, b):
    return lax.dot_general(
        a, b, (((1,), (1,)), ((), ())), precision=precise, preferred_element_type=F32
    )


def tn(a, b):
    return lax.dot_general(
        a, b, (((0,), (0,)), ((), ())), precision=precise, preferred_element_type=F32
    )


def nn(a, b):
    return jnp.dot(a, b, precision=precise, preferred_element_type=F32)


def call(kernel, name, outs, *args, scalars=0, scratch=(), cost=None):
    return pl.pallas_call(
        kernel,
        in_specs=[IN_SMEM] * scalars + [IN_VMEM] * (len(args) - scalars),
        out_specs=[IN_VMEM] * len(outs),
        out_shape=[jax.ShapeDtypeStruct(o, F32) for o in outs],
        scratch_shapes=list(scratch),
        compiler_params=pltpu.CompilerParams(vmem_limit_bytes=12 * MIB),
        cost_estimate=cost,
        name=name,
    )(*args)


def prep_kernel(rows, groups, ids_ref, own_ref, col_ref, blk_ref, w_ref, inv_ref, table_ref, held_ref, eye_ref, sem_ref):
    count, n, _ = held_ref.shape
    steps = sem_ref.shape[0]
    chunk = count // steps
    half = rows // 2
    me = ids_ref[0]
    odd = me % 2
    base = me * rows
    base_next = jnp.where(me == groups - 1, 0, me + 1) * rows
    base_last = jnp.where(me == 0, groups - 1, me - 1) * rows

    def fetch(step):
        span = pl.ds(step * chunk, chunk)
        return pltpu.make_async_copy(blk_ref.at[span], held_ref.at[span], sem_ref.at[step])

    for step in range(steps):
        fetch(step).start()
    table_ref[0] = me
    table_ref[1] = ids_ref[1]
    inv_ref[...] = jnp.zeros(inv_ref.shape, F32)
    lines = lax.broadcasted_iota(I32, eye_ref.shape, 0)
    lanes = lax.broadcasted_iota(I32, eye_ref.shape, 1)
    eye_ref[...] = jnp.where((lines == lanes) | (lines >= n), 1.0, 0.0).astype(BF16)

    def pack(step, carry):
        fetch(step).wait()
        for c in range(chunk):
            b = step * chunk + c
            r = own_ref[0, b]
            k = col_ref[0, b]
            mine = (k >= base) & (k < base + rows)
            ahead = (k >= base_next) & (k < base_next + half)
            local = k - jnp.where(mine, base, jnp.where(ahead, base_next, base_last))
            upper = (local >= half).astype(I32)
            near = local - half * upper
            swap = odd * upper + (1 - odd) * (1 - upper)
            slot = jnp.where(mine, near + half * swap, 2 * half + near + half * (1 - swap))
            top = (r >= half).astype(I32)
            r_at = r + half * (1 - odd) * (1 - 2 * top)
            table_ref[2 + b] = slot
            table_ref[2 + count + b] = r_at
            a = held_ref[b]
            if c % TURNS:
                t = a.T
                high = t.astype(BF16)
                w_ref[b, :, :n] = high
                w_ref[b, :, n:] = (t - high.astype(F32)).astype(BF16)
                inv_ref[r_at] = inv_ref[r_at] + jnp.sum(t, axis=0, keepdims=True)
            else:
                high = a.astype(BF16)
                low = (a - high.astype(F32)).astype(BF16)
                both = jnp.concatenate([high, low], axis=0)
                t = lax.dot_general(
                    eye_ref[...], both, (((1,), (1,)), ((), ())), preferred_element_type=F32
                )
                w_ref[b] = t[:n].astype(BF16)
                inv_ref[r_at] = inv_ref[r_at] + (t[n:n + 1, :n] + t[n:n + 1, n:])
        return carry

    lax.fori_loop(0, steps, pack, 0)
    inv_ref[...] = 1.0 / inv_ref[...]


def prep(ids, own, col, blocks, rows, groups):
    count, n, _ = blocks.shape
    own, col, blocks = (pltpu.with_memory_space_constraint(x, pltpu.HBM) for x in (own, col, blocks))
    return pl.pallas_call(
        functools.partial(prep_kernel, rows, groups),
        in_specs=[IN_SMEM] * 3 + [pl.BlockSpec(memory_space=pl.ANY)],
        out_specs=[IN_VMEM, IN_VMEM, IN_SMEM],
        out_shape=[pltpu.VMEM((count, n, 2 * n), BF16),
                   jax.ShapeDtypeStruct((rows, 1, n), F32),
                   jax.ShapeDtypeStruct((2 + 2 * count,), I32)],
        scratch_shapes=[
            pltpu.VMEM(blocks.shape, F32),
            pltpu.VMEM((n + 16, n), BF16),
            pltpu.SemaphoreType.DMA((count // math.gcd(count, CHUNK),)),
        ],
        compiler_params=pltpu.CompilerParams(vmem_limit_bytes=24 * MIB),
        cost_estimate=pl.CostEstimate(
            flops=2 * count * n * n * n, bytes_accessed=4 * blocks.size, transcendentals=0
        ),
        name="prep",
    )(ids, own, col, blocks)


def apply_kernel(recur, mate, *refs):
    refs = list(refs)
    table_ref, w_ref, inv_ref = refs[:3]
    panels = refs[3:7]
    del refs[:7]
    olds = [refs.pop(0) for _ in range(2 if recur else 0)]
    mates = [refs.pop(0) for _ in range(2 if mate else 0)]
    outs = [refs.pop(0) for _ in range(2)]
    parts = refs[:-2]
    sp_ref, acc_ref = refs[-2:]
    half, kk, n = panels[0].shape
    blocks = w_ref.shape[0]
    for i, ref in enumerate(panels):
        v = ref[...]
        high = v.astype(BF16)
        sp_ref[i * half:(i + 1) * half, :kk] = high
        sp_ref[i * half:(i + 1) * half, kk:] = (v - high.astype(F32)).astype(BF16)
    acc_ref[...] = jnp.zeros(acc_ref.shape, F32)
    unroll = math.gcd(blocks, UNROLL)

    def group(g, c):
        for u in range(unroll):
            b = g * unroll + u
            y = jnp.dot(sp_ref[table_ref[2 + b]], w_ref[b], preferred_element_type=F32)
            r = table_ref[2 + blocks + b]
            acc_ref[r] = acc_ref[r] + ((y[:kk, :n] + y[kk:, :n]) + (y[:kk, n:] + y[kk:, n:]))
        return c

    lax.fori_loop(0, blocks // unroll, group, 0)
    scale = (2.0 if recur else 1.0) / half_width
    for i in range(2):
        span = slice(i * half, (i + 1) * half)
        now = panels[i][...]
        image = (now - acc_ref[span] * inv_ref[span] - center * now) * scale
        if recur:
            image = image - olds[i][...]
        outs[i][...] = image
        if mate:
            acc_ref[span] = image
            parts[-1][span] = mates[i][...]
    if mate:
        count = len(parts) - 1
        me = table_ref[1]
        each = 2 * half // count
        for s in range(count):
            at = pl.ds((me ^ s) * each, each)
            parts[s][:, :kk] = parts[-1][at]
            parts[s][:, kk:] = acc_ref[at]


def apply(meta, pair, halo, old=(), mate=(), count=0):
    half, kk, n = pair[0].shape
    out = [jax.ShapeDtypeStruct((half, kk, n), F32)] * 2
    if mate:
        out += [jax.ShapeDtypeStruct((2 * half // count, 2 * kk, n), F32)] * count
    args = (*pair, *halo, *old, *mate)
    scratch = [pltpu.VMEM((4 * half, 2 * kk, n), BF16), pltpu.VMEM((2 * half, kk, n), F32)]
    if mate:
        scratch = [pltpu.VMEM((2 * half, kk, n), F32)] + scratch
    res = pl.pallas_call(
        functools.partial(apply_kernel, bool(old), bool(mate)),
        in_specs=[IN_SMEM] + [IN_VMEM] * (2 + len(args)),
        out_specs=[IN_VMEM] * len(out),
        out_shape=out,
        scratch_shapes=scratch,
        compiler_params=pltpu.CompilerParams(vmem_limit_bytes=12 * MIB),
        cost_estimate=pl.CostEstimate(
            flops=0, bytes_accessed=APPLY_BYTES, transcendentals=0
        ),
        name="apply" + "_recur" * bool(old) + "_parts" * bool(mate),
    )(*meta, *args)
    return tuple(res[:2]), tuple(res[2:])


def factor_kernel(nodes, g_ref, out_ref):
    n = g_ref.shape[0]
    p = PANEL
    out_ref[...] = g_ref[...] * (1.0 / nodes)
    sub = lax.broadcasted_iota(I32, (p, n), 0)
    lane = lax.broadcasted_iota(I32, (p, n), 1)
    for j in range(0, n, p):
        rows = out_ref[j:j + p]
        cols = [jnp.broadcast_to(rows[:, j + i:j + i + 1], (p, n)) for i in range(p)]
        rows = jnp.where((lane >= j) & (lane < j + p), jnp.where(lane - j == sub, 1.0, 0.0), rows)
        for i in range(p):
            root = lax.rsqrt(jnp.broadcast_to(cols[i][i:i + 1], (p, n)))
            ratio = jnp.where(sub > i, cols[i] * root, 0.0)
            scale = jnp.where(sub == i, root, 1.0)
            for k in range(i + 1, p):
                cols[k] = cols[k] - ratio * (jnp.broadcast_to(cols[k][i:i + 1], (p, n)) * root)
            rows = rows * scale - ratio * (jnp.broadcast_to(rows[i:i + 1], (p, n)) * root)
        out_ref[j:j + p] = jnp.where(lane < j + p, rows, 0.0)
        if j + p < n:
            change = nn(rows.T[j + p:], rows)
            lanes = lax.broadcasted_iota(I32, change.shape, 1)
            rest = out_ref[j + p:]
            out_ref[j + p:] = jnp.where((lanes >= j) & (lanes < j + p), 0.0, rest) - change


def inverse_factor(gram, nodes):
    n = gram.shape[0]
    return call(
        functools.partial(factor_kernel, nodes), "factor", [(n, n)], gram,
    )[0]


def gathered(ids_ref, parts, b, x_ref):
    each = parts[0].shape[1]
    me = ids_ref[1]
    for s, part in enumerate(parts):
        x_ref[b, pl.ds(pl.multiple_of((me ^ s) * each, each), each)] = part[b]
    return x_ref[b]


def couples(count):
    return [range(b, min(b + 2, count)) for b in range(0, count, 2)]


def wide(pieces):
    return jnp.concatenate(list(pieces), axis=1)


def gram_kernel(ids_ref, *refs):
    parts, (f_ref, g_ref) = refs[:-2], refs[-2:]
    total = jnp.zeros(g_ref.shape, F32)
    for pair in couples(f_ref.shape[0]):
        f = wide(gathered(ids_ref, parts, b, f_ref) for b in pair)
        total = total + nt(f, f)
    g_ref[...] = total


def cross_kernel(ids_ref, f_ref, g_ref, *refs):
    parts, (k_ref, x_ref) = refs[:-2], refs[-2:]
    total = jnp.zeros(k_ref.shape, F32)
    for pair in couples(f_ref.shape[0]):
        z = wide(gathered(ids_ref, parts, b, x_ref) for b in pair)
        total = total + nt(wide(f_ref[b] for b in pair), z)
    k_ref[...] = half_width * total + center * g_ref[...]


def turn_kernel(ids_ref, inv_ref, *refs):
    parts, (f_ref, g_ref, x_ref) = refs[:-3], refs[-3:]
    n = x_ref.shape[-1]
    total = jnp.zeros(g_ref.shape, F32)
    for pair in couples(f_ref.shape[0]):
        f = nn(inv_ref[...], wide(gathered(ids_ref, parts, b, x_ref) for b in pair))
        for i, b in enumerate(pair):
            f_ref[b] = f[:, i * n:(i + 1) * n]
        total = total + nt(f, f)
    g_ref[...] = total


def turn_cross_kernel(ids_ref, inv_ref, f_ref, g_ref, *refs):
    parts, (k_ref, x_ref) = refs[:-2], refs[-2:]
    total = jnp.zeros(g_ref.shape, F32)
    for pair in couples(f_ref.shape[0]):
        z = wide(gathered(ids_ref, parts, b, x_ref) for b in pair)
        total = total + nt(wide(f_ref[b] for b in pair), z)
    k_ref[...] = half_width * nt(total, inv_ref[...]) + center * g_ref[...]


def basis_kernel(ids_ref, inv_ref, f_ref, *refs):
    parts, x_ref = refs[:-1], refs[-1]
    each = parts[0].shape[1]
    me = ids_ref[1]
    n = x_ref.shape[-1]
    for pair in couples(f_ref.shape[0]):
        q = nn(inv_ref[...], wide(f_ref[b] for b in pair))
        for i, b in enumerate(pair):
            x_ref[b] = q[:, i * n:(i + 1) * n]
            for s, part in enumerate(parts):
                part[b] = x_ref[b, pl.ds(pl.multiple_of((me ^ s) * each, each), each)]


def proj_kernel(nodes, ids_ref, *refs):
    pairs, parts, x_ref = (refs[:2], refs[2:4]), refs[4:-1], refs[-1]
    each = parts[0].shape[1]
    me = ids_ref[1]
    for i, (inv_ref, image_ref) in enumerate(pairs):
        x_ref[...] = nt(nn(inv_ref[...], image_ref[...] * (1.0 / nodes)), inv_ref[...])
        for s, part in enumerate(parts):
            part[i] = x_ref[pl.ds(pl.multiple_of((me ^ s) * each, each), each)]


def slot_row(slot, half, odd):
    return slot + half * (1 - odd) * jnp.where(slot >= half, -1, 1)


def split_kernel(ids_ref, start_ref, *outs):
    half, kk, n = outs[0].shape
    odd = ids_ref[0] % 2
    for slot in range(2 * half):
        row = slot_row(slot, half, odd)
        piece = start_ref[:, pl.ds(pl.multiple_of(row * n, n), n)]
        for i in range(2):
            outs[2 * i + slot // half][slot % half] = piece[i * kk:(i + 1) * kk]


def join_kernel(half, ids_ref, *refs):
    parts, out_ref = refs[:-1], refs[-1]
    each, _, n = parts[0].shape
    odd = ids_ref[0] % 2
    me = ids_ref[1]
    for s, part in enumerate(parts):
        for b in range(each):
            row = slot_row((me ^ s) * each + b, half, odd)
            out_ref[:, pl.ds(pl.multiple_of(row * n, n), n)] = part[b]


def exchange(pair):
    count = lax.axis_size("node")
    even = [(i, i ^ 1) for i in range(count)]
    odd = [(i, (i - 1 if i % 2 == 0 else i + 1) % count) for i in range(count)]
    return lax.ppermute(pair[0], "node", even), lax.ppermute(pair[1], "node", odd)


def swap(value, axis, hop):
    return lax.ppermute(value, axis, [(i, i ^ hop) for i in range(lax.axis_size(axis))])


def swapped(parts):
    return [parts[0]] + [swap(parts[s], "col", s) for s in range(1, len(parts))]


def hops_of(*axes):
    return [(axis, 1 << i) for axis in axes for i in range((lax.axis_size(axis) - 1).bit_length())]


def rounds_of(*axes):
    rounds = []
    for axis in axes:
        bits = (lax.axis_size(axis) - 1).bit_length()
        while bits > 0:
            low = max(bits - 2, 0)
            rounds.append((axis, [1 << bit for bit in range(low, bits)]))
            bits = low
    return rounds


def round_swaps(value, axis, hops):
    hops = hops if len(hops) == 1 else [hops[0], hops[1], hops[0] ^ hops[1]]
    return [swap(value, axis, hop) for hop in hops]


def round_sum(value, got):
    value = value + got[0]
    return value if len(got) == 1 else value + (got[1] + got[2])


def body(blocks, owner_row, block_col, start):
    cols_here, width = start.shape
    block = blocks.shape[1]
    slots = width // block
    half = slots // 2
    count = lax.axis_size("col")
    nodes = width * lax.axis_size("node")
    vecs = cols_here * count
    each = cols_here // 2
    quarter = slots // count
    square = (vecs, vecs)
    held_shape = (quarter, vecs, block)
    held = pltpu.VMEM(held_shape, F32)
    ids = jnp.stack([lax.axis_index("node"), lax.axis_index("col")]).astype(I32)

    halves = call(split_kernel, "split", [(half, each, block)] * 4, ids, start, scalars=1)
    before = [tuple(halves[:2]), tuple(halves[2:])]
    w, inv, table = prep(ids, owner_row, block_col, blocks, slots, lax.axis_size("node"))
    meta = (table, w, inv)

    def advance(now, before=((), ()), parts=False):
        first, _ = apply(meta, now[0], exchange(now[0]), before[0])
        mate = first if parts else ()
        second, out = apply(meta, now[1], exchange(now[1]), before[1], mate, count)
        return [first, second], out

    now, _ = advance(before)
    for step in range(DEGREE - 1):
        after, parts = advance(now, before, step == DEGREE - 2)
        before, now = now, after
    panel, gram_first = call(gram_kernel, "gram", [held_shape, square], ids, *swapped(parts), scalars=1)
    after, parts = advance(now, parts=True)
    before, now = now, after
    image = swapped(parts)
    got, hops = None, hops_of("col", "node")
    gram = gram_first
    for step in range(DEGREE - 1):
        after = []
        for i in range(2):
            old, gram, got = lax.optimization_barrier((before[i], gram, got))
            if (step, i) == (1, 1):
                old, image = lax.optimization_barrier((old, image))
            if got is not None:
                gram = gram + got
            got = swap(gram, *hops.pop(0)) if hops and (step, i) != (1, 1) else None
            mate = after[0] if i == 1 and step == DEGREE - 2 else ()
            done, parts = apply(meta, now[i], exchange(now[i]), old, mate, count)
            after.append(done)
            if got is not None:
                gram, got, _ = lax.optimization_barrier((gram, got, done))
        before, now = now, after
    if got is not None:
        gram = gram + got
    for hop in hops:
        gram = gram + swap(gram, *hop)
    halos = [exchange(panels) for panels in now]
    halos[0], gram = lax.optimization_barrier((halos[0], gram))
    inverse_first = inverse_factor(gram, nodes)
    (image_first,) = call(
        cross_kernel, "cross", [square], ids, panel, gram_first, *image, scalars=1, scratch=[held]
    )
    turned, gram_last = call(
        turn_kernel, "turn", [held_shape, square], ids, inverse_first, *swapped(parts), scalars=1, scratch=[held]
    )
    first, _ = apply(meta, now[0], halos[0])
    gram = gram_last
    hops = hops_of("col", "node")
    for i, hop in enumerate(hops):
        got = swap(gram, *hop)
        if i == 1:
            got, halos[1] = lax.optimization_barrier((got, halos[1]))
            _, parts = apply(meta, now[1], halos[1], (), first, count)
            (image_last,) = call(
                turn_cross_kernel, "turn_cross", [square], ids, inverse_first, turned, gram_last,
                *swapped(parts), scalars=1, scratch=[held],
            )
        if i == len(hops) - 2:
            got, image_first = lax.optimization_barrier((got, image_first))
        if i == len(hops) - 1:
            got, image_last = lax.optimization_barrier((got, image_last))
        gram = gram + got
    inverse_last = inverse_factor(gram, nodes)
    parts = call(
        basis_kernel, "basis", [(quarter, cols_here, block)] * count, ids, inverse_last, turned,
        scalars=1, scratch=[held],
    )
    for i, each_round in enumerate(rounds_of("node")):
        if i == 1:
            parts, image_last = lax.optimization_barrier((parts, image_last))
        got_first = round_swaps(image_first, *each_round)
        got = round_swaps(image_last, *each_round)
        if i == 0:
            got, got_first, image_last, _ = lax.optimization_barrier((got, got_first, image_last, inverse_last))
        image_first = round_sum(image_first, got_first)
        image_last = round_sum(image_last, got)
    arrived = swapped(parts)
    parts = call(
        functools.partial(proj_kernel, nodes), "proj", [(2, cols_here, vecs)] * count, ids,
        inverse_first, image_first, inverse_last, image_last, scalars=1, scratch=[pltpu.VMEM(square, F32)],
    )
    (basis,) = call(
        functools.partial(join_kernel, half), "join", [(cols_here, width)], ids, *arrived, scalars=1
    )
    received, basis = lax.optimization_barrier((swapped(parts), basis))
    projected = sum(received)
    return basis, projected[0], projected[1]


def solution(mesh):
    placed = (P("node", None, None), P("node", None), P("node", None), P("col", "node"))
    return jax.shard_map(
        body,
        mesh=mesh,
        in_specs=placed,
        out_specs=(P("col", "node"), P("col", None), P("col", None)),
        check_vma=False,
    )
```

```python
import functools
import math
import jax
import jax.numpy as jnp
from jax import lax
from jax.experimental import pallas as pl
from jax.experimental.pallas import tpu as pltpu
from jax.sharding import PartitionSpec as P

DEGREE = 4
UNROLL = 72
CHUNK = 24
TURNS = 3
PANEL = 16
APPLY_BYTES = 4 << 20
F32, BF16, I32 = jnp.float32, jnp.bfloat16, jnp.int32
precise = lax.Precision.HIGHEST
center = 1.025
half_width = 0.975
MIB = 1 << 20
IN_VMEM = pl.BlockSpec(memory_space=pltpu.VMEM)
IN_SMEM = pl.BlockSpec(memory_space=pltpu.SMEM)


def nt(a, b):
    return lax.dot_general(
        a, b, (((1,), (1,)), ((), ())), precision=precise, preferred_element_type=F32
    )


def tn(a, b):
    return lax.dot_general(
        a, b, (((0,), (0,)), ((), ())), precision=precise, preferred_element_type=F32
    )


def nn(a, b):
    return jnp.dot(a, b, precision=precise, preferred_element_type=F32)


def call(kernel, name, outs, *args, scalars=0, scratch=(), cost=None):
    return pl.pallas_call(
        kernel,
        in_specs=[IN_SMEM] * scalars + [IN_VMEM] * (len(args) - scalars),
        out_specs=[IN_VMEM] * len(outs),
        out_shape=[jax.ShapeDtypeStruct(o, F32) for o in outs],
        scratch_shapes=list(scratch),
        compiler_params=pltpu.CompilerParams(vmem_limit_bytes=12 * MIB),
        cost_estimate=cost,
        name=name,
    )(*args)


def prep_kernel(rows, groups, ids_ref, own_ref, col_ref, blk_ref, w_ref, inv_ref, table_ref, held_ref, eye_ref, sem_ref):
    count, n, _ = held_ref.shape
    steps = sem_ref.shape[0]
    chunk = count // steps
    half = rows // 2
    me = ids_ref[0]
    odd = me % 2
    base = me * rows
    base_next = jnp.where(me == groups - 1, 0, me + 1) * rows
    base_last = jnp.where(me == 0, groups - 1, me - 1) * rows

    def fetch(step):
        span = pl.ds(step * chunk, chunk)
        return pltpu.make_async_copy(blk_ref.at[span], held_ref.at[span], sem_ref.at[step])

    for step in range(steps):
        fetch(step).start()
    table_ref[0] = me
    table_ref[1] = ids_ref[1]
    inv_ref[...] = jnp.zeros(inv_ref.shape, F32)
    lines = lax.broadcasted_iota(I32, eye_ref.shape, 0)
    lanes = lax.broadcasted_iota(I32, eye_ref.shape, 1)
    eye_ref[...] = jnp.where((lines == lanes) | (lines >= n), 1.0, 0.0).astype(BF16)

    def pack(step, carry):
        fetch(step).wait()
        for c in range(chunk):
            b = step * chunk + c
            r = own_ref[0, b]
            k = col_ref[0, b]
            mine = (k >= base) & (k < base + rows)
            ahead = (k >= base_next) & (k < base_next + half)
            local = k - jnp.where(mine, base, jnp.where(ahead, base_next, base_last))
            upper = (local >= half).astype(I32)
            near = local - half * upper
            swap = odd * upper + (1 - odd) * (1 - upper)
            slot = jnp.where(mine, near + half * swap, 2 * half + near + half * (1 - swap))
            top = (r >= half).astype(I32)
            r_at = r + half * (1 - odd) * (1 - 2 * top)
            table_ref[2 + b] = slot
            table_ref[2 + count + b] = r_at
            a = held_ref[b]
            if c % TURNS:
                t = a.T
                high = t.astype(BF16)
                w_ref[b, :, :n] = high
                w_ref[b, :, n:] = (t - high.astype(F32)).astype(BF16)
                inv_ref[r_at] = inv_ref[r_at] + jnp.sum(t, axis=0, keepdims=True)
            else:
                high = a.astype(BF16)
                low = (a - high.astype(F32)).astype(BF16)
                both = jnp.concatenate([high, low], axis=0)
                t = lax.dot_general(
                    eye_ref[...], both, (((1,), (1,)), ((), ())), preferred_element_type=F32
                )
                w_ref[b] = t[:n].astype(BF16)
                inv_ref[r_at] = inv_ref[r_at] + (t[n:n + 1, :n] + t[n:n + 1, n:])
        return carry

    lax.fori_loop(0, steps, pack, 0)
    inv_ref[...] = 1.0 / inv_ref[...]


def prep(ids, own, col, blocks, rows, groups):
    count, n, _ = blocks.shape
    own, col, blocks = (pltpu.with_memory_space_constraint(x, pltpu.HBM) for x in (own, col, blocks))
    return pl.pallas_call(
        functools.partial(prep_kernel, rows, groups),
        in_specs=[IN_SMEM] * 3 + [pl.BlockSpec(memory_space=pl.ANY)],
        out_specs=[IN_VMEM, IN_VMEM, IN_SMEM],
        out_shape=[pltpu.VMEM((count, n, 2 * n), BF16),
                   jax.ShapeDtypeStruct((rows, 1, n), F32),
                   jax.ShapeDtypeStruct((2 + 2 * count,), I32)],
        scratch_shapes=[
            pltpu.VMEM(blocks.shape, F32),
            pltpu.VMEM((n + 16, n), BF16),
            pltpu.SemaphoreType.DMA((count // math.gcd(count, CHUNK),)),
        ],
        compiler_params=pltpu.CompilerParams(vmem_limit_bytes=24 * MIB),
        cost_estimate=pl.CostEstimate(
            flops=2 * count * n * n * n, bytes_accessed=4 * blocks.size, transcendentals=0
        ),
        name="prep",
    )(ids, own, col, blocks)


def apply_kernel(recur, mate, *refs):
    refs = list(refs)
    table_ref, w_ref, inv_ref = refs[:3]
    panels = refs[3:7]
    del refs[:7]
    olds = [refs.pop(0) for _ in range(2 if recur else 0)]
    mates = [refs.pop(0) for _ in range(2 if mate else 0)]
    outs = [refs.pop(0) for _ in range(2)]
    parts = refs[:-2]
    sp_ref, acc_ref = refs[-2:]
    half, kk, n = panels[0].shape
    blocks = w_ref.shape[0]
    for i, ref in enumerate(panels):
        v = ref[...]
        high = v.astype(BF16)
        sp_ref[i * half:(i + 1) * half, :kk] = high
        sp_ref[i * half:(i + 1) * half, kk:] = (v - high.astype(F32)).astype(BF16)
    acc_ref[...] = jnp.zeros(acc_ref.shape, F32)
    unroll = math.gcd(blocks, UNROLL)

    def group(g, c):
        for u in range(unroll):
            b = g * unroll + u
            y = jnp.dot(sp_ref[table_ref[2 + b]], w_ref[b], preferred_element_type=F32)
            r = table_ref[2 + blocks + b]
            acc_ref[r] = acc_ref[r] + ((y[:kk, :n] + y[kk:, :n]) + (y[:kk, n:] + y[kk:, n:]))
        return c

    lax.fori_loop(0, blocks // unroll, group, 0)
    scale = (2.0 if recur else 1.0) / half_width
    for i in range(2):
        span = slice(i * half, (i + 1) * half)
        now = panels[i][...]
        image = (now - acc_ref[span] * inv_ref[span] - center * now) * scale
        if recur:
            image = image - olds[i][...]
        outs[i][...] = image
        if mate:
            acc_ref[span] = image
            parts[-1][span] = mates[i][...]
    if mate:
        count = len(parts) - 1
        me = table_ref[1]
        each = 2 * half // count
        for s in range(count):
            at = pl.ds((me ^ s) * each, each)
            parts[s][:, :kk] = parts[-1][at]
            parts[s][:, kk:] = acc_ref[at]


def apply(meta, pair, halo, old=(), mate=(), count=0):
    half, kk, n = pair[0].shape
    out = [jax.ShapeDtypeStruct((half, kk, n), F32)] * 2
    if mate:
        out += [jax.ShapeDtypeStruct((2 * half // count, 2 * kk, n), F32)] * count
    args = (*pair, *halo, *old, *mate)
    scratch = [pltpu.VMEM((4 * half, 2 * kk, n), BF16), pltpu.VMEM((2 * half, kk, n), F32)]
    if mate:
        scratch = [pltpu.VMEM((2 * half, kk, n), F32)] + scratch
    res = pl.pallas_call(
        functools.partial(apply_kernel, bool(old), bool(mate)),
        in_specs=[IN_SMEM] + [IN_VMEM] * (2 + len(args)),
        out_specs=[IN_VMEM] * len(out),
        out_shape=out,
        scratch_shapes=scratch,
        compiler_params=pltpu.CompilerParams(vmem_limit_bytes=12 * MIB),
        cost_estimate=pl.CostEstimate(
            flops=0, bytes_accessed=APPLY_BYTES, transcendentals=0
        ),
        name="apply" + "_recur" * bool(old) + "_parts" * bool(mate),
    )(*meta, *args)
    return tuple(res[:2]), tuple(res[2:])


def factor_kernel(nodes, g_ref, out_ref):
    n = g_ref.shape[0]
    p = PANEL
    out_ref[...] = g_ref[...] * (1.0 / nodes)
    sub = lax.broadcasted_iota(I32, (p, n), 0)
    lane = lax.broadcasted_iota(I32, (p, n), 1)
    for j in range(0, n, p):
        rows = out_ref[j:j + p]
        cols = [jnp.broadcast_to(rows[:, j + i:j + i + 1], (p, n)) for i in range(p)]
        rows = jnp.where((lane >= j) & (lane < j + p), jnp.where(lane - j == sub, 1.0, 0.0), rows)
        for i in range(p):
            root = lax.rsqrt(jnp.broadcast_to(cols[i][i:i + 1], (p, n)))
            ratio = jnp.where(sub > i, cols[i] * root, 0.0)
            scale = jnp.where(sub == i, root, 1.0)
            for k in range(i + 1, p):
                cols[k] = cols[k] - ratio * (jnp.broadcast_to(cols[k][i:i + 1], (p, n)) * root)
            rows = rows * scale - ratio * (jnp.broadcast_to(rows[i:i + 1], (p, n)) * root)
        out_ref[j:j + p] = jnp.where(lane < j + p, rows, 0.0)
        if j + p < n:
            change = nn(rows.T[j + p:], rows)
            lanes = lax.broadcasted_iota(I32, change.shape, 1)
            rest = out_ref[j + p:]
            out_ref[j + p:] = jnp.where((lanes >= j) & (lanes < j + p), 0.0, rest) - change


def inverse_factor(gram, nodes):
    n = gram.shape[0]
    return call(
        functools.partial(factor_kernel, nodes), "factor", [(n, n)], gram,
    )[0]


def gathered(ids_ref, parts, b, x_ref):
    each = parts[0].shape[1]
    me = ids_ref[1]
    for s, part in enumerate(parts):
        x_ref[b, pl.ds(pl.multiple_of((me ^ s) * each, each), each)] = part[b]
    return x_ref[b]


def couples(count):
    return [range(b, min(b + 2, count)) for b in range(0, count, 2)]


def wide(pieces):
    return jnp.concatenate(list(pieces), axis=1)


def gram_kernel(ids_ref, *refs):
    parts, (f_ref, g_ref) = refs[:-2], refs[-2:]
    total = jnp.zeros(g_ref.shape, F32)
    for pair in couples(f_ref.shape[0]):
        f = wide(gathered(ids_ref, parts, b, f_ref) for b in pair)
        total = total + nt(f, f)
    g_ref[...] = total


def cross_kernel(ids_ref, f_ref, g_ref, *refs):
    parts, (k_ref, x_ref) = refs[:-2], refs[-2:]
    total = jnp.zeros(k_ref.shape, F32)
    for pair in couples(f_ref.shape[0]):
        z = wide(gathered(ids_ref, parts, b, x_ref) for b in pair)
        total = total + nt(wide(f_ref[b] for b in pair), z)
    k_ref[...] = half_width * total + center * g_ref[...]


def turn_kernel(ids_ref, inv_ref, *refs):
    parts, (f_ref, g_ref, x_ref) = refs[:-3], refs[-3:]
    n = x_ref.shape[-1]
    total = jnp.zeros(g_ref.shape, F32)
    for pair in couples(f_ref.shape[0]):
        f = nn(inv_ref[...], wide(gathered(ids_ref, parts, b, x_ref) for b in pair))
        for i, b in enumerate(pair):
            f_ref[b] = f[:, i * n:(i + 1) * n]
        total = total + nt(f, f)
    g_ref[...] = total


def turn_cross_kernel(ids_ref, inv_ref, f_ref, g_ref, *refs):
    parts, (k_ref, x_ref) = refs[:-2], refs[-2:]
    total = jnp.zeros(g_ref.shape, F32)
    for pair in couples(f_ref.shape[0]):
        z = wide(gathered(ids_ref, parts, b, x_ref) for b in pair)
        total = total + nt(wide(f_ref[b] for b in pair), z)
    k_ref[...] = half_width * nt(total, inv_ref[...]) + center * g_ref[...]


def basis_kernel(ids_ref, inv_ref, f_ref, *refs):
    parts, x_ref = refs[:-1], refs[-1]
    each = parts[0].shape[1]
    me = ids_ref[1]
    n = x_ref.shape[-1]
    for pair in couples(f_ref.shape[0]):
        q = nn(inv_ref[...], wide(f_ref[b] for b in pair))
        for i, b in enumerate(pair):
            x_ref[b] = q[:, i * n:(i + 1) * n]
            for s, part in enumerate(parts):
                part[b] = x_ref[b, pl.ds(pl.multiple_of((me ^ s) * each, each), each)]


def proj_kernel(nodes, ids_ref, *refs):
    pairs, parts, x_ref = (refs[:2], refs[2:4]), refs[4:-1], refs[-1]
    each = parts[0].shape[1]
    me = ids_ref[1]
    for i, (inv_ref, image_ref) in enumerate(pairs):
        x_ref[...] = nt(nn(inv_ref[...], image_ref[...] * (1.0 / nodes)), inv_ref[...])
        for s, part in enumerate(parts):
            part[i] = x_ref[pl.ds(pl.multiple_of((me ^ s) * each, each), each)]


def slot_row(slot, half, odd):
    return slot + half * (1 - odd) * jnp.where(slot >= half, -1, 1)


def split_kernel(ids_ref, start_ref, *outs):
    half, kk, n = outs[0].shape
    odd = ids_ref[0] % 2
    for slot in range(2 * half):
        row = slot_row(slot, half, odd)
        piece = start_ref[:, pl.ds(pl.multiple_of(row * n, n), n)]
        for i in range(2):
            outs[2 * i + slot // half][slot % half] = piece[i * kk:(i + 1) * kk]


def join_kernel(half, ids_ref, *refs):
    parts, out_ref = refs[:-1], refs[-1]
    each, _, n = parts[0].shape
    odd = ids_ref[0] % 2
    me = ids_ref[1]
    for s, part in enumerate(parts):
        for b in range(each):
            row = slot_row((me ^ s) * each + b, half, odd)
            out_ref[:, pl.ds(pl.multiple_of(row * n, n), n)] = part[b]


def exchange(pair):
    count = lax.axis_size("node")
    even = [(i, i ^ 1) for i in range(count)]
    odd = [(i, (i - 1 if i % 2 == 0 else i + 1) % count) for i in range(count)]
    return lax.ppermute(pair[0], "node", even), lax.ppermute(pair[1], "node", odd)


def swap(value, axis, hop):
    return lax.ppermute(value, axis, [(i, i ^ hop) for i in range(lax.axis_size(axis))])


def swapped(parts):
    return [parts[0]] + [swap(parts[s], "col", s) for s in range(1, len(parts))]


def hops_of(*axes):
    return [(axis, 1 << i) for axis in axes for i in range((lax.axis_size(axis) - 1).bit_length())]


def rounds_of(*axes):
    rounds = []
    for axis in axes:
        bits = (lax.axis_size(axis) - 1).bit_length()
        while bits > 0:
            low = max(bits - 2, 0)
            rounds.append((axis, [1 << bit for bit in range(low, bits)]))
            bits = low
    return rounds


def round_swaps(value, axis, hops):
    hops = hops if len(hops) == 1 else [hops[0], hops[1], hops[0] ^ hops[1]]
    return [swap(value, axis, hop) for hop in hops]


def round_sum(value, got):
    value = value + got[0]
    return value if len(got) == 1 else value + (got[1] + got[2])


def body(blocks, owner_row, block_col, start):
    cols_here, width = start.shape
    block = blocks.shape[1]
    slots = width // block
    half = slots // 2
    count = lax.axis_size("col")
    nodes = width * lax.axis_size("node")
    vecs = cols_here * count
    each = cols_here // 2
    quarter = slots // count
    square = (vecs, vecs)
    held_shape = (quarter, vecs, block)
    held = pltpu.VMEM(held_shape, F32)
    ids = jnp.stack([lax.axis_index("node"), lax.axis_index("col")]).astype(I32)

    halves = call(split_kernel, "split", [(half, each, block)] * 4, ids, start, scalars=1)
    before = [tuple(halves[:2]), tuple(halves[2:])]
    w, inv, table = prep(ids, owner_row, block_col, blocks, slots, lax.axis_size("node"))
    meta = (table, w, inv)

    def advance(now, before=((), ()), parts=False):
        first, _ = apply(meta, now[0], exchange(now[0]), before[0])
        mate = first if parts else ()
        second, out = apply(meta, now[1], exchange(now[1]), before[1], mate, count)
        return [first, second], out

    now, _ = advance(before)
    for step in range(DEGREE - 1):
        after, parts = advance(now, before, step == DEGREE - 2)
        before, now = now, after
    panel, gram_first = call(gram_kernel, "gram", [held_shape, square], ids, *swapped(parts), scalars=1)
    after, parts = advance(now, parts=True)
    before, now = now, after
    image = swapped(parts)
    got, hops = None, hops_of("col", "node")
    gram = gram_first
    for step in range(DEGREE - 1):
        after = []
        for i in range(2):
            old, gram, got = lax.optimization_barrier((before[i], gram, got))
            if (step, i) == (1, 1):
                old, image = lax.optimization_barrier((old, image))
            if got is not None:
                gram = gram + got
            got = swap(gram, *hops.pop(0)) if hops and (step, i) != (1, 1) else None
            mate = after[0] if i == 1 and step == DEGREE - 2 else ()
            done, parts = apply(meta, now[i], exchange(now[i]), old, mate, count)
            after.append(done)
            if got is not None:
                gram, got, _ = lax.optimization_barrier((gram, got, done))
        before, now = now, after
    if got is not None:
        gram = gram + got
    for hop in hops:
        gram = gram + swap(gram, *hop)
    halos = [exchange(panels) for panels in now]
    halos[0], gram = lax.optimization_barrier((halos[0], gram))
    inverse_first = inverse_factor(gram, nodes)
    (image_first,) = call(
        cross_kernel, "cross", [square], ids, panel, gram_first, *image, scalars=1, scratch=[held]
    )
    turned, gram_last = call(
        turn_kernel, "turn", [held_shape, square], ids, inverse_first, *swapped(parts), scalars=1, scratch=[held]
    )
    first, _ = apply(meta, now[0], halos[0])
    gram = gram_last
    hops = hops_of("col", "node")
    for i, hop in enumerate(hops):
        got = swap(gram, *hop)
        if i == 1:
            got, halos[1] = lax.optimization_barrier((got, halos[1]))
            _, parts = apply(meta, now[1], halos[1], (), first, count)
            (image_last,) = call(
                turn_cross_kernel, "turn_cross", [square], ids, inverse_first, turned, gram_last,
                *swapped(parts), scalars=1, scratch=[held],
            )
        if i == len(hops) - 3:
            got, image_first = lax.optimization_barrier((got, image_first))
        if i == len(hops) - 1:
            got, image_last = lax.optimization_barrier((got, image_last))
        gram = gram + got
    inverse_last = inverse_factor(gram, nodes)
    parts = call(
        basis_kernel, "basis", [(quarter, cols_here, block)] * count, ids, inverse_last, turned,
        scalars=1, scratch=[held],
    )
    for i, each_round in enumerate(rounds_of("node")):
        if i == 1:
            parts, image_last = lax.optimization_barrier((parts, image_last))
        got_first = round_swaps(image_first, *each_round)
        got = round_swaps(image_last, *each_round)
        if i == 0:
            got, got_first, image_last, _ = lax.optimization_barrier((got, got_first, image_last, inverse_last))
        image_first = round_sum(image_first, got_first)
        image_last = round_sum(image_last, got)
    arrived = swapped(parts)
    parts = call(
        functools.partial(proj_kernel, nodes), "proj", [(2, cols_here, vecs)] * count, ids,
        inverse_first, image_first, inverse_last, image_last, scalars=1, scratch=[pltpu.VMEM(square, F32)],
    )
    (basis,) = call(
        functools.partial(join_kernel, half), "join", [(cols_here, width)], ids, *arrived, scalars=1
    )
    received, basis = lax.optimization_barrier((swapped(parts), basis))
    projected = sum(received)
    return basis, projected[0], projected[1]


def solution(mesh):
    placed = (P("node", None, None), P("node", None), P("node", None), P("col", "node"))
    return jax.shard_map(
        body,
        mesh=mesh,
        in_specs=placed,
        out_specs=(P("col", "node"), P("col", None), P("col", None)),
        check_vma=False,
    )
```
